32 devices in a mesh: ka: 8 (over z, y), cfg: 4 (over x, core).
Axes of the slice: x: 2, y: 2, z: 4, core: 2. Of those that a mesh axis runs over, the one named last changes fastest.
Arguments:
- medium_t: float32 [2, 2, 16, 16, 16], replicated, may hold values from -6 to 6
- structure: float32 [2, 2, 16, 16, 4096], P(None, None, None, None, ('ka', 'cfg')), may hold values from -0.12 to 0.12
- kmap: int32 [4096], P(('ka', 'cfg')), may hold values from 0 to 15, as said below
- occupation: int32 [32, 16], P(('ka', 'cfg')), may hold values from 0 to 1
- cfg_weight: float32 [32], P(('ka', 'cfg')), may hold values from 1 to 30
- shift_a: float32 [2, 2, 16, 16], replicated, may hold values from -0.18 to 0.18
- shift_b: float32 [2, 2, 16, 16], replicated, may hold values from -0.18 to 0.18
Outputs:
- coarse_tau: float32 [2, 2, 16, 16, 16], replicated
- avg_tau: float32 [2, 2, 256, 256], P(None, None, 'cfg')
- correction: float32 [2, 2, 4096], P(None, None, ('ka', 'cfg'))
The draws below stay inside these ranges and needn't reach their ends.
Inputs may be any that keep to these rules, and one draw needn't show every extreme that they name: `kmap`: every cluster momentum is named by exactly 4096 / 16 k-points.
All inputs are finite; a program needn't handle non-finite values.
Results may differ from the reference program's by a relative error of at most 0.00015.
Values sent between devices are 32-bit elements; how exact they have to be, the bound alone decides.
No kernel may reach another device: no remote copies, remote signals or barrier semaphores. Data moves between devices by JAX's collectives and lax.ppermute only.
A program may use at most 128 MiB of HBM per device.

```python
import math
import jax
import jax.numpy as jnp
from jax import lax

NC = 16
LM = 16
ENERGIES = 2
TERMS = 3
CFD = 1
NK = 16
KPTS = 4096
NCFG = 32


def draw_kmap(key, part):
    order_k = jax.random.permutation(key, KPTS)
    return (order_k % NK).astype(jnp.int32)


def draw_cfg_weight(key, part):
    base = jax.random.uniform(key, (NCFG,), jnp.float32)
    ramp = 1.0 + 2.0 * jnp.arange(NCFG, dtype=jnp.float32) / max(NCFG - 1, 1)
    scaled = jnp.exp(base * math.log(3.0))
    return scaled * ramp


def touch_ends(array, stream_key, smallest, top_value):
    spot = [jax.random.randint(jax.random.fold_in(stream_key, axis), (), 0, length) for axis, length in enumerate(array.shape)]
    longest = array.shape.index(max(array.shape))
    next_to = spot[:longest] + [(spot[longest] + 1) % array.shape[longest]] + spot[longest + 1:]
    return array.at[tuple(spot)].set(smallest).at[tuple(next_to)].set(top_value)


def shard_levels(key, extent, split, low, largest):
    factor_of, own = 1.0, jax.random.fold_in(key, 6)
    for axis_at, parts in split:
        steps = jnp.exp(jax.random.uniform(jax.random.fold_in(own, axis_at), (parts,), jnp.float32, low / len(split), largest / len(split)))
        factor_of = factor_of * jnp.repeat(steps, extent[axis_at] // parts).reshape([-1 if axis == axis_at else 1 for axis in range(len(extent))])
    return factor_of


def scatter_about(rng, extent, width, reach, split=(), kind=jnp.bfloat16):
    values = width * jax.random.normal(rng, extent, jnp.float32)
    if split:
        values = values * shard_levels(rng, extent, split, -0.22, 0.18)
    return jnp.clip(values, -reach, reach).astype(kind)


def setup_inputs(seed: int = 0) -> dict:
    streams_of = jax.random.split(jax.random.key(seed), 8)
    return {
        "medium_t": scatter_about(streams_of[0], (ENERGIES, 2, LM, LM, NK), 1.0, 6.0, (), jnp.float32),
        "structure": scatter_about(streams_of[1], (ENERGIES, 2, LM, LM, KPTS), 0.02, 0.12, ((4, 32),), jnp.float32),
        "kmap": draw_kmap(jax.random.fold_in(streams_of[7], 71), 0),
        "occupation": touch_ends(jax.random.randint(streams_of[3], (NCFG, NC), 0, 2), jax.random.fold_in(streams_of[3], 1), 0, 1).astype(jnp.int32),
        "cfg_weight": draw_cfg_weight(jax.random.fold_in(streams_of[7], 71), 0),
        "shift_a": scatter_about(streams_of[5], (ENERGIES, 2, LM, LM), 0.03, 0.18, (), jnp.float32),
        "shift_b": scatter_about(streams_of[6], (ENERGIES, 2, LM, LM), 0.03, 0.18, (), jnp.float32),
    }


HIGH = lax.Precision.HIGHEST


def phase_tables(count_sites):
    places = jnp.arange(count_sites, dtype=jnp.int32)
    half_n = count_sites // 2
    cell = places % half_n
    site_xyz = jnp.stack([cell // 4, (cell // 2) % 2, cell % 2], axis=1).astype(jnp.float32)
    site_xyz = site_xyz + 0.5 * (places >= half_n).astype(jnp.float32)[:, None]
    mom_hkl = jnp.stack([places // 4, (places // 2) % 2, places % 2], axis=1).astype(jnp.float32)
    angles = math.pi * jnp.sum(mom_hkl[:, None, :] * site_xyz[None, :, :], axis=2)
    differ = angles[:, :, None] - angles[:, None, :]
    return jnp.cos(differ), jnp.sin(differ)


def batch_mul(first_m, second_m):
    def single(left_m, right_m):
        return jnp.einsum("abk,bck->ack", left_m, right_m, precision=HIGH)
    return jnp.stack([single(first_m[0], second_m[0]) - single(first_m[1], second_m[1]),
                      single(first_m[0], second_m[1]) + single(first_m[1], second_m[0])])


def batch_trace(first_m, second_m):
    def single(left_m, right_m):
        return jnp.einsum("abk,bak->k", left_m, right_m, precision=HIGH)
    return jnp.stack([single(first_m[0], second_m[0]) - single(first_m[1], second_m[1]),
                      single(first_m[0], second_m[1]) + single(first_m[1], second_m[0])])


def momentum_onehot(kmap, count_moms):
    return (kmap[None, :] == jnp.arange(count_moms, dtype=jnp.int32)[:, None]).astype(jnp.float32)


def kpoint_terms(medium, structure, onehot):
    spread_m = jnp.einsum("xabm,mk->xabk", medium, onehot, precision=HIGH)
    factor_m = batch_mul(spread_m, structure)
    second_t = batch_mul(factor_m, spread_m)
    third_t = batch_mul(factor_m, second_t)
    kpoint_tau = spread_m + second_t + third_t
    partial_sum = jnp.einsum("xabk,mk->xabm", kpoint_tau, onehot, precision=HIGH)
    return partial_sum, batch_mul(kpoint_tau, kpoint_tau)


def to_cluster(moment_tau, cosine, sine_tab):
    count_sites = cosine.shape[1]
    chans = moment_tau.shape[1]

    def apply_phase(table, block):
        return jnp.einsum("mij,abm->iajb", table, block, precision=HIGH)
    real_part = (apply_phase(cosine, moment_tau[0]) - apply_phase(sine_tab, moment_tau[1])) / count_sites
    imag_part = (apply_phase(cosine, moment_tau[1]) + apply_phase(sine_tab, moment_tau[0])) / count_sites
    order_n = count_sites * chans
    return jnp.stack([real_part.reshape(order_n, order_n), imag_part.reshape(order_n, order_n)])


def to_moment(cluster_rows, cosine_rows, sine_rows):
    count_sites = cosine_rows.shape[2]
    chans = cluster_rows.shape[2] // count_sites
    real_in = cluster_rows[0].reshape(-1, chans, count_sites, chans)
    imag_in = cluster_rows[1].reshape(-1, chans, count_sites, chans)

    def apply_phase(table, block):
        return jnp.einsum("mij,iajb->abm", table, block, precision=HIGH)
    real_part = (apply_phase(cosine_rows, real_in) + apply_phase(sine_rows, imag_in)) / count_sites
    imag_part = (apply_phase(cosine_rows, imag_in) - apply_phase(sine_rows, real_in)) / count_sites
    return jnp.stack([real_part, imag_part])


def impurity_sum(cluster, shift_first, shift_second, occupied, weights):
    count_cfg, count_sites = occupied.shape
    order_n = cluster.shape[1]
    chans = order_n // count_sites
    share = occupied.astype(jnp.float32)[None, :, :, None, None]
    delta = share * shift_first[:, None, None] + (1.0 - share) * shift_second[:, None, None]
    current = jnp.broadcast_to(cluster[:, None], (2, count_cfg, order_n, order_n))

    def site_mul(left_m, right_m):
        return jnp.einsum("gsab,gsbc->gsac", left_m, right_m, precision=HIGH)

    def left_mul(left_m, right_m):
        return jnp.einsum("ij,gjc->gic", left_m, right_m, precision=HIGH)
    for sweep_idx in range(TERMS):
        blocks = current.reshape(2, count_cfg, count_sites, chans, order_n)
        scattered = jnp.stack([site_mul(delta[0], blocks[0]) - site_mul(delta[1], blocks[1]),
                               site_mul(delta[0], blocks[1]) + site_mul(delta[1], blocks[0])])
        scattered = scattered.reshape(2, count_cfg, order_n, order_n)
        product = jnp.stack([left_mul(cluster[0], scattered[0]) - left_mul(cluster[1], scattered[1]),
                             left_mul(cluster[0], scattered[1]) + left_mul(cluster[1], scattered[0])])
        current = cluster[:, None] - product
    return jnp.einsum("g,xgij->xij", weights, current, precision=HIGH)


def reference(medium_t, structure, kmap, occupation, cfg_weight, shift_a, shift_b):
    cosine, sine_tab = phase_tables(NC)
    onehot = momentum_onehot(kmap, NK)
    per_moment = KPTS // NK
    weight_total = jnp.sum(cfg_weight)
    occ_blocks = occupation.reshape(-1, CFD, NC)
    weight_blocks = cfg_weight.reshape(-1, CFD)
    coarse_list = []
    average_list = []
    correct_list = []
    for energy in range(ENERGIES):
        partial_sum, squared = kpoint_terms(medium_t[energy], structure[energy], onehot)
        coarse = partial_sum / per_moment
        cluster = to_cluster(coarse, cosine, sine_tab)

        def one_block(block_pair):
            return impurity_sum(cluster, shift_a[energy], shift_b[energy], block_pair[0], block_pair[1])
        sums = lax.map(one_block, (occ_blocks, weight_blocks))
        average = jnp.sum(sums, axis=0) / weight_total
        diff_moment = to_moment(average, cosine, sine_tab) - coarse
        spread_d = jnp.einsum("xabm,mk->xabk", diff_moment, onehot, precision=HIGH)
        coarse_list.append(coarse)
        average_list.append(average)
        correct_list.append(batch_trace(spread_d, squared))
    return jnp.stack(coarse_list), jnp.stack(average_list), jnp.stack(correct_list)
```

```python
import functools
import math

import jax
import jax.numpy as jnp
import numpy as np
from jax import lax
from jax.experimental import pallas as pl
from jax.experimental.pallas import tpu as pltpu
from jax.sharding import PartitionSpec as P

ENERGIES = 2
F32 = jnp.float32
BF16 = jnp.bfloat16
PAD_ROWS = 8


def site_geometry(count_sites):
    places = np.arange(count_sites)
    half_n = count_sites // 2
    cell = places % half_n
    site_xyz = np.stack([cell // 4, cell // 2 % 2, cell % 2], axis=1).astype(np.float64)
    site_xyz = site_xyz + 0.5 * (places >= half_n)[:, None]
    mom_hkl = np.stack([places // 4, places // 2 % 2, places % 2], axis=1).astype(np.float64)
    angles = math.pi * (mom_hkl[:, None, :] * site_xyz[None, :, :]).sum(axis=2)
    place_diff = np.zeros((count_sites, count_sites), np.int32)
    for i in range(count_sites):
        for j in range(count_sites):
            gap = (site_xyz[i] - site_xyz[j]) % 2.0
            place_diff[i, j] = int(np.argmin(np.abs(site_xyz % 2.0 - gap).sum(axis=1)))
    return angles, place_diff


def phase_constants(count_sites, chans):
    angles, place_diff = site_geometry(count_sites)
    cos_ms = np.rint(np.cos(angles))
    sin_ms = np.rint(np.sin(angles))
    eye = np.eye(chans)
    fwd = np.stack([np.kron(cos_ms, eye), np.kron(-sin_ms, eye)]) / count_sites
    back = np.stack([np.kron(cos_ms.T, eye), np.kron(sin_ms.T, eye)]) / count_sites
    rows = np.stack([np.repeat(cos_ms.T, chans, axis=1), np.repeat(sin_ms.T, chans, axis=1)])
    return (
        fwd.astype(np.float32),
        back.astype(np.float32),
        rows.astype(np.float32),
        place_diff,
    )


def iota(shape, dim):
    return lax.broadcasted_iota(jnp.int32, shape, dim)


def split(value, pieces):
    out = []
    for step in range(pieces):
        part = value.astype(BF16)
        out.append(part)
        if step + 1 < pieces:
            value = value - part.astype(F32)
    return out


def mm(left, right):
    return jnp.dot(left, right, preferred_element_type=F32)


def mm_nt(left, right):
    return lax.dot_general(left, right, (((1,), (1,)), ((), ())), preferred_element_type=F32)


def mm_exact(left, right_bf16, pieces=3):
    parts = split(left, pieces)
    total = mm(parts[-1], right_bf16)
    for part in parts[-2::-1]:
        total = total + mm(part, right_bf16)
    return total


def mm3(left, right):
    left_hi, left_lo = split(left, 2)
    right_hi, right_lo = split(right, 2)
    return mm(left_hi, right_lo) + mm(left_lo, right_hi) + mm(left_hi, right_hi)


def mm_high(left, right):
    return jnp.dot(left, right, preferred_element_type=F32, precision=lax.Precision.HIGHEST)


def cmul(left, right, mul=mm3):
    rows = left[0].shape[0]
    both = jnp.concatenate(left, axis=0)
    by_real = mul(both, right[0])
    by_imag = mul(both, right[1])
    return (by_real[:rows] - by_imag[rows:], by_imag[:rows] + by_real[rows:])


def cadd(*terms):
    real, imag = terms[0]
    for term in terms[1:]:
        real, imag = real + term[0], imag + term[1]
    return (real, imag)


def cscale(value, factor):
    return (value[0] * factor, value[1] * factor)


def block_diag(row, chans):
    width = row.shape[1]
    tiled = jnp.concatenate([row] * (width // chans), axis=0)
    keep = iota((width, width), 0) // chans == iota((width, width), 1) // chans
    return jnp.where(keep, tiled, 0.0)


def batch_mul(left, right, write, chans):
    group = 4

    def body(step, carry):
        base = step * (group * chans)
        sums = [[None] * 3 for _ in range(group)]
        for b in range(chans):
            rights = [right[part, b * chans : (b + 1) * chans, :] for part in range(3)]
            for g in range(group):
                for part in range(3):
                    lane = left[part, pl.ds(base + (g * chans + b), 1), :]
                    term = lane * rights[part]
                    old = sums[g][part]
                    sums[g][part] = term if old is None else old + term
        for g in range(group):
            both, twice, cross = sums[g]
            write(base + g * chans, both - twice, cross - both - twice)
        return carry

    lax.fori_loop(0, chans // group, body, 0)


def put3(ref, base, count, real, imag):
    rows = pl.ds(pl.multiple_of(base, count), count)
    ref[0, rows, :] = real
    ref[1, rows, :] = imag
    ref[2, rows, :] = real + imag


def first_kernel(
    parity, medium, structure, kmap, occupation, weight,
    keep, send, z_out, y_out, y_row, y_s, g_s, f_s, part_s,
):
    chans = structure.shape[2]
    count_k = structure.shape[4]
    count_m = medium.shape[3]
    width = count_m * chans
    flat = chans * chans
    momenta = kmap[...]
    onehot = (momenta == iota((count_m, count_k), 0)).astype(BF16)
    wide = (momenta == iota((width, count_k), 0) // chans).astype(BF16)
    same = iota((flat, width), 0) % chans == iota((flat, width), 1) % chans
    lanes_of = (iota((count_m, width), 0) == iota((count_m, width), 1) // chans).astype(BF16)

    def fold(value):
        return jnp.sum(jnp.where(same, value, 0.0).reshape(chans, chans, width), axis=1)

    for energy in range(ENERGIES):
        for part in range(2):
            med = medium[energy, part]
            y_row[energy, part] = fold(mm_exact(med, lanes_of))
            value = mm_exact(med, onehot)
            y_s[part] = value
            y_out[energy, part] = value
            g_s[part] = structure[energy, part].reshape(flat, count_k)
        y_s[2] = y_s[0] + y_s[1]
        g_s[2] = g_s[0] + g_s[1]

        def write_f(base, real, imag):
            put3(f_s, base, chans, real, imag)

        batch_mul(y_s, g_s, write_f, chans)

        def write_z(base, real, imag):
            rows = pl.ds(pl.multiple_of(base, chans), chans)
            z_out[energy, 0, rows, :] = real + f_s[0, rows, :]
            z_out[energy, 1, rows, :] = imag + f_s[1, rows, :]

        batch_mul(f_s, f_s, write_z, chans)
        for part in range(2):
            parts = split(z_out[energy, part], 3)
            total = mm_nt(parts[2], wide) + mm_nt(parts[1], wide) + mm_nt(parts[0], wide)
            part_s[energy, part * chans : (part + 1) * chans, :] = fold(total)

    sites = occupation.shape[1]
    pairs = sites * sites
    from_l = (iota((sites, pairs), 0) == iota((sites, pairs), 1) // sites).astype(BF16)
    from_j = (iota((sites, pairs), 0) == iota((sites, pairs), 1) % sites).astype(BF16)
    diag = iota((sites, sites), 0) == iota((sites, sites), 1)
    triple = jnp.zeros((sites, pairs), F32)
    weight_sum = jnp.zeros((1, 1), F32)
    for g in range(occupation.shape[0]):
        filled = occupation[g : g + 1, :].astype(F32)
        square = jnp.broadcast_to(filled, (sites, sites))
        column = jnp.sum(jnp.where(diag, square, 0.0), axis=1, keepdims=True)
        row_l = mm(square.astype(BF16), from_l)
        row_j = mm(square.astype(BF16), from_j)
        scale = weight[0:1, g : g + 1]
        triple = triple + column * (row_l * row_j) * scale
        weight_sum = weight_sum + scale
    own = parity[0]
    half = 2 * chans
    keep[0:half, :] = part_s[own]
    send[0:half, :] = part_s[1 - own]
    for ref in (keep, send):
        ref[half : half + sites, :] = triple
        ref[half + sites : half + sites + PAD_ROWS, :] = jnp.broadcast_to(
            weight_sum, (PAD_ROWS, pairs)
        )


def square_kernel(y_in, z_in, out, y_s, z_s, t_s):
    flat = out.shape[1]
    chans = math.isqrt(flat)
    for part in range(2):
        y_s[part] = y_in[part]
        z_s[part] = z_in[part]
    y_s[2] = y_in[0] + y_in[1]
    z_s[2] = z_in[0] + z_in[1]

    def write_t(base, real, imag):
        rows = pl.ds(pl.multiple_of(base, chans), chans)
        put3(t_s, base, chans, real + y_s[0, rows, :], imag + y_s[1, rows, :])

    batch_mul(z_s, y_s, write_t, chans)

    def write_o(base, real, imag):
        rows = pl.ds(pl.multiple_of(base, chans), chans)
        out[0, rows, :] = real
        out[1, rows, :] = imag

    batch_mul(t_s, t_s, write_o, chans)


def cluster_kernel(
    per_moment, own_rows,
    parity, diff_tab, summed, y_row, shift_a, shift_b, fwd, back, phases, own_phases,
    keep, send, lhs_s, site_s, corr_s, p_s, t3_s, a_s, n_s,
):
    own = parity[0]
    chans = shift_a.shape[2]
    width = summed.shape[1]
    sites = phases.shape[1]
    rows_n = own_phases.shape[1] * chans
    cols = (slice(0, chans), slice(chans, 2 * chans))

    y_val = (y_row[own, 0], y_row[own, 1])
    z_val = (summed[cols[0], :], summed[cols[1], :])
    y_diag = tuple(block_diag(v, chans) for v in y_val)
    coarse = cadd(y_val, cscale(cmul(z_val, y_diag), 1.0 / per_moment))

    base_t = (shift_b[own, 0], shift_b[own, 1])
    step_t = (shift_a[own, 0] - base_t[0], shift_a[own, 1] - base_t[1])

    def left_small(small, value):
        stack = jnp.concatenate(small, axis=0)
        by_real = mm_high(stack, value[0])
        by_imag = mm_high(stack, value[1])
        return (by_real[cols[0]] - by_imag[cols[1]], by_imag[cols[0]] + by_real[cols[1]])

    b_diag = tuple(block_diag(v, chans) for v in left_small(base_t, coarse))
    series = [coarse]
    for _ in range(3):
        series.append(cscale(cmul(series[-1], b_diag), -1.0))
    kern = [left_small(step_t, series[n]) for n in range(3)]
    whole = cadd(*series)

    def spread(i, carry):
        phase = (phases[0, pl.ds(i, 1), :], phases[1, pl.ds(i, 1), :])
        for n in range(3):
            rows = pl.ds(pl.multiple_of(n * width + i * chans, chans), chans)
            real, imag = kern[n]
            lhs_s[0, rows, :] = phase[0] * real - phase[1] * imag
            lhs_s[1, rows, :] = phase[0] * imag + phase[1] * real
        return carry

    lax.fori_loop(0, sites, spread, 0)
    base = 3 * width
    for i in range(own_phases.shape[1]):
        phase = (own_phases[0, i : i + 1, :], own_phases[1, i : i + 1, :])
        for n, (real, imag) in enumerate([whole] + series[:3]):
            start = base + n * rows_n + i * chans
            lhs_s[0, start : start + chans, :] = phase[0] * real - phase[1] * imag
            lhs_s[1, start : start + chans, :] = phase[0] * imag + phase[1] * real
    fwd_val = (fwd[0], fwd[1])

    def transform(step, carry):
        rows = pl.ds(pl.multiple_of(step * width, width), width)
        out = cmul(
            (lhs_s[0, rows, :], lhs_s[1, rows, :]),
            fwd_val,
            functools.partial(mm_exact, pieces=2),
        )
        site_s[0, rows, :] = out[0]
        site_s[1, rows, :] = out[1]
        return carry

    lax.fori_loop(0, (base + 4 * rows_n) // width, transform, 0)

    norm = 1.0 / summed[2 * chans + sites : 2 * chans + sites + 1, :]
    triple = summed[2 * chans : 2 * chans + sites, :] * norm
    lane_l = iota((sites, width), 1) // sites
    lane_j = iota((sites, width), 1) % sites
    row_i = iota((sites, width), 0)
    pair = jnp.where(lane_l == row_i, triple, 0.0)
    single = jnp.sum(jnp.where(lane_j == row_i, pair, 0.0), axis=0, keepdims=True)
    stack = jnp.concatenate(
        [block_diag(triple, sites), pair, jnp.broadcast_to(single, (PAD_ROWS, width))], axis=0
    )
    spread_j = (
        iota((width, width), 0) % sites == iota((width, width), 1) // chans
    ).astype(BF16)
    corr_s[...] = mm_exact(stack, spread_j)

    hi_lo = []
    for part in range(2):
        hi, lo = split(site_s[part, 0:width, 0:chans], 2)
        hi_lo += [hi.astype(F32), hi.astype(F32), lo.astype(F32)]
    for n, piece in enumerate(hi_lo):
        a_s[:, n * chans : (n + 1) * chans] = piece
    a_val = a_s[:, 0 : 6 * chans].astype(BF16)
    t3_s[...] = jnp.zeros_like(t3_s)

    def triple_step(step, carry):
        rows = pl.ds(pl.multiple_of(step * chans, chans), chans)
        real_hi, real_lo = split(site_s[0, rows, :], 2)
        imag_hi, imag_lo = split(site_s[1, rows, :], 2)
        right_real = jnp.concatenate(
            [real_hi, real_lo, real_hi, -imag_hi, -imag_lo, -imag_hi], axis=0
        )
        right_imag = jnp.concatenate(
            [imag_hi, imag_lo, imag_hi, real_hi, real_lo, real_hi], axis=0
        )
        p_s[0] = mm(a_val, right_real)
        p_s[1] = mm(a_val, right_imag)
        for i in range(sites):
            gap = diff_tab[i, step]
            source = pl.ds(pl.multiple_of(gap * chans, chans), chans)
            scale = corr_s[pl.ds(step * sites + i, 1), :]
            here = slice(i * chans, (i + 1) * chans)
            t3_s[0, here, :] += scale * p_s[0, source, :]
            t3_s[1, here, :] += scale * p_s[1, source, :]
        return carry

    lax.fori_loop(0, sites, triple_step, 0)

    occupied = corr_s[width + sites : width + sites + 1, :]

    def middle(i, carry):
        rows = pl.ds(pl.multiple_of(i * chans, chans), chans)
        after = pl.ds(pl.multiple_of(width + i * chans, chans), chans)
        pair_row = corr_s[pl.ds(width + i, 1), :]
        on_diag = iota((chans, width), 0) + i * chans == iota((chans, width), 1)
        first = jnp.where(on_diag, occupied, 0.0)
        for part in range(2):
            lead = pair_row * site_s[part, rows, :]
            if part == 0:
                lead = lead - first
            n_s[part, after, :] = lead
            n_s[part, rows, :] = lead + pair_row * site_s[part, after, :] - t3_s[part, rows, :]
        return carry

    lax.fori_loop(0, sites, middle, 0)

    def site_rows(n):
        start = base + n * rows_n
        return (site_s[0, start : start + rows_n, :], site_s[1, start : start + rows_n, :])

    def kernel_of(n):
        rows = slice(n * width, (n + 1) * width)
        return (site_s[0, rows, :], site_s[1, rows, :])

    mid = [(n_s[0, n * width : (n + 1) * width, :], n_s[1, n * width : (n + 1) * width, :]) for n in range(2)]
    lead_rows = [site_rows(n) for n in range(4)]
    minus = -occupied
    q_zero = cadd(cmul(lead_rows[1], mid[0]), cmul(lead_rows[2], mid[1]), cscale(lead_rows[3], minus))
    q_one = cadd(cmul(lead_rows[1], mid[1]), cscale(lead_rows[2], minus))
    q_two = cscale(lead_rows[1], minus)
    result = cadd(
        lead_rows[0],
        cmul(q_zero, kernel_of(0)),
        cmul(q_one, kernel_of(1)),
        cmul(q_two, kernel_of(2)),
    )

    back_val = (back[0], back[1])
    means = []
    for n in range(2):
        moved = cmul(mid[n], back_val, functools.partial(mm_exact, pieces=2))
        lhs_s[0, n * width : (n + 1) * width, :] = moved[0]
        lhs_s[1, n * width : (n + 1) * width, :] = moved[1]

        def gather(i, carry):
            rows = pl.ds(pl.multiple_of(n * width + i * chans, chans), chans)
            phase = (phases[0, pl.ds(i, 1), :], phases[1, pl.ds(i, 1), :])
            real, imag = lhs_s[0, rows, :], lhs_s[1, rows, :]
            return (
                carry[0] + phase[0] * real + phase[1] * imag,
                carry[1] + phase[0] * imag - phase[1] * real,
            )

        zero = jnp.zeros((chans, width), F32)
        means.append(lax.fori_loop(0, sites, gather, (zero, zero)))
    mean_diag = [tuple(block_diag(v, chans) for v in pair_val) for pair_val in means]
    kern_diag = [tuple(block_diag(v, chans) for v in pair_val) for pair_val in kern]
    filled = -jnp.mean(occupied, axis=1, keepdims=True)
    u_zero = cadd(
        cmul(series[0], mean_diag[0]), cmul(series[1], mean_diag[1]), cscale(series[2], filled)
    )
    u_one = cadd(cmul(series[0], mean_diag[1]), cscale(series[1], filled))
    u_two = cscale(series[0], filled)
    change = cadd(
        series[1],
        series[2],
        series[3],
        cmul(u_zero, kern_diag[0]),
        cmul(u_one, kern_diag[1]),
        cmul(u_two, kern_diag[2]),
    )
    for ref, start in ((keep, 0), (send, own_rows)):
        for part in range(2):
            ref[part * own_rows : (part + 1) * own_rows, :] = result[part][start : start + own_rows]
            for n, value in enumerate((change, coarse)):
                at = 2 * own_rows + (2 * n + part) * chans
                ref[at : at + chans, :] = value[part]


def last_kernel(own_rows, parity, kept, got, kmap, squares, avg, coarse, correction):
    own = parity[0]
    chans = (kept.shape[0] - 2 * own_rows) // 4
    width = kept.shape[1]
    flat = coarse.shape[2]
    count_m = coarse.shape[3]
    count_k = kmap.shape[1]
    onehot = kmap[...] == iota((count_m, count_k), 0)
    spread_b = (iota((chans, flat), 0) == iota((chans, flat), 1) % chans).astype(BF16)
    same_b = iota((width, flat), 0) % chans == iota((width, flat), 1) // chans
    pick_m = (iota((width, count_m), 0) // chans == iota((width, count_m), 1)).astype(BF16)
    same_c = iota((flat, width), 0) % chans == iota((flat, width), 1) % chans
    for ref, energy in ((kept, own), (got, 1 - own)):
        moved = []
        for part in range(2):
            avg[energy, part] = ref[part * own_rows : (part + 1) * own_rows, :]
            at = 2 * own_rows + part * chans
            turned = mm_exact(ref[at : at + chans, :].T, spread_b)
            turned = jnp.where(same_b, turned, 0.0).reshape(count_m, chans, flat)
            moved.append(jnp.sum(turned, axis=1))
            at = 2 * own_rows + (2 + part) * chans
            row = ref[at : at + chans, :]
            tall = jnp.broadcast_to(row[:, None, :], (chans, chans, width)).reshape(flat, width)
            coarse[energy, part] = mm_exact(jnp.where(same_c, tall, 0.0), pick_m)
        both = jnp.concatenate(moved, axis=0)
        by_real = mm_high(both, squares[energy, 0])
        by_imag = mm_high(both, squares[energy, 1])
        real = by_real[:count_m] - by_imag[count_m:]
        imag = by_imag[:count_m] + by_real[count_m:]
        correction[energy, 0:1, :] = jnp.sum(jnp.where(onehot, real, 0.0), axis=0, keepdims=True)
        correction[energy, 1:2, :] = jnp.sum(jnp.where(onehot, imag, 0.0), axis=0, keepdims=True)


def shape_of(*extent):
    return jax.ShapeDtypeStruct(extent, F32)


SMEM_SPEC = pl.BlockSpec(memory_space=pltpu.SMEM)
VMEM_SPEC = pl.BlockSpec(memory_space=pltpu.VMEM)


def call(body, outs, scratch, scalars, args, cost):
    return pl.pallas_call(
        body,
        out_shape=outs,
        in_specs=[SMEM_SPEC] * scalars + [VMEM_SPEC] * (len(args) - scalars),
        out_specs=jax.tree.map(lambda _: VMEM_SPEC, outs),
        scratch_shapes=scratch,
        cost_estimate=pl.CostEstimate(flops=cost, bytes_accessed=cost // 64, transcendentals=0),
    )(*args)


def exchange_stages(ka_size, cfg_size):
    total = ka_size * cfg_size
    bits = []
    step = 2
    while step < total:
        bits.append(step)
        step *= 2
    stages = []
    for at in range(0, len(bits), 2):
        group = bits[at : at + 2]
        stages.append(group if len(group) == 1 else [group[0], group[1], group[0] + group[1]])
    return stages


def swap(value, mask, total):
    return lax.ppermute(value, ("ka", "cfg"), [(i, i ^ mask) for i in range(total)])


def per_device(medium_t, structure, kmap, occupation, cfg_weight, shift_a, shift_b):
    ka_size, cfg_size = lax.axis_size("ka"), lax.axis_size("cfg")
    total = ka_size * cfg_size
    sites = occupation.shape[1]
    chans, count_m = medium_t.shape[2], medium_t.shape[4]
    count_k = kmap.shape[0]
    flat = chans * chans
    width = count_m * chans
    per_moment = count_k * total // count_m
    own_sites = sites // cfg_size
    own_rows = own_sites * chans
    chip_rows = 2 * own_rows
    sum_rows = 2 * chans + sites + PAD_ROWS
    fwd, back, phases, place_diff = phase_constants(sites, chans)

    cfg_at = lax.axis_index("cfg")
    parity = (cfg_at % 2).reshape(1).astype(jnp.int32)
    phases = jnp.asarray(phases)
    own_phases = jnp.concatenate(
        [
            lax.dynamic_slice_in_dim(phases, cfg_at * own_sites, own_sites, 1),
            lax.dynamic_slice_in_dim(phases, (cfg_at ^ 1) * own_sites, own_sites, 1),
        ],
        axis=1,
    )
    kmap_row = kmap.reshape(1, count_k)

    keep, send, z_val, y_val, y_row = call(
        first_kernel,
        (
            shape_of(sum_rows, width),
            shape_of(sum_rows, width),
            shape_of(ENERGIES, 2, flat, count_k),
            shape_of(ENERGIES, 2, flat, count_k),
            shape_of(ENERGIES, 2, chans, width),
        ),
        [pltpu.VMEM((3, flat, count_k), F32)] * 3 + [pltpu.VMEM((ENERGIES, 2 * chans, width), F32)],
        1,
        (
            parity,
            medium_t.reshape(ENERGIES, 2, flat, count_m),
            structure,
            kmap_row,
            occupation,
            cfg_weight.reshape(1, -1),
        ),
        1 << 24,
    )
    summed = keep + swap(send, 1, total)
    for stage in exchange_stages(ka_size, cfg_size):
        arrived = [swap(summed, mask, total) for mask in stage]
        for value in arrived:
            summed = summed + value
    squares = jnp.stack(
        [
            call(
                square_kernel,
                shape_of(2, flat, count_k),
                [pltpu.VMEM((3, flat, count_k), F32)] * 3,
                0,
                (y_val[energy], z_val[energy]),
                1 << 24,
            )
            for energy in range(ENERGIES)
        ]
    )
    out_rows = 2 * own_rows + 4 * chans
    lhs_rows = 3 * width + 4 * chip_rows
    kept, sent = call(
        functools.partial(cluster_kernel, per_moment, own_rows),
        (shape_of(out_rows, width), shape_of(out_rows, width)),
        [
            pltpu.VMEM((2, lhs_rows, width), F32),
            pltpu.VMEM((2, lhs_rows, width), F32),
            pltpu.VMEM((width + sites + PAD_ROWS, width), F32),
            pltpu.VMEM((2, width, width), F32),
            pltpu.VMEM((2, width, width), F32),
            pltpu.VMEM((width, 128), F32),
            pltpu.VMEM((2, 2 * width, width), F32),
        ],
        2,
        (
            parity,
            jnp.asarray(place_diff),
            summed,
            y_row,
            shift_a,
            shift_b,
            jnp.asarray(fwd, BF16),
            jnp.asarray(back, BF16),
            phases,
            own_phases,
        ),
        1 << 26,
    )
    got = swap(sent, 1, total)
    avg, coarse, correction = call(
        functools.partial(last_kernel, own_rows),
        (
            shape_of(ENERGIES, 2, own_rows, width),
            shape_of(ENERGIES, 2, flat, count_m),
            shape_of(ENERGIES, 2, count_k),
        ),
        [],
        1,
        (parity, kept, got, kmap_row, squares),
        1 << 22,
    )
    return (coarse.reshape(ENERGIES, 2, chans, chans, count_m), avg, correction)


def solution(mesh):
    placed = (
        P(),
        P(None, None, None, None, ("ka", "cfg")),
        P(("ka", "cfg")),
        P(("ka", "cfg"), None),
        P(("ka", "cfg")),
        P(),
        P(),
    )
    return jax.shard_map(
        per_device,
        mesh=mesh,
        in_specs=placed,
        out_specs=(P(), P(None, None, "cfg", None), P(None, None, ("ka", "cfg"))),
        check_vma=False,
    )
```

```python
import functools
import math

import jax
import jax.numpy as jnp
import numpy as np
from jax import lax
from jax.experimental import pallas as pl
from jax.experimental.pallas import tpu as pltpu
from jax.sharding import PartitionSpec as P

ENERGIES = 2
F32 = jnp.float32
BF16 = jnp.bfloat16
PAD_ROWS = 8
KERNEL_VMEM = 20 << 20


def site_geometry(count_sites):
    places = np.arange(count_sites)
    half_n = count_sites // 2
    cell = places % half_n
    site_xyz = np.stack([cell // 4, cell // 2 % 2, cell % 2], axis=1).astype(np.float64)
    site_xyz = site_xyz + 0.5 * (places >= half_n)[:, None]
    mom_hkl = np.stack([places // 4, places // 2 % 2, places % 2], axis=1).astype(np.float64)
    angles = math.pi * (mom_hkl[:, None, :] * site_xyz[None, :, :]).sum(axis=2)
    place_diff = np.zeros((count_sites, count_sites), np.int32)
    for i in range(count_sites):
        for j in range(count_sites):
            gap = (site_xyz[i] - site_xyz[j]) % 2.0
            place_diff[i, j] = int(np.argmin(np.abs(site_xyz % 2.0 - gap).sum(axis=1)))
    return angles, place_diff


def phase_constants(count_sites, chans):
    angles, place_diff = site_geometry(count_sites)
    cos_ms = np.rint(np.cos(angles))
    sin_ms = np.rint(np.sin(angles))
    eye = np.eye(chans)
    fwd = np.stack([np.kron(cos_ms, eye), np.kron(-sin_ms, eye)]) / count_sites
    back = np.stack([np.kron(cos_ms.T, eye), np.kron(sin_ms.T, eye)]) / count_sites
    rows = np.stack([np.repeat(cos_ms.T, chans, axis=1), np.repeat(sin_ms.T, chans, axis=1)])
    return (
        fwd.astype(np.float32),
        back.astype(np.float32),
        rows.astype(np.float32),
        place_diff,
    )


def iota(shape, dim):
    return lax.broadcasted_iota(jnp.int32, shape, dim)


def split(value, pieces):
    out = []
    for step in range(pieces):
        part = value.astype(BF16)
        out.append(part)
        if step + 1 < pieces:
            value = value - part.astype(F32)
    return out


def mm(left, right):
    return jnp.dot(left, right, preferred_element_type=F32)


def mm_nt(left, right):
    return lax.dot_general(left, right, (((1,), (1,)), ((), ())), preferred_element_type=F32)


def mm_exact(left, right_bf16, pieces=3):
    parts = split(left, pieces)
    total = mm(parts[-1], right_bf16)
    for part in parts[-2::-1]:
        total = total + mm(part, right_bf16)
    return total


def mm3(left, right):
    left_hi, left_lo = split(left, 2)
    right_hi, right_lo = split(right, 2)
    return mm(left_hi, right_lo) + mm(left_lo, right_hi) + mm(left_hi, right_hi)


def mm_high(left, right):
    return jnp.dot(left, right, preferred_element_type=F32, precision=lax.Precision.HIGHEST)


def cmul(left, right, mul=mm3):
    rows = left[0].shape[0]
    both = jnp.concatenate(left, axis=0)
    by_real = mul(both, right[0])
    by_imag = mul(both, right[1])
    return (by_real[:rows] - by_imag[rows:], by_imag[:rows] + by_real[rows:])


def cadd(*terms):
    real, imag = terms[0]
    for term in terms[1:]:
        real, imag = real + term[0], imag + term[1]
    return (real, imag)


def cscale(value, factor):
    return (value[0] * factor, value[1] * factor)


def block_diag(row, chans):
    width = row.shape[1]
    tiled = jnp.concatenate([row] * (width // chans), axis=0)
    keep = iota((width, width), 0) // chans == iota((width, width), 1) // chans
    return jnp.where(keep, tiled, 0.0)


def batch_mul(left, right, write, chans):
    group = 4

    def body(step, carry):
        base = step * (group * chans)
        sums = [[None] * 3 for _ in range(group)]
        for b in range(chans):
            rights = [right[part, b * chans : (b + 1) * chans, :] for part in range(3)]
            for g in range(group):
                for part in range(3):
                    lane = left[part, pl.ds(base + (g * chans + b), 1), :]
                    term = lane * rights[part]
                    old = sums[g][part]
                    sums[g][part] = term if old is None else old + term
        for g in range(group):
            both, twice, cross = sums[g]
            write(base + g * chans, both - twice, cross - both - twice)
        return carry

    lax.fori_loop(0, chans // group, body, 0)


def put3(ref, base, count, real, imag):
    rows = pl.ds(pl.multiple_of(base, count), count)
    ref[0, rows, :] = real
    ref[1, rows, :] = imag
    ref[2, rows, :] = real + imag


def first_kernel(
    cfg_at, medium, structure, kmap, occupation, weight,
    keep, send, z_first, z_second, y_first, y_second, y_row, y_s, g_s, f_s, part_s,
):
    chans = structure.shape[2]
    count_k = structure.shape[4]
    count_m = medium.shape[3]
    width = count_m * chans
    flat = chans * chans
    momenta = kmap[...]
    onehot = (momenta == iota((count_m, count_k), 0)).astype(BF16)
    wide = (momenta == iota((width, count_k), 0) // chans).astype(BF16)
    same = iota((flat, width), 0) % chans == iota((flat, width), 1) % chans
    lanes_of = (iota((count_m, width), 0) == iota((count_m, width), 1) // chans).astype(BF16)

    def fold(value):
        return jnp.sum(jnp.where(same, value, 0.0).reshape(chans, chans, width), axis=1)

    for energy, (z_out, y_out) in enumerate(((z_first, y_first), (z_second, y_second))):
        for part in range(2):
            med = medium[energy, part]
            y_row[energy, part] = fold(mm_exact(med, lanes_of))
            value = mm_exact(med, onehot)
            y_s[part] = value
            y_out[part] = value
            g_s[part] = structure[energy, part].reshape(flat, count_k)
        y_s[2] = y_s[0] + y_s[1]
        g_s[2] = g_s[0] + g_s[1]

        def write_f(base, real, imag):
            put3(f_s, base, chans, real, imag)

        batch_mul(y_s, g_s, write_f, chans)

        def write_z(base, real, imag, z_out=z_out):
            rows = pl.ds(pl.multiple_of(base, chans), chans)
            z_out[0, rows, :] = real + f_s[0, rows, :]
            z_out[1, rows, :] = imag + f_s[1, rows, :]

        batch_mul(f_s, f_s, write_z, chans)
        for part in range(2):
            parts = split(z_out[part], 3)
            total = mm_nt(parts[2], wide) + mm_nt(parts[1], wide) + mm_nt(parts[0], wide)
            part_s[energy, part * chans : (part + 1) * chans, :] = fold(total)

    sites = occupation.shape[1]
    pairs = sites * sites
    from_l = (iota((sites, pairs), 0) == iota((sites, pairs), 1) // sites).astype(BF16)
    from_j = (iota((sites, pairs), 0) == iota((sites, pairs), 1) % sites).astype(BF16)
    diag = iota((sites, sites), 0) == iota((sites, sites), 1)
    triple = jnp.zeros((sites, pairs), F32)
    weight_sum = jnp.zeros((1, 1), F32)
    for g in range(occupation.shape[0]):
        filled = occupation[g : g + 1, :].astype(F32)
        square = jnp.broadcast_to(filled, (sites, sites))
        column = jnp.sum(jnp.where(diag, square, 0.0), axis=1, keepdims=True)
        row_l = mm(square.astype(BF16), from_l)
        row_j = mm(square.astype(BF16), from_j)
        scale = weight[0:1, g : g + 1]
        triple = triple + column * (row_l * row_j) * scale
        weight_sum = weight_sum + scale
    own = cfg_at[0] % 2
    half = 2 * chans
    keep[0:half, :] = part_s[own]
    send[0:half, :] = part_s[1 - own]
    for ref in (keep, send):
        ref[half : half + sites, :] = triple
        ref[half + sites : half + sites + PAD_ROWS, :] = jnp.broadcast_to(
            weight_sum, (PAD_ROWS, pairs)
        )


def square_kernel(y_in, z_in, out, y_s, z_s, t_s):
    flat = out.shape[1]
    chans = math.isqrt(flat)
    for part in range(2):
        y_s[part] = y_in[part]
        z_s[part] = z_in[part]
    y_s[2] = y_in[0] + y_in[1]
    z_s[2] = z_in[0] + z_in[1]

    def write_t(base, real, imag):
        rows = pl.ds(pl.multiple_of(base, chans), chans)
        put3(t_s, base, chans, real + y_s[0, rows, :], imag + y_s[1, rows, :])

    batch_mul(z_s, y_s, write_t, chans)

    def write_o(base, real, imag):
        rows = pl.ds(pl.multiple_of(base, chans), chans)
        out[0, rows, :] = real
        out[1, rows, :] = imag

    batch_mul(t_s, t_s, write_o, chans)


def cluster_kernel(
    per_moment, own_rows,
    cfg_at, diff_tab, summed, y_row, shift_a, shift_b, fwd, back, phases,
    keep, send, lhs_s, site_s, corr_s, p_s, t3_s, a_s, n_s,
):
    own = cfg_at[0] % 2
    chans = shift_a.shape[2]
    width = summed.shape[1]
    sites = phases.shape[1]
    own_sites = own_rows // chans
    rows_n = 2 * own_rows
    own_start = cfg_at[0] * own_sites
    other_start = (cfg_at[0] + 1 - 2 * own) * own_sites
    cols = (slice(0, chans), slice(chans, 2 * chans))

    y_val = (y_row[own, 0], y_row[own, 1])
    z_val = (summed[cols[0], :], summed[cols[1], :])
    y_diag = tuple(block_diag(v, chans) for v in y_val)
    coarse = cadd(y_val, cscale(cmul(z_val, y_diag), 1.0 / per_moment))

    base_t = (shift_b[own, 0], shift_b[own, 1])
    step_t = (shift_a[own, 0] - base_t[0], shift_a[own, 1] - base_t[1])

    def left_small(small, value):
        stack = jnp.concatenate(small, axis=0)
        by_real = mm_high(stack, value[0])
        by_imag = mm_high(stack, value[1])
        return (by_real[cols[0]] - by_imag[cols[1]], by_imag[cols[0]] + by_real[cols[1]])

    b_diag = tuple(block_diag(v, chans) for v in left_small(base_t, coarse))
    series = [coarse]
    for _ in range(3):
        series.append(cscale(cmul(series[-1], b_diag), -1.0))
    kern = [left_small(step_t, series[n]) for n in range(3)]
    whole = cadd(*series)

    for i in range(sites):
        phase = (phases[0, i : i + 1, :], phases[1, i : i + 1, :])
        for n, (real, imag) in enumerate(kern):
            start = n * width + i * chans
            lhs_s[0, start : start + chans, :] = phase[0] * real - phase[1] * imag
            lhs_s[1, start : start + chans, :] = phase[0] * imag + phase[1] * real

    base = 3 * width
    for i in range(2 * own_sites):
        site = own_start + i if i < own_sites else other_start + (i - own_sites)
        phase = (phases[0, pl.ds(site, 1), :], phases[1, pl.ds(site, 1), :])
        for n, (real, imag) in enumerate([whole] + series[:3]):
            start = base + n * rows_n + i * chans
            lhs_s[0, start : start + chans, :] = phase[0] * real - phase[1] * imag
            lhs_s[1, start : start + chans, :] = phase[0] * imag + phase[1] * real
    fwd_val = (fwd[0], fwd[1])

    for start in range(0, base + 4 * rows_n, width):
        rows = slice(start, start + width)
        out = cmul(
            (lhs_s[0, rows, :], lhs_s[1, rows, :]),
            fwd_val,
            functools.partial(mm_exact, pieces=2),
        )
        site_s[0, rows, :] = out[0]
        site_s[1, rows, :] = out[1]

    norm = 1.0 / summed[2 * chans + sites : 2 * chans + sites + 1, :]
    triple = summed[2 * chans : 2 * chans + sites, :] * norm
    lane_l = iota((sites, width), 1) // sites
    lane_j = iota((sites, width), 1) % sites
    row_i = iota((sites, width), 0)
    pair = jnp.where(lane_l == row_i, triple, 0.0)
    single = jnp.sum(jnp.where(lane_j == row_i, pair, 0.0), axis=0, keepdims=True)
    stack = jnp.concatenate(
        [block_diag(triple, sites), pair, jnp.broadcast_to(single, (PAD_ROWS, width))], axis=0
    )
    spread_j = (
        iota((width, width), 0) % sites == iota((width, width), 1) // chans
    ).astype(BF16)
    corr_s[...] = mm_exact(stack, spread_j)

    hi_lo = []
    for part in range(2):
        hi, lo = split(site_s[part, 0:width, 0:chans], 2)
        hi_lo += [hi.astype(F32), hi.astype(F32), lo.astype(F32)]
    for n, piece in enumerate(hi_lo):
        a_s[:, n * chans : (n + 1) * chans] = piece
    a_val = a_s[:, 0 : 6 * chans].astype(BF16)
    t3_s[...] = jnp.zeros_like(t3_s)

    together = p_s.shape[0]

    def triple_step(step, carry):
        for t in range(together):
            at = step * together + t
            rows = pl.ds(pl.multiple_of(at * chans, chans), chans)
            real_hi, real_lo = split(site_s[0, rows, :], 2)
            imag_hi, imag_lo = split(site_s[1, rows, :], 2)
            right_real = jnp.concatenate(
                [real_hi, real_lo, real_hi, -imag_hi, -imag_lo, -imag_hi], axis=0
            )
            right_imag = jnp.concatenate(
                [imag_hi, imag_lo, imag_hi, real_hi, real_lo, real_hi], axis=0
            )
            p_s[t, 0] = mm(a_val, right_real)
            p_s[t, 1] = mm(a_val, right_imag)
        for i in range(sites):
            here = slice(i * chans, (i + 1) * chans)
            total = [t3_s[0, here, :], t3_s[1, here, :]]
            for t in range(together):
                at = step * together + t
                source = pl.ds(pl.multiple_of(diff_tab[i, at] * chans, chans), chans)
                scale = corr_s[pl.ds(at * sites + i, 1), :]
                for part in range(2):
                    total[part] = total[part] + scale * p_s[t, part, source, :]
            for part in range(2):
                t3_s[part, here, :] = total[part]
        return carry

    lax.fori_loop(0, sites // together, triple_step, 0)

    occupied = corr_s[width + sites : width + sites + 1, :]

    def middle(i, carry):
        rows = pl.ds(pl.multiple_of(i * chans, chans), chans)
        after = pl.ds(pl.multiple_of(width + i * chans, chans), chans)
        pair_row = corr_s[pl.ds(width + i, 1), :]
        on_diag = iota((chans, width), 0) + i * chans == iota((chans, width), 1)
        first = jnp.where(on_diag, occupied, 0.0)
        for part in range(2):
            lead = pair_row * site_s[part, rows, :]
            if part == 0:
                lead = lead - first
            n_s[part, after, :] = lead
            n_s[part, rows, :] = lead + pair_row * site_s[part, after, :] - t3_s[part, rows, :]
        return carry

    lax.fori_loop(0, sites, middle, 0)

    def site_rows(n):
        start = base + n * rows_n
        return (site_s[0, start : start + rows_n, :], site_s[1, start : start + rows_n, :])

    def kernel_of(n):
        rows = slice(n * width, (n + 1) * width)
        return (site_s[0, rows, :], site_s[1, rows, :])

    mid = [(n_s[0, n * width : (n + 1) * width, :], n_s[1, n * width : (n + 1) * width, :]) for n in range(2)]
    lead_rows = [site_rows(n) for n in range(4)]
    minus = -occupied
    q_zero = cadd(cmul(lead_rows[1], mid[0]), cmul(lead_rows[2], mid[1]), cscale(lead_rows[3], minus))
    q_one = cadd(cmul(lead_rows[1], mid[1]), cscale(lead_rows[2], minus))
    q_two = cscale(lead_rows[1], minus)
    result = cadd(
        lead_rows[0],
        cmul(q_zero, kernel_of(0)),
        cmul(q_one, kernel_of(1)),
        cmul(q_two, kernel_of(2)),
    )

    back_val = (back[0], back[1])
    means = []
    for n in range(2):
        moved = cmul(mid[n], back_val, functools.partial(mm_exact, pieces=2))
        lhs_s[0, n * width : (n + 1) * width, :] = moved[0]
        lhs_s[1, n * width : (n + 1) * width, :] = moved[1]

        def gather(i, carry):
            rows = pl.ds(pl.multiple_of(n * width + i * chans, chans), chans)
            phase = (phases[0, pl.ds(i, 1), :], phases[1, pl.ds(i, 1), :])
            real, imag = lhs_s[0, rows, :], lhs_s[1, rows, :]
            return (
                carry[0] + phase[0] * real + phase[1] * imag,
                carry[1] + phase[0] * imag - phase[1] * real,
            )

        zero = jnp.zeros((chans, width), F32)
        means.append(lax.fori_loop(0, sites, gather, (zero, zero)))
    mean_diag = [tuple(block_diag(v, chans) for v in pair_val) for pair_val in means]
    kern_diag = [tuple(block_diag(v, chans) for v in pair_val) for pair_val in kern]
    filled = -jnp.mean(occupied, axis=1, keepdims=True)
    u_zero = cadd(
        cmul(series[0], mean_diag[0]), cmul(series[1], mean_diag[1]), cscale(series[2], filled)
    )
    u_one = cadd(cmul(series[0], mean_diag[1]), cscale(series[1], filled))
    u_two = cscale(series[0], filled)
    change = cadd(
        series[1],
        series[2],
        series[3],
        cmul(u_zero, kern_diag[0]),
        cmul(u_one, kern_diag[1]),
        cmul(u_two, kern_diag[2]),
    )
    for ref, start in ((keep, 0), (send, own_rows)):
        for part in range(2):
            ref[part * own_rows : (part + 1) * own_rows, :] = result[part][start : start + own_rows]
            for n, value in enumerate((change, coarse)):
                at = 2 * own_rows + (2 * n + part) * chans
                ref[at : at + chans, :] = value[part]


def last_kernel(
    own_rows, cfg_at, kept, got, kmap, square_first, square_second, avg, coarse, correction, d_s
):
    own = cfg_at[0] % 2
    chans = (kept.shape[0] - 2 * own_rows) // 4
    width = kept.shape[1]
    flat = coarse.shape[2]
    count_m = coarse.shape[3]
    count_k = kmap.shape[1]
    onehot = kmap[...] == iota((count_m, count_k), 0)
    spread_b = (iota((chans, flat), 0) == iota((chans, flat), 1) % chans).astype(BF16)
    same_b = iota((width, flat), 0) % chans == iota((width, flat), 1) // chans
    pick_m = (iota((width, count_m), 0) // chans == iota((width, count_m), 1)).astype(BF16)
    same_c = iota((flat, width), 0) % chans == iota((flat, width), 1) % chans
    for ref, energy in ((kept, own), (got, 1 - own)):
        moved = []
        for part in range(2):
            avg[energy, part] = ref[part * own_rows : (part + 1) * own_rows, :]
            at = 2 * own_rows + part * chans
            turned = mm_exact(ref[at : at + chans, :].T, spread_b)
            turned = jnp.where(same_b, turned, 0.0).reshape(count_m, chans, flat)
            moved.append(jnp.sum(turned, axis=1))
            at = 2 * own_rows + (2 + part) * chans
            row = ref[at : at + chans, :]
            tall = jnp.broadcast_to(row[:, None, :], (chans, chans, width)).reshape(flat, width)
            coarse[energy, part] = mm_exact(jnp.where(same_c, tall, 0.0), pick_m)
        d_s[energy] = jnp.concatenate(moved, axis=0)
    for energy, square in enumerate((square_first, square_second)):
        both = d_s[energy]
        by_real = mm3(both, square[0])
        by_imag = mm3(both, square[1])
        real = by_real[:count_m] - by_imag[count_m:]
        imag = by_imag[:count_m] + by_real[count_m:]
        correction[energy, 0:1, :] = jnp.sum(jnp.where(onehot, real, 0.0), axis=0, keepdims=True)
        correction[energy, 1:2, :] = jnp.sum(jnp.where(onehot, imag, 0.0), axis=0, keepdims=True)


def shape_of(*extent):
    return jax.ShapeDtypeStruct(extent, F32)


SMEM_SPEC = pl.BlockSpec(memory_space=pltpu.SMEM)
VMEM_SPEC = pl.BlockSpec(memory_space=pltpu.VMEM)


def call(body, outs, scratch, scalars, args, cost):
    return pl.pallas_call(
        body,
        out_shape=outs,
        in_specs=[SMEM_SPEC] * scalars + [VMEM_SPEC] * (len(args) - scalars),
        out_specs=jax.tree.map(lambda _: VMEM_SPEC, outs),
        scratch_shapes=scratch,
        compiler_params=pltpu.CompilerParams(vmem_limit_bytes=KERNEL_VMEM),
        cost_estimate=pl.CostEstimate(flops=cost, bytes_accessed=cost // 64, transcendentals=0),
    )(*args)


def exchange_stages(ka_size, cfg_size):
    total = ka_size * cfg_size
    bits = []
    step = 2
    while step < total:
        bits.append(step)
        step *= 2
    stages = []
    for at in range(0, len(bits), 2):
        group = bits[at : at + 2]
        stages.append(group if len(group) == 1 else [group[0], group[1], group[0] + group[1]])
    return stages


def swap(value, mask, total):
    return lax.ppermute(value, ("ka", "cfg"), [(i, i ^ mask) for i in range(total)])


def step(medium_t, structure, kmap, occupation, cfg_weight, shift_a, shift_b):
    ka_size, cfg_size = lax.axis_size("ka"), lax.axis_size("cfg")
    total = ka_size * cfg_size
    sites = occupation.shape[1]
    chans, count_m = medium_t.shape[2], medium_t.shape[4]
    count_k = kmap.shape[0]
    flat = chans * chans
    width = count_m * chans
    per_moment = count_k * total // count_m
    own_sites = sites // cfg_size
    own_rows = own_sites * chans
    chip_rows = 2 * own_rows
    sum_rows = 2 * chans + sites + PAD_ROWS
    fwd, back, phases, place_diff = phase_constants(sites, chans)

    cfg_at = lax.axis_index("cfg").astype(jnp.int32).reshape(1)
    phases = jnp.asarray(phases)
    kmap_row = kmap.reshape(1, count_k)

    keep, send, *z_y, y_row = call(
        first_kernel,
        (
            shape_of(sum_rows, width),
            shape_of(sum_rows, width),
            *[shape_of(2, flat, count_k)] * (2 * ENERGIES),
            shape_of(ENERGIES, 2, chans, width),
        ),
        [pltpu.VMEM((3, flat, count_k), F32)] * 3 + [pltpu.VMEM((ENERGIES, 2 * chans, width), F32)],
        1,
        (
            cfg_at,
            medium_t.reshape(ENERGIES, 2, flat, count_m),
            structure,
            kmap_row,
            occupation,
            cfg_weight.reshape(1, -1),
        ),
        1 << 24,
    )
    summed = keep + swap(send, 1, total)
    squares = []
    for energy in range(ENERGIES):
        squares.append(
            call(
                square_kernel,
                shape_of(2, flat, count_k),
                [pltpu.VMEM((3, flat, count_k), F32)] * 3,
                0,
                (z_y[ENERGIES + energy], z_y[energy]),
                1 << 24,
            )
        )
    for stage in exchange_stages(ka_size, cfg_size):
        arrived = []
        for mask in stage:
            arrived.append(swap(summed, mask, total))
        for value in arrived:
            summed = summed + value
    out_rows = 2 * own_rows + 4 * chans
    lhs_rows = 3 * width + 4 * chip_rows
    kept, sent = call(
        functools.partial(cluster_kernel, per_moment, own_rows),
        (shape_of(out_rows, width), shape_of(out_rows, width)),
        [
            pltpu.VMEM((2, lhs_rows, width), F32),
            pltpu.VMEM((2, lhs_rows, width), F32),
            pltpu.VMEM((width + sites + PAD_ROWS, width), F32),
            pltpu.VMEM((4, 2, width, width), F32),
            pltpu.VMEM((2, width, width), F32),
            pltpu.VMEM((width, 128), F32),
            pltpu.VMEM((2, 2 * width, width), F32),
        ],
        2,
        (
            cfg_at,
            jnp.asarray(place_diff),
            summed,
            y_row,
            shift_a,
            shift_b,
            jnp.asarray(fwd, BF16),
            jnp.asarray(back, BF16),
            phases,
        ),
        1 << 26,
    )
    got = swap(sent, 1, total)
    avg, coarse, correction = call(
        functools.partial(last_kernel, own_rows),
        (
            shape_of(ENERGIES, 2, own_rows, width),
            shape_of(ENERGIES, 2, flat, count_m),
            shape_of(ENERGIES, 2, count_k),
        ),
        [pltpu.VMEM((ENERGIES, 2 * count_m, flat), F32)],
        1,
        (cfg_at, kept, got, kmap_row, *squares),
        1 << 22,
    )
    return (coarse.reshape(ENERGIES, 2, chans, chans, count_m), avg, correction)


def solution(mesh):
    placed = (
        P(),
        P(None, None, None, None, ("ka", "cfg")),
        P(("ka", "cfg")),
        P(("ka", "cfg"), None),
        P(("ka", "cfg")),
        P(),
        P(),
    )
    return jax.shard_map(
        step,
        mesh=mesh,
        in_specs=placed,
        out_specs=(P(), P(None, None, "cfg", None), P(None, None, ("ka", "cfg"))),
        check_vma=False,
    )
```

```python
import functools
import math

import jax
import jax.numpy as jnp
import numpy as np
from jax import lax
from jax.experimental import pallas as pl
from jax.experimental.pallas import tpu as pltpu
from jax.sharding import PartitionSpec as P

ENERGIES = 2
F32 = jnp.float32
BF16 = jnp.bfloat16
PAD_ROWS = 8
KERNEL_VMEM = 20 << 20


def site_geometry(count_sites):
    places = np.arange(count_sites)
    half_n = count_sites // 2
    cell = places % half_n
    site_xyz = np.stack([cell // 4, cell // 2 % 2, cell % 2], axis=1).astype(np.float64)
    site_xyz = site_xyz + 0.5 * (places >= half_n)[:, None]
    mom_hkl = np.stack([places // 4, places // 2 % 2, places % 2], axis=1).astype(np.float64)
    angles = math.pi * (mom_hkl[:, None, :] * site_xyz[None, :, :]).sum(axis=2)
    place_diff = np.zeros((count_sites, count_sites), np.int32)
    for i in range(count_sites):
        for j in range(count_sites):
            gap = (site_xyz[i] - site_xyz[j]) % 2.0
            place_diff[i, j] = int(np.argmin(np.abs(site_xyz % 2.0 - gap).sum(axis=1)))
    return angles, place_diff


def phase_constants(count_sites, chans):
    angles, place_diff = site_geometry(count_sites)
    cos_ms = np.rint(np.cos(angles))
    sin_ms = np.rint(np.sin(angles))
    eye = np.eye(chans)
    fwd = np.stack([np.kron(cos_ms, eye), np.kron(-sin_ms, eye)]) / count_sites
    back = np.stack([np.kron(cos_ms.T, eye), np.kron(sin_ms.T, eye)]) / count_sites
    rows = np.stack([np.repeat(cos_ms.T, chans, axis=1), np.repeat(sin_ms.T, chans, axis=1)])
    return (
        fwd.astype(np.float32),
        back.astype(np.float32),
        rows.astype(np.float32),
        place_diff,
    )


def iota(shape, dim):
    return lax.broadcasted_iota(jnp.int32, shape, dim)


def split(value, pieces):
    out = []
    for step in range(pieces):
        part = value.astype(BF16)
        out.append(part)
        if step + 1 < pieces:
            value = value - part.astype(F32)
    return out


def mm(left, right):
    return jnp.dot(left, right, preferred_element_type=F32)


def mm_nt(left, right):
    return lax.dot_general(left, right, (((1,), (1,)), ((), ())), preferred_element_type=F32)


def mm_exact(left, right_bf16, pieces=3):
    parts = split(left, pieces)
    total = mm(parts[-1], right_bf16)
    for part in parts[-2::-1]:
        total = total + mm(part, right_bf16)
    return total


def mm3(left, right):
    left_hi, left_lo = split(left, 2)
    right_hi, right_lo = split(right, 2)
    return mm(left_hi, right_lo) + mm(left_lo, right_hi) + mm(left_hi, right_hi)


def mm_high(left, right):
    return jnp.dot(left, right, preferred_element_type=F32, precision=lax.Precision.HIGHEST)


def cmul(left, right, mul=mm3):
    rows = left[0].shape[0]
    both = jnp.concatenate(left, axis=0)
    by_real = mul(both, right[0])
    by_imag = mul(both, right[1])
    return (by_real[:rows] - by_imag[rows:], by_imag[:rows] + by_real[rows:])


def cadd(*terms):
    real, imag = terms[0]
    for term in terms[1:]:
        real, imag = real + term[0], imag + term[1]
    return (real, imag)


def cscale(value, factor):
    return (value[0] * factor, value[1] * factor)


def block_diag(row, chans):
    width = row.shape[1]
    tiled = jnp.concatenate([row] * (width // chans), axis=0)
    keep = iota((width, width), 0) // chans == iota((width, width), 1) // chans
    return jnp.where(keep, tiled, 0.0)


def batch_mul(left, right, write, chans):
    group = 4

    def body(step, carry):
        base = step * (group * chans)
        sums = [[None] * 3 for _ in range(group)]
        for b in range(chans):
            rights = [right[part, b * chans : (b + 1) * chans, :] for part in range(3)]
            for g in range(group):
                for part in range(3):
                    lane = left[part, pl.ds(base + (g * chans + b), 1), :]
                    term = lane * rights[part]
                    old = sums[g][part]
                    sums[g][part] = term if old is None else old + term
        for g in range(group):
            both, twice, cross = sums[g]
            write(base + g * chans, both - twice, cross - both - twice)
        return carry

    lax.fori_loop(0, chans // group, body, 0)


def put3(ref, base, count, real, imag):
    rows = pl.ds(pl.multiple_of(base, count), count)
    ref[0, rows, :] = real
    ref[1, rows, :] = imag
    ref[2, rows, :] = real + imag


def first_kernel(
    cfg_at, medium, structure, kmap, occupation, weight,
    keep, send, z_first, z_second, y_first, y_second, y_row, y_s, g_s, f_s, part_s,
):
    chans = structure.shape[2]
    count_k = structure.shape[4]
    count_m = medium.shape[3]
    width = count_m * chans
    flat = chans * chans
    momenta = kmap[...]
    onehot = (momenta == iota((count_m, count_k), 0)).astype(BF16)
    wide = (momenta == iota((width, count_k), 0) // chans).astype(BF16)
    same = iota((flat, width), 0) % chans == iota((flat, width), 1) % chans
    lanes_of = (iota((count_m, width), 0) == iota((count_m, width), 1) // chans).astype(BF16)

    def fold(value):
        return jnp.sum(jnp.where(same, value, 0.0).reshape(chans, chans, width), axis=1)

    for energy, (z_out, y_out) in enumerate(((z_first, y_first), (z_second, y_second))):
        for part in range(2):
            med = medium[energy, part]
            y_row[energy, part] = fold(mm_exact(med, lanes_of))
            value = mm_exact(med, onehot)
            y_s[part] = value
            y_out[part] = value
            g_s[part] = structure[energy, part].reshape(flat, count_k)
        y_s[2] = y_s[0] + y_s[1]
        g_s[2] = g_s[0] + g_s[1]

        def write_f(base, real, imag):
            put3(f_s, base, chans, real, imag)

        batch_mul(y_s, g_s, write_f, chans)

        def write_z(base, real, imag, z_out=z_out):
            rows = pl.ds(pl.multiple_of(base, chans), chans)
            z_out[0, rows, :] = real + f_s[0, rows, :]
            z_out[1, rows, :] = imag + f_s[1, rows, :]

        batch_mul(f_s, f_s, write_z, chans)
        for part in range(2):
            parts = split(z_out[part], 3)
            total = mm_nt(parts[2], wide) + mm_nt(parts[1], wide) + mm_nt(parts[0], wide)
            part_s[energy, part * chans : (part + 1) * chans, :] = fold(total)

    sites = occupation.shape[1]
    pairs = sites * sites
    from_l = (iota((sites, pairs), 0) == iota((sites, pairs), 1) // sites).astype(BF16)
    from_j = (iota((sites, pairs), 0) == iota((sites, pairs), 1) % sites).astype(BF16)
    diag = iota((sites, sites), 0) == iota((sites, sites), 1)
    triple = jnp.zeros((sites, pairs), F32)
    weight_sum = jnp.zeros((1, 1), F32)
    for g in range(occupation.shape[0]):
        filled = occupation[g : g + 1, :].astype(F32)
        square = jnp.broadcast_to(filled, (sites, sites))
        column = jnp.sum(jnp.where(diag, square, 0.0), axis=1, keepdims=True)
        row_l = mm(square.astype(BF16), from_l)
        row_j = mm(square.astype(BF16), from_j)
        scale = weight[0:1, g : g + 1]
        triple = triple + column * (row_l * row_j) * scale
        weight_sum = weight_sum + scale
    own = cfg_at[0] % 2
    half = 2 * chans
    keep[0:half, :] = part_s[own]
    send[0:half, :] = part_s[1 - own]
    for ref in (keep, send):
        ref[half : half + sites, :] = triple
        ref[half + sites : half + sites + PAD_ROWS, :] = jnp.broadcast_to(
            weight_sum, (PAD_ROWS, pairs)
        )


def square_kernel(y_in, z_in, out, y_s, z_s, t_s):
    flat = out.shape[1]
    chans = math.isqrt(flat)
    for part in range(2):
        y_s[part] = y_in[part]
        z_s[part] = z_in[part]
    y_s[2] = y_in[0] + y_in[1]
    z_s[2] = z_in[0] + z_in[1]

    def write_t(base, real, imag):
        rows = pl.ds(pl.multiple_of(base, chans), chans)
        put3(t_s, base, chans, real + y_s[0, rows, :], imag + y_s[1, rows, :])

    batch_mul(z_s, y_s, write_t, chans)

    def write_o(base, real, imag):
        rows = pl.ds(pl.multiple_of(base, chans), chans)
        out[0, rows, :] = real
        out[1, rows, :] = imag

    batch_mul(t_s, t_s, write_o, chans)


def cluster_kernel(
    per_moment, own_rows, place_diff,
    cfg_at, summed, y_row, shift_a, shift_b, fwd, back, phases,
    keep, send, lhs_s, site_s, corr_s, p_s, a_s, n_s,
):
    own = cfg_at[0] % 2
    chans = shift_a.shape[2]
    width = summed.shape[1]
    sites = phases.shape[1]
    own_sites = own_rows // chans
    rows_n = 2 * own_rows
    own_start = cfg_at[0] * own_sites
    other_start = (cfg_at[0] + 1 - 2 * own) * own_sites
    cols = (slice(0, chans), slice(chans, 2 * chans))

    y_val = (y_row[own, 0], y_row[own, 1])
    z_val = (summed[cols[0], :], summed[cols[1], :])
    y_diag = tuple(block_diag(v, chans) for v in y_val)
    coarse = cadd(y_val, cscale(cmul(z_val, y_diag), 1.0 / per_moment))

    base_t = (shift_b[own, 0], shift_b[own, 1])
    step_t = (shift_a[own, 0] - base_t[0], shift_a[own, 1] - base_t[1])

    stack = jnp.concatenate(base_t + step_t, axis=0)
    by_real = mm_high(stack, coarse[0])
    by_imag = mm_high(stack, coarse[1])

    def small_part(at):
        here, after = slice(at * chans, (at + 1) * chans), slice((at + 1) * chans, (at + 2) * chans)
        return (by_real[here] - by_imag[after], by_imag[here] + by_real[after])

    def rows_by(rows, diag):
        count = len(rows)
        out = cmul(
            tuple(jnp.concatenate([row[part] for row in rows], axis=0) for part in range(2)), diag
        )
        return [
            tuple(out[part][n * chans : (n + 1) * chans] for part in range(2)) for n in range(count)
        ]

    power, lead_kern = small_part(0), small_part(2)
    power_diag = tuple(block_diag(v, chans) for v in power)
    first, first_kern, power = rows_by([coarse, lead_kern, power], power_diag)
    first, first_kern = cscale(first, -1.0), cscale(first_kern, -1.0)
    power_diag = tuple(block_diag(v, chans) for v in power)
    second, third, second_kern = rows_by([coarse, first, lead_kern], power_diag)
    series = [coarse, first, second, third]
    kern = [lead_kern, first_kern, second_kern]
    whole = cadd(*series)

    for i in range(sites):
        phase = (phases[0, i : i + 1, :], phases[1, i : i + 1, :])
        for n, (real, imag) in enumerate(kern):
            start = n * width + i * chans
            lhs_s[0, start : start + chans, :] = phase[0] * real - phase[1] * imag
            lhs_s[1, start : start + chans, :] = phase[0] * imag + phase[1] * real

    base = 3 * width
    for i in range(2 * own_sites):
        site = own_start + i if i < own_sites else other_start + (i - own_sites)
        phase = (phases[0, pl.ds(site, 1), :], phases[1, pl.ds(site, 1), :])
        for n, (real, imag) in enumerate([whole] + series[:3]):
            start = base + n * rows_n + i * chans
            lhs_s[0, start : start + chans, :] = phase[0] * real - phase[1] * imag
            lhs_s[1, start : start + chans, :] = phase[0] * imag + phase[1] * real
    fwd_val = (fwd[0], fwd[1])

    for start in range(0, base + 4 * rows_n, width):
        rows = slice(start, start + width)
        out = cmul(
            (lhs_s[0, rows, :], lhs_s[1, rows, :]),
            fwd_val,
            functools.partial(mm_exact, pieces=2),
        )
        site_s[0, rows, :] = out[0]
        site_s[1, rows, :] = out[1]

    norm = 1.0 / summed[2 * chans + sites : 2 * chans + sites + 1, :]
    triple = summed[2 * chans : 2 * chans + sites, :] * norm
    lane_l = iota((sites, width), 1) // sites
    lane_j = iota((sites, width), 1) % sites
    row_i = iota((sites, width), 0)
    pair = jnp.where(lane_l == row_i, triple, 0.0)
    single = jnp.sum(jnp.where(lane_j == row_i, pair, 0.0), axis=0, keepdims=True)
    stack = jnp.concatenate(
        [block_diag(triple, sites), pair, jnp.broadcast_to(single, (PAD_ROWS, width))], axis=0
    )
    spread_j = (
        iota((width, width), 0) % sites == iota((width, width), 1) // chans
    ).astype(BF16)
    corr_s[...] = mm_exact(stack, spread_j)

    hi_lo = []
    for part in range(2):
        hi, lo = split(site_s[part, 0:width, 0:chans], 2)
        hi_lo += [hi.astype(F32), hi.astype(F32), lo.astype(F32)]
    for n, piece in enumerate(hi_lo):
        a_s[:, n * chans : (n + 1) * chans] = piece
    a_val = a_s[:, 0 : 6 * chans].astype(BF16)
    for at in range(sites):
        rows = slice(at * chans, (at + 1) * chans)
        real_hi, real_lo = split(site_s[0, rows, :], 2)
        imag_hi, imag_lo = split(site_s[1, rows, :], 2)
        right_real = jnp.concatenate(
            [real_hi, real_lo, real_hi, -imag_hi, -imag_lo, -imag_hi], axis=0
        )
        right_imag = jnp.concatenate(
            [imag_hi, imag_lo, imag_hi, real_hi, real_lo, real_hi], axis=0
        )
        p_s[at, 0] = mm(a_val, right_real)
        p_s[at, 1] = mm(a_val, right_imag)

    occupied = corr_s[width + sites : width + sites + 1, :]

    for i in range(sites):
        rows = slice(i * chans, (i + 1) * chans)
        after = slice(width + i * chans, width + (i + 1) * chans)
        pair_row = corr_s[width + i : width + i + 1, :]
        on_diag = iota((chans, width), 0) + i * chans == iota((chans, width), 1)
        for part in range(2):
            total = None
            for at in range(sites):
                gap = int(place_diff[i, at])
                scale = corr_s[at * sites + i : at * sites + i + 1, :]
                term = scale * p_s[at, part, gap * chans : (gap + 1) * chans, :]
                total = term if total is None else total + term
            lead = pair_row * site_s[part, rows, :]
            if part == 0:
                lead = lead - jnp.where(on_diag, occupied, 0.0)
            n_s[part, after, :] = lead
            n_s[part, rows, :] = lead + pair_row * site_s[part, after, :] - total

    def site_rows(n):
        start = base + n * rows_n
        return (site_s[0, start : start + rows_n, :], site_s[1, start : start + rows_n, :])

    def kernel_of(n):
        rows = slice(n * width, (n + 1) * width)
        return (site_s[0, rows, :], site_s[1, rows, :])

    mid = [(n_s[0, n * width : (n + 1) * width, :], n_s[1, n * width : (n + 1) * width, :]) for n in range(2)]
    lead_rows = [site_rows(n) for n in range(4)]
    minus = -occupied
    q_zero = cadd(cmul(lead_rows[1], mid[0]), cmul(lead_rows[2], mid[1]), cscale(lead_rows[3], minus))
    q_one = cadd(cmul(lead_rows[1], mid[1]), cscale(lead_rows[2], minus))
    q_two = cscale(lead_rows[1], minus)
    result = cadd(
        lead_rows[0],
        cmul(q_zero, kernel_of(0)),
        cmul(q_one, kernel_of(1)),
        cmul(q_two, kernel_of(2)),
    )

    back_val = (back[0], back[1])
    means = []
    for n in range(2):
        moved = cmul(mid[n], back_val, functools.partial(mm_exact, pieces=2))
        total = None
        for i in range(sites):
            rows = slice(i * chans, (i + 1) * chans)
            phase = (phases[0, i : i + 1, :], phases[1, i : i + 1, :])
            real, imag = moved[0][rows], moved[1][rows]
            term = (phase[0] * real + phase[1] * imag, phase[0] * imag - phase[1] * real)
            total = term if total is None else cadd(total, term)
        means.append(total)
    mean_diag = [tuple(block_diag(v, chans) for v in pair_val) for pair_val in means]
    kern_diag = [tuple(block_diag(v, chans) for v in pair_val) for pair_val in kern]
    filled = -jnp.mean(occupied, axis=1, keepdims=True)
    u_zero = cadd(
        cmul(series[0], mean_diag[0]), cmul(series[1], mean_diag[1]), cscale(series[2], filled)
    )
    u_one = cadd(cmul(series[0], mean_diag[1]), cscale(series[1], filled))
    u_two = cscale(series[0], filled)
    change = cadd(
        series[1],
        series[2],
        series[3],
        cmul(u_zero, kern_diag[0]),
        cmul(u_one, kern_diag[1]),
        cmul(u_two, kern_diag[2]),
    )
    for ref, start in ((keep, 0), (send, own_rows)):
        for part in range(2):
            ref[part * own_rows : (part + 1) * own_rows, :] = result[part][start : start + own_rows]
            for n, value in enumerate((change, coarse)):
                at = 2 * own_rows + (2 * n + part) * chans
                ref[at : at + chans, :] = value[part]


def last_kernel(
    own_rows, cfg_at, kept, got, kmap, square_first, square_second, avg, coarse, correction, d_s
):
    own = cfg_at[0] % 2
    chans = (kept.shape[0] - 2 * own_rows) // 4
    width = kept.shape[1]
    flat = coarse.shape[2]
    count_m = coarse.shape[3]
    count_k = kmap.shape[1]
    onehot = kmap[...] == iota((count_m, count_k), 0)
    spread_b = (iota((chans, flat), 0) == iota((chans, flat), 1) % chans).astype(BF16)
    same_b = iota((width, flat), 0) % chans == iota((width, flat), 1) // chans
    pick_m = (iota((width, count_m), 0) // chans == iota((width, count_m), 1)).astype(BF16)
    same_c = iota((flat, width), 0) % chans == iota((flat, width), 1) % chans
    for ref, energy in ((kept, own), (got, 1 - own)):
        moved = []
        for part in range(2):
            avg[energy, part] = ref[part * own_rows : (part + 1) * own_rows, :]
            at = 2 * own_rows + part * chans
            turned = mm_exact(ref[at : at + chans, :].T, spread_b)
            turned = jnp.where(same_b, turned, 0.0).reshape(count_m, chans, flat)
            moved.append(jnp.sum(turned, axis=1))
            at = 2 * own_rows + (2 + part) * chans
            row = ref[at : at + chans, :]
            tall = jnp.broadcast_to(row[:, None, :], (chans, chans, width)).reshape(flat, width)
            coarse[energy, part] = mm_exact(jnp.where(same_c, tall, 0.0), pick_m)
        d_s[energy] = jnp.concatenate(moved, axis=0)
    for energy, square in enumerate((square_first, square_second)):
        both = d_s[energy]
        by_real = mm3(both, square[0])
        by_imag = mm3(both, square[1])
        real = by_real[:count_m] - by_imag[count_m:]
        imag = by_imag[:count_m] + by_real[count_m:]
        correction[energy, 0:1, :] = jnp.sum(jnp.where(onehot, real, 0.0), axis=0, keepdims=True)
        correction[energy, 1:2, :] = jnp.sum(jnp.where(onehot, imag, 0.0), axis=0, keepdims=True)


def shape_of(*extent):
    return jax.ShapeDtypeStruct(extent, F32)


SMEM_SPEC = pl.BlockSpec(memory_space=pltpu.SMEM)
VMEM_SPEC = pl.BlockSpec(memory_space=pltpu.VMEM)


def call(body, outs, scratch, scalars, args, cost):
    return pl.pallas_call(
        body,
        out_shape=outs,
        in_specs=[SMEM_SPEC] * scalars + [VMEM_SPEC] * (len(args) - scalars),
        out_specs=jax.tree.map(lambda _: VMEM_SPEC, outs),
        scratch_shapes=scratch,
        compiler_params=pltpu.CompilerParams(vmem_limit_bytes=KERNEL_VMEM),
        cost_estimate=pl.CostEstimate(flops=cost, bytes_accessed=cost // 64, transcendentals=0),
    )(*args)


def exchange_stages(ka_size, cfg_size):
    total = ka_size * cfg_size
    bits = []
    step = 2
    while step < total:
        bits.append(step)
        step *= 2
    stages = []
    for at in range(0, len(bits), 2):
        group = bits[at : at + 2]
        stages.append(group if len(group) == 1 else [group[0], group[1], group[0] + group[1]])
    return stages


def swap(value, mask, total):
    return lax.ppermute(value, ("ka", "cfg"), [(i, i ^ mask) for i in range(total)])


def step(medium_t, structure, kmap, occupation, cfg_weight, shift_a, shift_b):
    ka_size, cfg_size = lax.axis_size("ka"), lax.axis_size("cfg")
    total = ka_size * cfg_size
    sites = occupation.shape[1]
    chans, count_m = medium_t.shape[2], medium_t.shape[4]
    count_k = kmap.shape[0]
    flat = chans * chans
    width = count_m * chans
    per_moment = count_k * total // count_m
    own_sites = sites // cfg_size
    own_rows = own_sites * chans
    chip_rows = 2 * own_rows
    sum_rows = 2 * chans + sites + PAD_ROWS
    fwd, back, phases, place_diff = phase_constants(sites, chans)

    cfg_at = lax.axis_index("cfg").astype(jnp.int32).reshape(1)
    phases = jnp.asarray(phases)
    kmap_row = kmap.reshape(1, count_k)

    keep, send, *z_y, y_row = call(
        first_kernel,
        (
            shape_of(sum_rows, width),
            shape_of(sum_rows, width),
            *[shape_of(2, flat, count_k)] * (2 * ENERGIES),
            shape_of(ENERGIES, 2, chans, width),
        ),
        [pltpu.VMEM((3, flat, count_k), F32)] * 3 + [pltpu.VMEM((ENERGIES, 2 * chans, width), F32)],
        1,
        (
            cfg_at,
            medium_t.reshape(ENERGIES, 2, flat, count_m),
            structure,
            kmap_row,
            occupation,
            cfg_weight.reshape(1, -1),
        ),
        1 << 24,
    )
    summed = keep + swap(send, 1, total)
    squares = []
    for energy in range(ENERGIES):
        squares.append(
            call(
                square_kernel,
                shape_of(2, flat, count_k),
                [pltpu.VMEM((3, flat, count_k), F32)] * 3,
                0,
                (z_y[ENERGIES + energy], z_y[energy]),
                1 << 24,
            )
        )
    for stage in exchange_stages(ka_size, cfg_size):
        arrived = []
        for mask in stage:
            arrived.append(swap(summed, mask, total))
        for value in arrived:
            summed = summed + value
    out_rows = 2 * own_rows + 4 * chans
    lhs_rows = 3 * width + 4 * chip_rows
    kept, sent = call(
        functools.partial(cluster_kernel, per_moment, own_rows, place_diff),
        (shape_of(out_rows, width), shape_of(out_rows, width)),
        [
            pltpu.VMEM((2, lhs_rows, width), F32),
            pltpu.VMEM((2, lhs_rows, width), F32),
            pltpu.VMEM((width + sites + PAD_ROWS, width), F32),
            pltpu.VMEM((sites, 2, width, width), F32),
            pltpu.VMEM((width, 128), F32),
            pltpu.VMEM((2, 2 * width, width), F32),
        ],
        1,
        (
            cfg_at,
            summed,
            y_row,
            shift_a,
            shift_b,
            jnp.asarray(fwd, BF16),
            jnp.asarray(back, BF16),
            phases,
        ),
        1 << 26,
    )
    got = swap(sent, 1, total)
    avg, coarse, correction = call(
        functools.partial(last_kernel, own_rows),
        (
            shape_of(ENERGIES, 2, own_rows, width),
            shape_of(ENERGIES, 2, flat, count_m),
            shape_of(ENERGIES, 2, count_k),
        ),
        [pltpu.VMEM((ENERGIES, 2 * count_m, flat), F32)],
        1,
        (cfg_at, kept, got, kmap_row, *squares),
        1 << 22,
    )
    return (coarse.reshape(ENERGIES, 2, chans, chans, count_m), avg, correction)


def solution(mesh):
    placed = (
        P(),
        P(None, None, None, None, ("ka", "cfg")),
        P(("ka", "cfg")),
        P(("ka", "cfg"), None),
        P(("ka", "cfg")),
        P(),
        P(),
    )
    return jax.shard_map(
        step,
        mesh=mesh,
        in_specs=placed,
        out_specs=(P(), P(None, None, "cfg", None), P(None, None, ("ka", "cfg"))),
        check_vma=False,
    )
```

```python
import functools
import math

import jax
import jax.numpy as jnp
import numpy as np
from jax import lax
from jax.experimental import pallas as pl
from jax.experimental.pallas import tpu as pltpu
from jax.sharding import PartitionSpec as P

ENERGIES = 2
F32 = jnp.float32
BF16 = jnp.bfloat16
PAD_ROWS = 8
SLOT = 32
KERNEL_VMEM = 20 << 20


def site_geometry(count_sites):
    places = np.arange(count_sites)
    half_n = count_sites // 2
    cell = places % half_n
    site_xyz = np.stack([cell // 4, cell // 2 % 2, cell % 2], axis=1).astype(np.float64)
    site_xyz = site_xyz + 0.5 * (places >= half_n)[:, None]
    mom_hkl = np.stack([places // 4, places // 2 % 2, places % 2], axis=1).astype(np.float64)
    angles = math.pi * (mom_hkl[:, None, :] * site_xyz[None, :, :]).sum(axis=2)
    place_diff = np.zeros((count_sites, count_sites), np.int32)
    for i in range(count_sites):
        for j in range(count_sites):
            gap = (site_xyz[i] - site_xyz[j]) % 2.0
            place_diff[i, j] = int(np.argmin(np.abs(site_xyz % 2.0 - gap).sum(axis=1)))
    return angles, place_diff


def phase_constants(count_sites, chans):
    angles, place_diff = site_geometry(count_sites)
    cos_ms = np.rint(np.cos(angles))
    sin_ms = np.rint(np.sin(angles))
    eye = np.eye(chans)
    fwd = np.stack([np.kron(cos_ms, eye), np.kron(-sin_ms, eye)]) / count_sites
    back = np.stack([np.kron(cos_ms.T, eye), np.kron(sin_ms.T, eye)]) / count_sites
    rows = np.stack([np.repeat(cos_ms.T, chans, axis=1), np.repeat(sin_ms.T, chans, axis=1)])
    return (
        fwd.astype(np.float32),
        back.astype(np.float32),
        rows.astype(np.float32),
        place_diff,
    )


def iota(shape, dim):
    return lax.broadcasted_iota(jnp.int32, shape, dim)


def split(value, pieces):
    out = []
    for step in range(pieces):
        part = value.astype(BF16)
        out.append(part)
        if step + 1 < pieces:
            value = value - part.astype(F32)
    return out


def mm(left, right):
    return jnp.dot(left, right, preferred_element_type=F32)


def mm_nt(left, right):
    return lax.dot_general(left, right, (((1,), (1,)), ((), ())), preferred_element_type=F32)


def mm_exact(left, right_bf16, pieces=3):
    parts = split(left, pieces)
    total = mm(parts[-1], right_bf16)
    for part in parts[-2::-1]:
        total = total + mm(part, right_bf16)
    return total


def mm3(left, right):
    left_hi, left_lo = split(left, 2)
    right_hi, right_lo = split(right, 2)
    return mm(left_hi, right_lo) + mm(left_lo, right_hi) + mm(left_hi, right_hi)


def mm_high(left, right):
    return jnp.dot(left, right, preferred_element_type=F32, precision=lax.Precision.HIGHEST)


def cmul(left, right, mul=mm3):
    rows = left[0].shape[0]
    both = jnp.concatenate(left, axis=0)
    by_real = mul(both, right[0])
    by_imag = mul(both, right[1])
    return (by_real[:rows] - by_imag[rows:], by_imag[:rows] + by_real[rows:])


def cadd(*terms):
    real, imag = terms[0]
    for term in terms[1:]:
        real, imag = real + term[0], imag + term[1]
    return (real, imag)


def cscale(value, factor):
    return (value[0] * factor, value[1] * factor)


def block_diag(row, chans):
    width = row.shape[1]
    tiled = jnp.concatenate([row] * (width // chans), axis=0)
    keep = iota((width, width), 0) // chans == iota((width, width), 1) // chans
    return jnp.where(keep, tiled, 0.0)


def batch_mul(left, right, write, chans):
    group = 4

    def body(step, carry):
        base = step * (group * chans)
        sums = [[None] * 3 for _ in range(group)]
        for b in range(chans):
            rights = [right[part, b * chans : (b + 1) * chans, :] for part in range(3)]
            for g in range(group):
                for part in range(3):
                    lane = left[part, pl.ds(base + (g * chans + b), 1), :]
                    term = lane * rights[part]
                    old = sums[g][part]
                    sums[g][part] = term if old is None else old + term
        for g in range(group):
            both, twice, cross = sums[g]
            write(base + g * chans, both - twice, cross - both - twice)
        return carry

    lax.fori_loop(0, chans // group, body, 0)


def put3(ref, base, count, real, imag):
    rows = pl.ds(pl.multiple_of(base, count), count)
    ref[0, rows, :] = real
    ref[1, rows, :] = imag
    ref[2, rows, :] = real + imag


def kpoint_energy(medium, kmap, packed, z_out, y_out, y_s, g_s, f_s):
    flat, count_m = medium[0].shape
    count_k = kmap.shape[1]
    chans = math.isqrt(flat)
    width = packed.shape[1]
    onehot = (kmap == iota((count_m, count_k), 0)).astype(BF16)
    wide = (kmap == iota((width, count_k), 0) // chans).astype(BF16)
    same = iota((flat, width), 0) % chans == iota((flat, width), 1) % chans

    def fold(value):
        return jnp.sum(jnp.where(same, value, 0.0).reshape(chans, chans, width), axis=1)

    for part in range(2):
        value = mm_exact(medium[part], onehot)
        y_s[part] = value
        y_out[part] = value
    y_s[2] = y_s[0] + y_s[1]
    g_s[2] = g_s[0] + g_s[1]
    batch_mul(y_s, g_s, lambda base, real, imag: put3(f_s, base, chans, real, imag), chans)

    def write_z(base, real, imag):
        rows = pl.ds(pl.multiple_of(base, chans), chans)
        z_out[0, rows, :] = real + f_s[0, rows, :]
        z_out[1, rows, :] = imag + f_s[1, rows, :]

    batch_mul(f_s, f_s, write_z, chans)
    for part in range(2):
        parts = split(z_out[part], 3)
        total = mm_nt(parts[2], wide) + mm_nt(parts[1], wide) + mm_nt(parts[0], wide)
        packed[part * chans : (part + 1) * chans, :] = fold(total)

    return fold


def occupation_slots(place, occupation, weight, rows, width):
    count, sites = occupation.shape
    lane = iota((sites, width), 1) % SLOT
    to_slot = (iota((sites, width), 0) == lane).astype(BF16)
    slots = jnp.zeros((rows, width), F32)
    for g in range(count):
        filled = jnp.broadcast_to(occupation[g : g + 1, :].astype(BF16), (sites, sites))
        line = mm(filled, to_slot)[0:1] + jnp.where(lane[0:1] == sites, weight[g], 0.0)
        at = place * count + g
        per_row = width // SLOT
        here = (iota((rows, width), 0) == at // per_row) & (
            iota((rows, width), 1) // SLOT == at % per_row
        )
        slots = slots + jnp.where(here, line, 0.0)
    return slots


def send_kernel(
    place, weight, medium, structure, kmap, occupation,
    packed, z_out, y_out, medium_own, structure_own, kmap_own,
    y_s, g_s, f_s, medium_s, occupation_s, sems,
):
    own = place[0] % 2
    copies = [
        (kmap, kmap_own),
        (medium.at[1 - own], medium_s),
        (structure.at[1 - own, 0], g_s.at[0]),
        (structure.at[1 - own, 1], g_s.at[1]),
        (occupation, occupation_s),
        (medium.at[own], medium_own),
        (structure.at[own], structure_own),
    ]
    copies = [pltpu.make_async_copy(src, dst, sems.at[n]) for n, (src, dst) in enumerate(copies)]
    for copy in copies:
        copy.start()
    for copy in copies[:5]:
        copy.wait()
    medium_val = (medium_s[0], medium_s[1])
    kpoint_energy(medium_val, kmap_own[...], packed, z_out, y_out, y_s, g_s, f_s)
    half = 2 * math.isqrt(medium_s.shape[1])
    packed[half:, :] = occupation_slots(
        place[0], occupation_s[...], weight, packed.shape[0] - half, packed.shape[1]
    )
    for copy in copies[5:]:
        copy.wait()


def keep_kernel(sent, medium, structure, kmap, packed, z_out, y_out, y_row, y_s, g_s, f_s):
    for part in range(2):
        g_s[part] = structure[part]
    medium_val = (medium[0], medium[1])
    fold = kpoint_energy(medium_val, kmap[...], packed, z_out, y_out, y_s, g_s, f_s)
    half = 2 * y_row.shape[1]
    packed[half:, :] = sent[half:, :]
    count_m, width = medium.shape[2], packed.shape[1]
    lanes_of = (iota((count_m, width), 0) == iota((count_m, width), 1) * count_m // width).astype(BF16)
    for part in range(2):
        y_row[part] = fold(mm_exact(medium_val[part], lanes_of))


def square_kernel(y_in, z_in, out, y_s, z_s, t_s):
    flat = out.shape[1]
    chans = math.isqrt(flat)
    for part in range(2):
        y_s[part] = y_in[part]
        z_s[part] = z_in[part]
    y_s[2] = y_in[0] + y_in[1]
    z_s[2] = z_in[0] + z_in[1]

    def write_t(base, real, imag):
        rows = pl.ds(pl.multiple_of(base, chans), chans)
        put3(t_s, base, chans, real + y_s[0, rows, :], imag + y_s[1, rows, :])

    batch_mul(z_s, y_s, write_t, chans)

    def write_o(base, real, imag):
        rows = pl.ds(pl.multiple_of(base, chans), chans)
        out[0, rows, :] = real
        out[1, rows, :] = imag

    batch_mul(t_s, t_s, write_o, chans)


def cluster_kernel(
    per_moment, own_rows, place_diff,
    cfg_at, summed, y_row, shift_a, shift_b, fwd, back, phases,
    keep, send, lhs_s, site_s, corr_s, p_s, a_s, n_s,
):
    own = cfg_at[0] % 2
    chans = shift_a.shape[2]
    width = summed.shape[1]
    sites = phases.shape[1]
    own_sites = own_rows // chans
    rows_n = 2 * own_rows
    own_start = cfg_at[0] * own_sites
    other_start = (cfg_at[0] + 1 - 2 * own) * own_sites
    cols = (slice(0, chans), slice(chans, 2 * chans))

    y_val = (y_row[0], y_row[1])
    z_val = (summed[cols[0], :], summed[cols[1], :])
    y_diag = tuple(block_diag(v, chans) for v in y_val)
    coarse = cadd(y_val, cscale(cmul(z_val, y_diag), 1.0 / per_moment))

    base_t = (shift_b[own, 0], shift_b[own, 1])
    step_t = (shift_a[own, 0] - base_t[0], shift_a[own, 1] - base_t[1])

    stack = jnp.concatenate(base_t + step_t, axis=0)
    by_real = mm_high(stack, coarse[0])
    by_imag = mm_high(stack, coarse[1])

    def small_part(at):
        here, after = slice(at * chans, (at + 1) * chans), slice((at + 1) * chans, (at + 2) * chans)
        return (by_real[here] - by_imag[after], by_imag[here] + by_real[after])

    def rows_by(rows, diag):
        count = len(rows)
        out = cmul(
            tuple(jnp.concatenate([row[part] for row in rows], axis=0) for part in range(2)), diag
        )
        return [
            tuple(out[part][n * chans : (n + 1) * chans] for part in range(2)) for n in range(count)
        ]

    power, lead_kern = small_part(0), small_part(2)
    power_diag = tuple(block_diag(v, chans) for v in power)
    first, first_kern, power = rows_by([coarse, lead_kern, power], power_diag)
    first, first_kern = cscale(first, -1.0), cscale(first_kern, -1.0)
    power_diag = tuple(block_diag(v, chans) for v in power)
    second, third, second_kern = rows_by([coarse, first, lead_kern], power_diag)
    series = [coarse, first, second, third]
    kern = [lead_kern, first_kern, second_kern]
    whole = cadd(*series)

    for i in range(sites):
        phase = (phases[0, i : i + 1, :], phases[1, i : i + 1, :])
        for n, (real, imag) in enumerate(kern):
            start = n * width + i * chans
            lhs_s[0, start : start + chans, :] = phase[0] * real - phase[1] * imag
            lhs_s[1, start : start + chans, :] = phase[0] * imag + phase[1] * real

    base = 3 * width
    for i in range(2 * own_sites):
        site = own_start + i if i < own_sites else other_start + (i - own_sites)
        phase = (phases[0, pl.ds(site, 1), :], phases[1, pl.ds(site, 1), :])
        for n, (real, imag) in enumerate([whole] + series[:3]):
            start = base + n * rows_n + i * chans
            lhs_s[0, start : start + chans, :] = phase[0] * real - phase[1] * imag
            lhs_s[1, start : start + chans, :] = phase[0] * imag + phase[1] * real
    fwd_val = (fwd[0], fwd[1])

    for start in range(0, base + 4 * rows_n, width):
        rows = slice(start, start + width)
        out = cmul(
            (lhs_s[0, rows, :], lhs_s[1, rows, :]),
            fwd_val,
            functools.partial(mm_exact, pieces=2),
        )
        site_s[0, rows, :] = out[0]
        site_s[1, rows, :] = out[1]

    slots = summed[2 * chans :, :]
    groups = width // SLOT
    slot_of = iota(slots.shape, 1) // SLOT
    unpacked = jnp.concatenate([jnp.where(slot_of == n, slots, 0.0) for n in range(groups)], axis=0)
    place_in = iota((width, width), 0) % SLOT
    col = iota((width, width), 1)
    row_l = mm(unpacked.astype(BF16), (place_in == col // sites).astype(BF16))
    row_j = mm(unpacked.astype(BF16), (place_in == col % sites).astype(BF16))
    sites_in = (iota((sites, width), 1) % SLOT == iota((sites, width), 0)).astype(BF16)
    filled_t = mm_nt(sites_in, unpacked.astype(BF16)).astype(BF16)
    weights = jnp.sum(
        jnp.where(iota(unpacked.shape, 1) % SLOT == sites, unpacked, 0.0), axis=1, keepdims=True
    )
    norm = 1.0 / jnp.sum(weights, axis=0, keepdims=True)
    pieces = split(weights * (row_l * row_j), 3)
    triple = mm(filled_t, pieces[2]) + mm(filled_t, pieces[1]) + mm(filled_t, pieces[0])
    triple = triple * norm
    lane_l = iota((sites, width), 1) // sites
    lane_j = iota((sites, width), 1) % sites
    row_i = iota((sites, width), 0)
    pair = jnp.where(lane_l == row_i, triple, 0.0)
    single = jnp.sum(jnp.where(lane_j == row_i, pair, 0.0), axis=0, keepdims=True)
    stack = jnp.concatenate(
        [block_diag(triple, sites), pair, jnp.broadcast_to(single, (PAD_ROWS, width))], axis=0
    )
    spread_j = (
        iota((width, width), 0) % sites == iota((width, width), 1) // chans
    ).astype(BF16)
    corr_s[...] = mm_exact(stack, spread_j)

    hi_lo = []
    for part in range(2):
        hi, lo = split(site_s[part, 0:width, 0:chans], 2)
        hi_lo += [hi.astype(F32), hi.astype(F32), lo.astype(F32)]
    for n, piece in enumerate(hi_lo):
        a_s[:, n * chans : (n + 1) * chans] = piece
    a_val = a_s[:, 0 : 6 * chans].astype(BF16)
    for at in range(sites):
        rows = slice(at * chans, (at + 1) * chans)
        real_hi, real_lo = split(site_s[0, rows, :], 2)
        imag_hi, imag_lo = split(site_s[1, rows, :], 2)
        right_real = jnp.concatenate(
            [real_hi, real_lo, real_hi, -imag_hi, -imag_lo, -imag_hi], axis=0
        )
        right_imag = jnp.concatenate(
            [imag_hi, imag_lo, imag_hi, real_hi, real_lo, real_hi], axis=0
        )
        p_s[at, 0] = mm(a_val, right_real)
        p_s[at, 1] = mm(a_val, right_imag)

    occupied = corr_s[width + sites : width + sites + 1, :]

    for i in range(sites):
        rows = slice(i * chans, (i + 1) * chans)
        after = slice(width + i * chans, width + (i + 1) * chans)
        pair_row = corr_s[width + i : width + i + 1, :]
        on_diag = iota((chans, width), 0) + i * chans == iota((chans, width), 1)
        for part in range(2):
            total = None
            for at in range(sites):
                gap = int(place_diff[i, at])
                scale = corr_s[at * sites + i : at * sites + i + 1, :]
                term = scale * p_s[at, part, gap * chans : (gap + 1) * chans, :]
                total = term if total is None else total + term
            lead = pair_row * site_s[part, rows, :]
            if part == 0:
                lead = lead - jnp.where(on_diag, occupied, 0.0)
            n_s[part, after, :] = lead
            n_s[part, rows, :] = lead + pair_row * site_s[part, after, :] - total

    def site_rows(n):
        start = base + n * rows_n
        return (site_s[0, start : start + rows_n, :], site_s[1, start : start + rows_n, :])

    def kernel_of(n):
        rows = slice(n * width, (n + 1) * width)
        return (site_s[0, rows, :], site_s[1, rows, :])

    mid = [(n_s[0, n * width : (n + 1) * width, :], n_s[1, n * width : (n + 1) * width, :]) for n in range(2)]
    lead_rows = [site_rows(n) for n in range(4)]
    minus = -occupied
    q_zero = cadd(cmul(lead_rows[1], mid[0]), cmul(lead_rows[2], mid[1]), cscale(lead_rows[3], minus))
    q_one = cadd(cmul(lead_rows[1], mid[1]), cscale(lead_rows[2], minus))
    q_two = cscale(lead_rows[1], minus)
    result = cadd(
        lead_rows[0],
        cmul(q_zero, kernel_of(0)),
        cmul(q_one, kernel_of(1)),
        cmul(q_two, kernel_of(2)),
    )

    back_val = (back[0], back[1])
    means = []
    for n in range(2):
        moved = cmul(mid[n], back_val, functools.partial(mm_exact, pieces=2))
        total = None
        for i in range(sites):
            rows = slice(i * chans, (i + 1) * chans)
            phase = (phases[0, i : i + 1, :], phases[1, i : i + 1, :])
            real, imag = moved[0][rows], moved[1][rows]
            term = (phase[0] * real + phase[1] * imag, phase[0] * imag - phase[1] * real)
            total = term if total is None else cadd(total, term)
        means.append(total)
    mean_diag = [tuple(block_diag(v, chans) for v in pair_val) for pair_val in means]
    kern_diag = [tuple(block_diag(v, chans) for v in pair_val) for pair_val in kern]
    filled = -jnp.mean(occupied, axis=1, keepdims=True)
    u_zero = cadd(
        cmul(series[0], mean_diag[0]), cmul(series[1], mean_diag[1]), cscale(series[2], filled)
    )
    u_one = cadd(cmul(series[0], mean_diag[1]), cscale(series[1], filled))
    u_two = cscale(series[0], filled)
    change = cadd(
        series[1],
        series[2],
        series[3],
        cmul(u_zero, kern_diag[0]),
        cmul(u_one, kern_diag[1]),
        cmul(u_two, kern_diag[2]),
    )
    for ref, start in ((keep, 0), (send, own_rows)):
        for part in range(2):
            ref[part * own_rows : (part + 1) * own_rows, :] = result[part][start : start + own_rows]
            for n, value in enumerate((change, coarse)):
                at = 2 * own_rows + (2 * n + part) * chans
                ref[at : at + chans, :] = value[part]


def last_kernel(
    own_rows, cfg_at, kept, got, kmap, square_own, square_other, avg, coarse, correction
):
    own = cfg_at[0] % 2
    chans = (kept.shape[0] - 2 * own_rows) // 4
    width = kept.shape[1]
    flat = coarse.shape[2]
    count_m = coarse.shape[3]
    count_k = kmap.shape[1]
    onehot = kmap[...] == iota((count_m, count_k), 0)
    spread_b = (iota((chans, flat), 0) == iota((chans, flat), 1) % chans).astype(BF16)
    same_b = iota((width, flat), 0) % chans == iota((width, flat), 1) // chans
    pick_m = (iota((width, count_m), 0) // chans == iota((width, count_m), 1)).astype(BF16)
    same_c = iota((flat, width), 0) % chans == iota((flat, width), 1) % chans
    for at_slot, (ref, energy) in enumerate(((kept, own), (got, 1 - own))):
        moved = []
        for part in range(2):
            avg[energy, part] = ref[part * own_rows : (part + 1) * own_rows, :]
            at = 2 * own_rows + part * chans
            turned = mm_exact(ref[at : at + chans, :].T, spread_b)
            turned = jnp.where(same_b, turned, 0.0).reshape(count_m, chans, flat)
            moved.append(jnp.sum(turned, axis=1))
            at = 2 * own_rows + (2 + part) * chans
            row = ref[at : at + chans, :]
            tall = jnp.broadcast_to(row[:, None, :], (chans, chans, width)).reshape(flat, width)
            coarse[energy, part] = mm_exact(jnp.where(same_c, tall, 0.0), pick_m)
        both = jnp.concatenate(moved, axis=0)
        square = (square_own, square_other)[at_slot]
        by_real = mm3(both, square[0])
        by_imag = mm3(both, square[1])
        real = by_real[:count_m] - by_imag[count_m:]
        imag = by_imag[:count_m] + by_real[count_m:]
        correction[energy, 0:1, :] = jnp.sum(jnp.where(onehot, real, 0.0), axis=0, keepdims=True)
        correction[energy, 1:2, :] = jnp.sum(jnp.where(onehot, imag, 0.0), axis=0, keepdims=True)


def shape_of(*extent):
    return jax.ShapeDtypeStruct(extent, F32)


SMEM_SPEC = pl.BlockSpec(memory_space=pltpu.SMEM)
VMEM_SPEC = pl.BlockSpec(memory_space=pltpu.VMEM)


def call(body, outs, scratch, scalars, args, cost, spec=None):
    return pl.pallas_call(
        body,
        out_shape=outs,
        in_specs=[SMEM_SPEC] * scalars + [spec or VMEM_SPEC] * (len(args) - scalars),
        out_specs=jax.tree.map(lambda _: VMEM_SPEC, outs),
        scratch_shapes=scratch,
        compiler_params=pltpu.CompilerParams(vmem_limit_bytes=KERNEL_VMEM),
        cost_estimate=pl.CostEstimate(flops=cost, bytes_accessed=cost // 64, transcendentals=0),
    )(*args)


def exchange_stages(ka_size, cfg_size):
    total = ka_size * cfg_size
    bits = []
    step = 2
    while step < total:
        bits.append(step)
        step *= 2
    stages = []
    for at in range(0, len(bits), 2):
        group = bits[at : at + 2]
        stages.append(group if len(group) == 1 else [group[0], group[1], group[0] + group[1]])
    return stages


def swap(value, mask, total):
    return lax.ppermute(value, ("ka", "cfg"), [(i, i ^ mask) for i in range(total)])


def step(medium_t, structure, kmap, occupation, cfg_weight, shift_a, shift_b):
    ka_size, cfg_size = lax.axis_size("ka"), lax.axis_size("cfg")
    total = ka_size * cfg_size
    count_cfg = occupation.shape[0] * total
    sites = occupation.shape[1]
    chans, count_m = medium_t.shape[2], medium_t.shape[4]
    count_k = kmap.shape[0]
    flat = chans * chans
    width = count_m * chans
    per_moment = count_k * total // count_m
    own_sites = sites // cfg_size
    own_rows = own_sites * chans
    chip_rows = 2 * own_rows
    slot_rows = -(-count_cfg * SLOT // width)
    sum_rows = 2 * chans + -(-slot_rows // 8) * 8
    fwd, back, phases, place_diff = phase_constants(sites, chans)

    cfg_at = lax.axis_index("cfg").astype(jnp.int32).reshape(1)
    phases = jnp.asarray(phases)
    kmap_row = kmap.reshape(1, count_k)

    place = lax.axis_index(("ka", "cfg")).astype(jnp.int32).reshape(1)
    inputs = (
        place,
        cfg_weight,
        medium_t.reshape(ENERGIES, 2, flat, count_m),
        structure.reshape(ENERGIES, 2, flat, count_k),
        kmap_row,
        occupation,
    )
    inputs = inputs[:2] + tuple(
        pltpu.with_memory_space_constraint(value, pltpu.HBM) for value in inputs[2:]
    )
    outs = (
        shape_of(sum_rows, width),
        shape_of(2, flat, count_k),
        shape_of(2, flat, count_k),
    )
    own_outs = (
        shape_of(2, flat, count_m),
        shape_of(2, flat, count_k),
        jax.ShapeDtypeStruct((1, count_k), jnp.int32),
    )
    work = [pltpu.VMEM((3, flat, count_k), F32)] * 3
    local = [
        pltpu.VMEM((2, flat, count_m), F32),
        pltpu.VMEM(occupation.shape, jnp.int32),
        pltpu.SemaphoreType.DMA((7,)),
    ]
    send, z_other, y_other, *own = call(
        send_kernel,
        outs + own_outs,
        work + local,
        2,
        inputs,
        1 << 23,
        spec=pl.BlockSpec(memory_space=pltpu.HBM),
    )
    arrived = swap(send, 1, total)
    keep, z_own, y_own, y_row = call(
        keep_kernel, outs + (shape_of(2, chans, width),), work, 0, (send, *own), 1 << 23
    )
    summed = keep + arrived
    y_z = ((y_own, z_own), (y_other, z_other))
    squares = []
    for energy in range(ENERGIES):
        squares.append(
            call(
                square_kernel,
                shape_of(2, flat, count_k),
                [pltpu.VMEM((3, flat, count_k), F32)] * 3,
                0,
                y_z[energy],
                1 << 24,
            )
        )
    for stage in exchange_stages(ka_size, cfg_size):
        arrived = []
        for mask in stage:
            arrived.append(swap(summed, mask, total))
        for value in arrived:
            summed = summed + value
    out_rows = 2 * own_rows + 4 * chans
    lhs_rows = 3 * width + 4 * chip_rows
    kept, sent = call(
        functools.partial(cluster_kernel, per_moment, own_rows, place_diff),
        (shape_of(out_rows, width), shape_of(out_rows, width)),
        [
            pltpu.VMEM((2, lhs_rows, width), F32),
            pltpu.VMEM((2, lhs_rows, width), F32),
            pltpu.VMEM((width + sites + PAD_ROWS, width), F32),
            pltpu.VMEM((sites, 2, width, width), F32),
            pltpu.VMEM((width, 128), F32),
            pltpu.VMEM((2, 2 * width, width), F32),
        ],
        1,
        (
            cfg_at,
            summed,
            y_row,
            shift_a,
            shift_b,
            jnp.asarray(fwd, BF16),
            jnp.asarray(back, BF16),
            phases,
        ),
        1 << 26,
    )
    got = swap(sent, 1, total)
    avg, coarse, correction = call(
        functools.partial(last_kernel, own_rows),
        (
            shape_of(ENERGIES, 2, own_rows, width),
            shape_of(ENERGIES, 2, flat, count_m),
            shape_of(ENERGIES, 2, count_k),
        ),
        [],
        1,
        (cfg_at, kept, got, kmap_row, *squares),
        1 << 22,
    )
    return (coarse.reshape(ENERGIES, 2, chans, chans, count_m), avg, correction)


def solution(mesh):
    placed = (
        P(),
        P(None, None, None, None, ("ka", "cfg")),
        P(("ka", "cfg")),
        P(("ka", "cfg"), None),
        P(("ka", "cfg")),
        P(),
        P(),
    )
    return jax.shard_map(
        step,
        mesh=mesh,
        in_specs=placed,
        out_specs=(P(), P(None, None, "cfg", None), P(None, None, ("ka", "cfg"))),
        check_vma=False,
    )
```

```python
import functools
import math

import jax
import jax.numpy as jnp
import numpy as np
from jax import lax
from jax.experimental import pallas as pl
from jax.experimental.pallas import tpu as pltpu
from jax.sharding import PartitionSpec as P

ENERGIES = 2
F32 = jnp.float32
BF16 = jnp.bfloat16
PAD_ROWS = 8
SLOT = 32
KERNEL_VMEM = 20 << 20


def site_geometry(count_sites):
    places = np.arange(count_sites)
    half_n = count_sites // 2
    cell = places % half_n
    site_xyz = np.stack([cell // 4, cell // 2 % 2, cell % 2], axis=1).astype(np.float64)
    site_xyz = site_xyz + 0.5 * (places >= half_n)[:, None]
    mom_hkl = np.stack([places // 4, places // 2 % 2, places % 2], axis=1).astype(np.float64)
    angles = math.pi * (mom_hkl[:, None, :] * site_xyz[None, :, :]).sum(axis=2)
    place_diff = np.zeros((count_sites, count_sites), np.int32)
    for i in range(count_sites):
        for j in range(count_sites):
            gap = (site_xyz[i] - site_xyz[j]) % 2.0
            place_diff[i, j] = int(np.argmin(np.abs(site_xyz % 2.0 - gap).sum(axis=1)))
    return angles, place_diff


def phase_constants(count_sites, chans):
    angles, place_diff = site_geometry(count_sites)
    cells = count_sites // 2
    signs = np.rint(np.cos(angles[:, :cells]))
    turn = angles[:, cells]
    to_cells = np.kron(signs, np.eye(chans)) / count_sites
    turns = np.stack([np.rint(np.cos(turn)), np.rint(np.sin(turn))])
    turns = np.repeat(turns, chans, axis=1)
    return (
        jnp.asarray(to_cells, BF16),
        jnp.asarray(to_cells.T, BF16),
        jnp.asarray(np.concatenate([turns] * (chans // 2)), F32),
        place_diff,
    )


def iota(shape, dim):
    return lax.broadcasted_iota(jnp.int32, shape, dim)


def split(value, pieces):
    out = []
    for step in range(pieces):
        part = value.astype(BF16)
        out.append(part)
        if step + 1 < pieces:
            value = value - part.astype(F32)
    return out


def mm(left, right):
    return jnp.dot(left, right, preferred_element_type=F32)


def mm_nt(left, right):
    return lax.dot_general(left, right, (((1,), (1,)), ((), ())), preferred_element_type=F32)


def mm_exact(left, right_bf16, pieces=3):
    rows = left.shape[0]
    out = mm(jnp.concatenate(split(left, pieces), axis=0), right_bf16)
    total = out[(pieces - 1) * rows :]
    for at in range(pieces - 2, -1, -1):
        total = total + out[at * rows : (at + 1) * rows]
    return total


def mm3(left, right):
    rows = left.shape[0]
    left_hi, left_lo = split(left, 2)
    right_hi, right_lo = split(right, 2)
    out = mm(jnp.concatenate([left_hi, left_lo], axis=0), right_hi)
    return (mm(left_hi, right_lo) + out[rows:]) + out[:rows]


def mm3_deep(left, right):
    left_hi, left_lo = split(left, 2)
    right_hi, right_lo = split(right, 2)
    return mm(
        jnp.concatenate([left_hi, left_lo, left_hi], axis=1),
        jnp.concatenate([right_lo, right_hi, right_hi], axis=0),
    )


def mm_high(left, right):
    return jnp.dot(left, right, preferred_element_type=F32, precision=lax.Precision.HIGHEST)


def cmul(left, right, mul=mm3):
    rows = left[0].shape[0]
    both = jnp.concatenate(left, axis=0)
    by_real = mul(both, right[0])
    by_imag = mul(both, right[1])
    return (by_real[:rows] - by_imag[rows:], by_imag[:rows] + by_real[rows:])


def flip_cells(value, step):
    lanes = value.shape[1]
    ahead = pltpu.roll(value, step, 1)
    if 2 * step == lanes:
        return ahead
    behind = pltpu.roll(value, lanes - step, 1)
    return jnp.where(iota(value.shape, 1) // step % 2 == 1, ahead, behind)


def cell_orders(value, chans):
    count = value.shape[1] // chans
    orders = {0: value}
    at = 0
    for step in range(1, count):
        bit = count // 2
        while step % 2 == 0:
            step //= 2
            bit //= 2
        value = flip_cells(value, bit * chans)
        at ^= bit
        orders[at] = value
    return [orders[n] for n in range(count)]


def sum_cells(values, chans):
    bit = len(values) // 2
    while bit:
        values = [values[n] + flip_cells(values[n + bit], bit * chans) for n in range(bit)]
        bit //= 2
    return values[0]


def turned(value, turns, back=False):
    cos_t, sin_t = turns[0:1], turns[1:2]
    if back:
        sin_t = -sin_t
    return (cos_t * value[0] - sin_t * value[1], cos_t * value[1] + sin_t * value[0])


def cadd(*terms):
    real, imag = terms[0]
    for term in terms[1:]:
        real, imag = real + term[0], imag + term[1]
    return (real, imag)


def cscale(value, factor):
    return (value[0] * factor, value[1] * factor)


def block_diag(row, chans):
    width = row.shape[1]
    tiled = jnp.concatenate([row] * (width // chans), axis=0)
    keep = iota((width, width), 0) // chans == iota((width, width), 1) // chans
    return jnp.where(keep, tiled, 0.0)


def batch_mul(left, right, write, chans):
    group = 4

    def body(step, carry):
        base = step * (group * chans)
        sums = [[None] * 3 for _ in range(group)]
        for b in range(chans):
            rights = [right[part, b * chans : (b + 1) * chans, :] for part in range(3)]
            for g in range(group):
                for part in range(3):
                    lane = left[part, pl.ds(base + (g * chans + b), 1), :]
                    term = lane * rights[part]
                    old = sums[g][part]
                    sums[g][part] = term if old is None else old + term
        for g in range(group):
            both, twice, cross = sums[g]
            write(base + g * chans, both - twice, cross - both - twice)
        return carry

    lax.fori_loop(0, chans // group, body, 0)


def put3(ref, base, count, real, imag):
    rows = pl.ds(pl.multiple_of(base, count), count)
    ref[0, rows, :] = real
    ref[1, rows, :] = imag
    ref[2, rows, :] = real + imag


def kpoint_energy(medium, kmap, packed, z_out, y_out, y_s, g_s, f_s):
    flat, count_m = medium[0].shape
    count_k = kmap.shape[1]
    chans = math.isqrt(flat)
    width = packed.shape[1]
    onehot = (kmap == iota((count_m, count_k), 0)).astype(BF16)
    wide = (kmap == iota((width, count_k), 0) // chans).astype(BF16)
    same = iota((flat, width), 0) % chans == iota((flat, width), 1) % chans

    def fold(value):
        return jnp.sum(jnp.where(same, value, 0.0).reshape(chans, chans, width), axis=1)

    for part in range(2):
        value = mm_exact(medium[part], onehot)
        y_s[part] = value
        y_out[part] = value
    y_s[2] = y_s[0] + y_s[1]
    g_s[2] = g_s[0] + g_s[1]
    batch_mul(y_s, g_s, lambda base, real, imag: put3(f_s, base, chans, real, imag), chans)

    def write_z(base, real, imag):
        rows = pl.ds(pl.multiple_of(base, chans), chans)
        z_out[0, rows, :] = real + f_s[0, rows, :]
        z_out[1, rows, :] = imag + f_s[1, rows, :]

    batch_mul(f_s, f_s, write_z, chans)
    for part in range(2):
        parts = split(z_out[part], 3)
        total = mm_nt(parts[2], wide) + mm_nt(parts[1], wide) + mm_nt(parts[0], wide)
        packed[part * chans : (part + 1) * chans, :] = fold(total)

    return fold


def occupation_slots(place, occupation, weight, rows, width):
    count, sites = occupation.shape
    lane = iota((sites, width), 1) % SLOT
    to_slot = (iota((sites, width), 0) == lane).astype(BF16)
    slots = jnp.zeros((rows, width), F32)
    for g in range(count):
        filled = jnp.broadcast_to(occupation[g : g + 1, :].astype(BF16), (sites, sites))
        line = mm(filled, to_slot)[0:1] + jnp.where(lane[0:1] == sites, weight[g], 0.0)
        at = place * count + g
        per_row = width // SLOT
        here = (iota((rows, width), 0) == at // per_row) & (
            iota((rows, width), 1) // SLOT == at % per_row
        )
        slots = slots + jnp.where(here, line, 0.0)
    return slots


def send_kernel(
    place, weight, medium, structure, kmap, occupation,
    packed, z_out, y_out, medium_own, structure_own, kmap_own,
    y_s, g_s, f_s, medium_s, occupation_s, sems,
):
    own = place[0] % 2
    copies = [
        (kmap, kmap_own),
        (medium.at[1 - own], medium_s),
        (structure.at[1 - own, 0], g_s.at[0]),
        (structure.at[1 - own, 1], g_s.at[1]),
        (occupation, occupation_s),
        (medium.at[own], medium_own),
        (structure.at[own], structure_own),
    ]
    copies = [pltpu.make_async_copy(src, dst, sems.at[n]) for n, (src, dst) in enumerate(copies)]
    for copy in copies:
        copy.start()
    for copy in copies[:5]:
        copy.wait()
    medium_val = (medium_s[0], medium_s[1])
    kpoint_energy(medium_val, kmap_own[...], packed, z_out, y_out, y_s, g_s, f_s)
    half = 2 * math.isqrt(medium_s.shape[1])
    packed[half:, :] = occupation_slots(
        place[0], occupation_s[...], weight, packed.shape[0] - half, packed.shape[1]
    )
    for copy in copies[5:]:
        copy.wait()


def keep_kernel(sent, medium, structure, kmap, packed, z_out, y_out, y_row, y_s, g_s, f_s):
    for part in range(2):
        g_s[part] = structure[part]
    medium_val = (medium[0], medium[1])
    fold = kpoint_energy(medium_val, kmap[...], packed, z_out, y_out, y_s, g_s, f_s)
    half = 2 * y_row.shape[1]
    packed[half:, :] = sent[half:, :]
    count_m, width = medium.shape[2], packed.shape[1]
    lanes_of = (iota((count_m, width), 0) == iota((count_m, width), 1) * count_m // width).astype(BF16)
    for part in range(2):
        y_row[part] = fold(mm_exact(medium_val[part], lanes_of))


def square_kernel(y_in, z_in, out, y_s, z_s, t_s):
    flat = out.shape[1]
    chans = math.isqrt(flat)
    for part in range(2):
        y_s[part] = y_in[part]
        z_s[part] = z_in[part]
    y_s[2] = y_in[0] + y_in[1]
    z_s[2] = z_in[0] + z_in[1]

    def write_t(base, real, imag):
        rows = pl.ds(pl.multiple_of(base, chans), chans)
        put3(t_s, base, chans, real + y_s[0, rows, :], imag + y_s[1, rows, :])

    batch_mul(z_s, y_s, write_t, chans)

    def write_o(base, real, imag):
        rows = pl.ds(pl.multiple_of(base, chans), chans)
        out[0, rows, :] = real
        out[1, rows, :] = imag

    batch_mul(t_s, t_s, write_o, chans)


def cluster_kernel(
    per_moment, own_rows, place_diff,
    cfg_at, summed, y_row, shift_a, shift_b, to_cells, from_cells, turn_rows,
    keep, send, site_s, corr_s, p_s, a_s, n_s, c_s,
):
    own = cfg_at[0] % 2
    chans = shift_a.shape[2]
    width = summed.shape[1]
    sites = width // turn_rows.shape[0]
    cells = sites // 2
    half = cells * chans
    turns = turn_rows[0:2, :]
    own_sites = own_rows // chans
    rows_n = 2 * own_rows
    own_start = cfg_at[0] * own_sites
    other_start = (cfg_at[0] + 1 - 2 * own) * own_sites
    cols = (slice(0, chans), slice(chans, 2 * chans))

    y_val = (y_row[0], y_row[1])
    z_val = (summed[cols[0], :], summed[cols[1], :])
    y_diag = tuple(block_diag(v, chans) for v in y_val)
    coarse = cadd(y_val, cscale(cmul(z_val, y_diag), 1.0 / per_moment))

    base_t = (shift_b[own, 0], shift_b[own, 1])
    step_t = (shift_a[own, 0] - base_t[0], shift_a[own, 1] - base_t[1])

    stack = jnp.concatenate(base_t + step_t, axis=0)
    by_real = mm_high(stack, coarse[0])
    by_imag = mm_high(stack, coarse[1])

    def small_part(at):
        here, after = slice(at * chans, (at + 1) * chans), slice((at + 1) * chans, (at + 2) * chans)
        return (by_real[here] - by_imag[after], by_imag[here] + by_real[after])

    def rows_by(rows, diag):
        count = len(rows)
        out = cmul(
            tuple(jnp.concatenate([row[part] for row in rows], axis=0) for part in range(2)), diag
        )
        return [
            tuple(out[part][n * chans : (n + 1) * chans] for part in range(2)) for n in range(count)
        ]

    power, lead_kern = small_part(0), small_part(2)
    power_diag = tuple(block_diag(v, chans) for v in power)
    cell_map = to_cells[...]

    def to_differences(values):
        rows = []
        for step in range(2):
            for value in values:
                for variant in (value, turned(value, turns)):
                    rows += [split(part, 2)[step] for part in variant]
        out = mm(jnp.concatenate(rows, axis=0), cell_map)
        count = len(values) * 4 * chans
        out = out[count:] + out[:count]
        blocks = [out[n * chans : (n + 1) * chans] for n in range(4 * len(values))]
        return [
            [[blocks[4 * n + 2 * side + part] for part in range(2)] for side in range(2)]
            for n in range(len(values))
        ]

    def kern_to_sites(n, sides):
        start = n * width
        for part in range(2):
            lower = cell_orders(sides[0][part], chans)
            upper = cell_orders(sides[1][part], chans)
            for c in range(cells):
                low = slice(start + c * chans, start + (c + 1) * chans)
                high = slice(start + half + c * chans, start + half + (c + 1) * chans)
                site_s[part, low, 0:half] = lower[c]
                site_s[part, high, half:width] = lower[c]
                site_s[part, high, 0:half] = upper[c]
                site_s[part, low, half:width] = upper[c ^ (cells - 1)]

    first, first_kern, power = rows_by([coarse, lead_kern, power], power_diag)
    first, first_kern = cscale(first, -1.0), cscale(first_kern, -1.0)
    power_diag = tuple(block_diag(v, chans) for v in power)
    (lead_sides,) = to_differences([lead_kern])
    kern_to_sites(0, lead_sides)
    second, third, second_kern = rows_by([coarse, first, lead_kern], power_diag)
    series = [coarse, first, second, third]
    kern = [lead_kern, first_kern, second_kern]
    whole = cadd(*series)

    hi_lo = []
    for part in range(2):
        hi, lo = split(site_s[part, 0:width, 0:chans], 2)
        hi_lo += [hi.astype(F32), hi.astype(F32), lo.astype(F32)]
    for n, piece in enumerate(hi_lo):
        a_s[:, n * chans : (n + 1) * chans] = piece
    a_val = a_s[:, 0 : 6 * chans].astype(BF16)
    far = cells // 2
    for c in range(far):
        rows = slice(c * chans, (c + 1) * chans)
        high = slice(half + c * chans, half + (c + 1) * chans)
        pieces = []
        for part in range(2):
            line = jnp.concatenate([site_s[part, rows, 0:half], site_s[part, high, 0:half]], axis=1)
            pieces += split(line, 2)
        real_hi, real_lo, imag_hi, imag_lo = pieces
        for part, right in enumerate(
            (
                [real_hi, real_lo, real_hi, -imag_hi, -imag_lo, -imag_hi],
                [imag_hi, imag_lo, imag_hi, real_hi, real_lo, real_hi],
            )
        ):
            out = mm(a_val, jnp.concatenate(right, axis=0))
            for side in range(2):
                value = out[:, side * half : (side + 1) * half]
                p_s[c, side, part] = value
                p_s[c + far, side, part] = flip_cells(value, half // 2)

    others = [whole] + series[:3]
    sides_of = to_differences(kern[1:] + others)
    kern_to_sites(1, sides_of[0])
    kern_to_sites(2, sides_of[1])
    base = 3 * width
    for n, sides in enumerate(sides_of[2:]):
        for side in range(2):
            for part in range(2):
                for c, value in enumerate(cell_orders(sides[side][part], chans)):
                    c_s[n, side, part, c] = value
    for group, first_site in enumerate((own_start, other_start)):
        for i in range(own_sites):
            cell = (first_site + i) % cells
            above = (first_site + i) // cells
            turned_cell = above * cell + (1 - above) * (cells - 1 - cell)
            for n in range(4):
                start = base + n * rows_n + (group * own_sites + i) * chans
                for part in range(2):
                    site_s[part, start : start + chans, 0:half] = c_s[n, above, part, cell]
                    site_s[part, start : start + chans, half:width] = c_s[
                        n, 1 - above, part, turned_cell
                    ]

    slots = summed[2 * chans :, :]
    groups = width // SLOT
    slot_of = iota(slots.shape, 1) // SLOT
    unpacked = jnp.concatenate([jnp.where(slot_of == n, slots, 0.0) for n in range(groups)], axis=0)
    place_in = iota((width, width), 0) % SLOT
    col = iota((width, width), 1)
    row_l = mm(unpacked.astype(BF16), (place_in == col // sites).astype(BF16))
    row_j = mm(unpacked.astype(BF16), (place_in == col % sites).astype(BF16))
    sites_in = (iota((sites, width), 1) % SLOT == iota((sites, width), 0)).astype(BF16)
    filled_t = mm_nt(sites_in, unpacked.astype(BF16)).astype(BF16)
    weights = jnp.sum(
        jnp.where(iota(unpacked.shape, 1) % SLOT == sites, unpacked, 0.0), axis=1, keepdims=True
    )
    norm = 1.0 / jnp.sum(weights, axis=0, keepdims=True)
    pieces = split(weights * (row_l * row_j), 3)
    triple = mm(filled_t, pieces[2]) + mm(filled_t, pieces[1]) + mm(filled_t, pieces[0])
    triple = triple * norm
    lane_l = iota((sites, width), 1) // sites
    lane_j = iota((sites, width), 1) % sites
    row_i = iota((sites, width), 0)
    pair = jnp.where(lane_l == row_i, triple, 0.0)
    single = jnp.sum(jnp.where(lane_j == row_i, pair, 0.0), axis=0, keepdims=True)
    stack = jnp.concatenate(
        [block_diag(triple, sites), pair, jnp.broadcast_to(single, (PAD_ROWS, width))], axis=0
    )
    spread_j = (
        iota((width, width), 0) % sites == iota((width, width), 1) // chans
    ).astype(BF16)
    corr_s[...] = mm_exact(stack, spread_j)

    occupied = corr_s[width + sites : width + sites + 1, :]

    for i in range(sites):
        rows = slice(i * chans, (i + 1) * chans)
        after = slice(width + i * chans, width + (i + 1) * chans)
        pair_row = corr_s[width + i : width + i + 1, :]
        on_diag = iota((chans, width), 0) + i * chans == iota((chans, width), 1)
        for part in range(2):
            halves = []
            for side in range(2):
                lanes = slice(side * half, (side + 1) * half)
                total = None
                for at in range(sites):
                    gap = int(place_diff[i, at])
                    above, cell = divmod(at, cells)
                    if side == 1 and above == 0:
                        cell = cell ^ (cells - 1)
                    scale = corr_s[at * sites + i : at * sites + i + 1, lanes]
                    term = scale * p_s[cell, side ^ above, part, gap * chans : (gap + 1) * chans, :]
                    total = term if total is None else total + term
                halves.append(total)
            total = jnp.concatenate(halves, axis=1)
            lead = pair_row * site_s[part, rows, :]
            if part == 0:
                lead = lead - jnp.where(on_diag, occupied, 0.0)
            n_s[part, after, :] = lead
            n_s[part, rows, :] = lead + pair_row * site_s[part, after, :] - total

    mid = [(n_s[0, n * width : (n + 1) * width, :], n_s[1, n * width : (n + 1) * width, :]) for n in range(2)]
    stack = []
    for value in mid:
        for part in range(2):
            low = [value[part][c * chans : (c + 1) * chans] for c in range(cells)]
            high = [value[part][half + c * chans : half + (c + 1) * chans] for c in range(cells)]
            stack.append(
                sum_cells([low[c][:, :half] + high[c][:, half:] for c in range(cells)], chans)
            )
            crossed = sum_cells([low[c][:, half:] for c in range(cells)], chans)
            for bit in (1, 2, 4):
                crossed = flip_cells(crossed, bit * chans)
            stack.append(sum_cells([high[c][:, :half] for c in range(cells)], chans) + crossed)
    moved = mm_exact(jnp.concatenate(stack, axis=0), from_cells[...], pieces=2)
    moved = [moved[n * chans : (n + 1) * chans] for n in range(8)]
    means = [
        cadd(
            (moved[4 * n], moved[4 * n + 2]),
            turned((moved[4 * n + 1], moved[4 * n + 3]), turns, back=True),
        )
        for n in range(2)
    ]
    kern_diag = [tuple(block_diag(v, chans) for v in pair_val) for pair_val in kern[:2]]
    filled = -jnp.mean(occupied, axis=1, keepdims=True)
    mean_zero, mean_one, last = rows_by([means[0], means[1], series[2]], kern_diag[0])
    (mean_next,) = rows_by([means[1]], kern_diag[1])
    v_zero = cadd(mean_zero, mean_next, cscale(kern[2], filled))
    v_one = cadd(mean_one, cscale(kern[1], filled))
    change = cadd(
        series[1],
        series[2],
        series[3],
        cmul(series[0], tuple(block_diag(v, chans) for v in v_zero)),
        cmul(series[1], tuple(block_diag(v, chans) for v in v_one)),
        cscale(last, filled),
    )

    def site_rows(n):
        start = base + n * rows_n
        return (site_s[0, start : start + rows_n, :], site_s[1, start : start + rows_n, :])

    def side_by_side(*values):
        return tuple(jnp.concatenate([v[part] for v in values], axis=1) for part in range(2))

    lead_rows = [site_rows(n) for n in range(4)]
    minus = -occupied
    q_zero = cadd(
        cmul(side_by_side(lead_rows[1], lead_rows[2]), (n_s[0], n_s[1]), mm3_deep),
        cscale(lead_rows[3], minus),
    )
    q_one = cadd(cmul(lead_rows[1], mid[1], mm3_deep), cscale(lead_rows[2], minus))
    q_two = cscale(lead_rows[1], minus)
    kernels = (site_s[0, 0 : 3 * width, :], site_s[1, 0 : 3 * width, :])
    q_all = side_by_side(q_zero, q_one, q_two)
    parts = []
    for group in range(2):
        rows = slice(group * own_rows, (group + 1) * own_rows)
        parts.append(cmul(tuple(v[rows] for v in q_all), kernels, mm3_deep))
    result = cadd(
        lead_rows[0],
        tuple(jnp.concatenate([p[part] for p in parts], axis=0) for part in range(2)),
    )

    for ref, start in ((keep, 0), (send, own_rows)):
        for part in range(2):
            ref[part * own_rows : (part + 1) * own_rows, :] = result[part][start : start + own_rows]
            for n, value in enumerate((change, coarse)):
                at = 2 * own_rows + (2 * n + part) * chans
                ref[at : at + chans, :] = value[part]


def last_kernel(
    own_rows, cfg_at, kept, got, kmap, square_own, square_other, avg, coarse, correction
):
    own = cfg_at[0] % 2
    chans = (kept.shape[0] - 2 * own_rows) // 4
    width = kept.shape[1]
    flat = coarse.shape[2]
    count_m = coarse.shape[3]
    count_k = kmap.shape[1]
    onehot = kmap[...] == iota((count_m, count_k), 0)
    spread_b = (iota((chans, flat), 0) == iota((chans, flat), 1) % chans).astype(BF16)
    same_b = iota((width, flat), 0) % chans == iota((width, flat), 1) // chans
    pick_m = (iota((width, count_m), 0) // chans == iota((width, count_m), 1)).astype(BF16)
    same_c = iota((flat, width), 0) % chans == iota((flat, width), 1) % chans
    for at_slot, (ref, energy) in enumerate(((kept, own), (got, 1 - own))):
        moved = []
        for part in range(2):
            avg[energy, part] = ref[part * own_rows : (part + 1) * own_rows, :]
            at = 2 * own_rows + part * chans
            turned = mm_exact(ref[at : at + chans, :].T, spread_b)
            turned = jnp.where(same_b, turned, 0.0).reshape(count_m, chans, flat)
            moved.append(jnp.sum(turned, axis=1))
            at = 2 * own_rows + (2 + part) * chans
            row = ref[at : at + chans, :]
            tall = jnp.broadcast_to(row[:, None, :], (chans, chans, width)).reshape(flat, width)
            coarse[energy, part] = mm_exact(jnp.where(same_c, tall, 0.0), pick_m)
        both = jnp.concatenate(moved, axis=0)
        square = (square_own, square_other)[at_slot]
        by_real = mm3(both, square[0])
        by_imag = mm3(both, square[1])
        real = by_real[:count_m] - by_imag[count_m:]
        imag = by_imag[:count_m] + by_real[count_m:]
        correction[energy, 0:1, :] = jnp.sum(jnp.where(onehot, real, 0.0), axis=0, keepdims=True)
        correction[energy, 1:2, :] = jnp.sum(jnp.where(onehot, imag, 0.0), axis=0, keepdims=True)


def shape_of(*extent):
    return jax.ShapeDtypeStruct(extent, F32)


SMEM_SPEC = pl.BlockSpec(memory_space=pltpu.SMEM)
VMEM_SPEC = pl.BlockSpec(memory_space=pltpu.VMEM)


def call(body, outs, scratch, scalars, args, cost, spec=None):
    return pl.pallas_call(
        body,
        out_shape=outs,
        in_specs=[SMEM_SPEC] * scalars + [spec or VMEM_SPEC] * (len(args) - scalars),
        out_specs=jax.tree.map(lambda _: VMEM_SPEC, outs),
        scratch_shapes=scratch,
        compiler_params=pltpu.CompilerParams(vmem_limit_bytes=KERNEL_VMEM),
        cost_estimate=pl.CostEstimate(flops=cost, bytes_accessed=cost // 64, transcendentals=0),
    )(*args)


def exchange_stages(ka_size, cfg_size):
    total = ka_size * cfg_size
    bits = []
    step = 2
    while step < total:
        bits.append(step)
        step *= 2
    stages = []
    for at in range(0, len(bits), 2):
        group = bits[at : at + 2]
        stages.append(group if len(group) == 1 else [group[0], group[1], group[0] + group[1]])
    return stages


def swap(value, mask, total):
    return lax.ppermute(value, ("ka", "cfg"), [(i, i ^ mask) for i in range(total)])


def step(medium_t, structure, kmap, occupation, cfg_weight, shift_a, shift_b):
    ka_size, cfg_size = lax.axis_size("ka"), lax.axis_size("cfg")
    total = ka_size * cfg_size
    count_cfg = occupation.shape[0] * total
    sites = occupation.shape[1]
    chans, count_m = medium_t.shape[2], medium_t.shape[4]
    count_k = kmap.shape[0]
    flat = chans * chans
    width = count_m * chans
    per_moment = count_k * total // count_m
    own_sites = sites // cfg_size
    own_rows = own_sites * chans
    chip_rows = 2 * own_rows
    slot_rows = -(-count_cfg * SLOT // width)
    sum_rows = 2 * chans + -(-slot_rows // 8) * 8
    *tables, place_diff = phase_constants(sites, chans)

    cfg_at = lax.axis_index("cfg").astype(jnp.int32).reshape(1)
    kmap_row = kmap.reshape(1, count_k)

    place = lax.axis_index(("ka", "cfg")).astype(jnp.int32).reshape(1)
    inputs = (
        place,
        cfg_weight,
        medium_t.reshape(ENERGIES, 2, flat, count_m),
        structure.reshape(ENERGIES, 2, flat, count_k),
        kmap_row,
        occupation,
    )
    inputs = inputs[:2] + tuple(
        pltpu.with_memory_space_constraint(value, pltpu.HBM) for value in inputs[2:]
    )
    outs = (
        shape_of(sum_rows, width),
        shape_of(2, flat, count_k),
        shape_of(2, flat, count_k),
    )
    own_outs = (
        shape_of(2, flat, count_m),
        shape_of(2, flat, count_k),
        jax.ShapeDtypeStruct((1, count_k), jnp.int32),
    )
    work = [pltpu.VMEM((3, flat, count_k), F32)] * 3
    local = [
        pltpu.VMEM((2, flat, count_m), F32),
        pltpu.VMEM(occupation.shape, jnp.int32),
        pltpu.SemaphoreType.DMA((7,)),
    ]
    send, z_other, y_other, *own = call(
        send_kernel,
        outs + own_outs,
        work + local,
        2,
        inputs,
        1 << 23,
        spec=pl.BlockSpec(memory_space=pltpu.HBM),
    )
    arrived = swap(send, 1, total)
    keep, z_own, y_own, y_row = call(
        keep_kernel, outs + (shape_of(2, chans, width),), work, 0, (send, *own), 1 << 23
    )
    summed = keep + arrived
    y_z = ((y_own, z_own), (y_other, z_other))
    squares = []
    for energy in range(ENERGIES):
        squares.append(
            call(
                square_kernel,
                shape_of(2, flat, count_k),
                [pltpu.VMEM((3, flat, count_k), F32)] * 3,
                0,
                y_z[energy],
                1 << 24,
            )
        )
    for stage in exchange_stages(ka_size, cfg_size):
        arrived = []
        for mask in stage:
            arrived.append(swap(summed, mask, total))
        for value in arrived:
            summed = summed + value
    out_rows = 2 * own_rows + 4 * chans
    kept, sent = call(
        functools.partial(cluster_kernel, per_moment, own_rows, place_diff),
        (shape_of(out_rows, width), shape_of(out_rows, width)),
        [
            pltpu.VMEM((2, 3 * width + 4 * chip_rows, width), F32),
            pltpu.VMEM((width + sites + PAD_ROWS, width), F32),
            pltpu.VMEM((sites // 2, 2, 2, width, width // 2), F32),
            pltpu.VMEM((width, 128), F32),
            pltpu.VMEM((2, 2 * width, width), F32),
            pltpu.VMEM((4, 2, 2, sites // 2, chans, width // 2), F32),
        ],
        1,
        (
            cfg_at,
            summed,
            y_row,
            shift_a,
            shift_b,
            *tables,
        ),
        1 << 26,
    )
    got = swap(sent, 1, total)
    avg, coarse, correction = call(
        functools.partial(last_kernel, own_rows),
        (
            shape_of(ENERGIES, 2, own_rows, width),
            shape_of(ENERGIES, 2, flat, count_m),
            shape_of(ENERGIES, 2, count_k),
        ),
        [],
        1,
        (cfg_at, kept, got, kmap_row, *squares),
        1 << 22,
    )
    return (coarse.reshape(ENERGIES, 2, chans, chans, count_m), avg, correction)


def solution(mesh):
    placed = (
        P(),
        P(None, None, None, None, ("ka", "cfg")),
        P(("ka", "cfg")),
        P(("ka", "cfg"), None),
        P(("ka", "cfg")),
        P(),
        P(),
    )
    return jax.shard_map(
        step,
        mesh=mesh,
        in_specs=placed,
        out_specs=(P(), P(None, None, "cfg", None), P(None, None, ("ka", "cfg"))),
        check_vma=False,
    )
```

```python
import functools
import math

import jax
import jax.numpy as jnp
import numpy as np
from jax import lax
from jax.experimental import pallas as pl
from jax.experimental.pallas import tpu as pltpu
from jax.sharding import PartitionSpec as P

ENERGIES = 2
F32 = jnp.float32
BF16 = jnp.bfloat16
PAD_ROWS = 8
SLOT = 32
KERNEL_VMEM = 20 << 20


def site_geometry(count_sites):
    places = np.arange(count_sites)
    half_n = count_sites // 2
    cell = places % half_n
    site_xyz = np.stack([cell // 4, cell // 2 % 2, cell % 2], axis=1).astype(np.float64)
    site_xyz = site_xyz + 0.5 * (places >= half_n)[:, None]
    mom_hkl = np.stack([places // 4, places // 2 % 2, places % 2], axis=1).astype(np.float64)
    angles = math.pi * (mom_hkl[:, None, :] * site_xyz[None, :, :]).sum(axis=2)
    place_diff = np.zeros((count_sites, count_sites), np.int32)
    for i in range(count_sites):
        for j in range(count_sites):
            gap = (site_xyz[i] - site_xyz[j]) % 2.0
            place_diff[i, j] = int(np.argmin(np.abs(site_xyz % 2.0 - gap).sum(axis=1)))
    return angles, place_diff


def phase_constants(count_sites, chans):
    angles, place_diff = site_geometry(count_sites)
    cells = count_sites // 2
    signs = np.rint(np.cos(angles[:, :cells]))
    turn = angles[:, cells]
    to_cells = np.kron(signs, np.eye(chans)) / count_sites
    turns = np.stack([np.rint(np.cos(turn)), np.rint(np.sin(turn))])
    turns = np.repeat(turns, chans, axis=1)
    return (
        jnp.asarray(to_cells, BF16),
        jnp.asarray(to_cells.T, BF16),
        jnp.asarray(np.concatenate([turns] * (chans // 2)), F32),
        place_diff,
    )


def iota(shape, dim):
    return lax.broadcasted_iota(jnp.int32, shape, dim)


def split(value, pieces):
    out = []
    for step in range(pieces):
        part = value.astype(BF16)
        out.append(part)
        if step + 1 < pieces:
            value = value - part.astype(F32)
    return out


def mm(left, right):
    return jnp.dot(left, right, preferred_element_type=F32)


def mm_nt(left, right):
    return lax.dot_general(left, right, (((1,), (1,)), ((), ())), preferred_element_type=F32)


def mm_exact(left, right_bf16, pieces=3):
    rows = left.shape[0]
    out = mm(jnp.concatenate(split(left, pieces), axis=0), right_bf16)
    total = out[(pieces - 1) * rows :]
    for at in range(pieces - 2, -1, -1):
        total = total + out[at * rows : (at + 1) * rows]
    return total


def mm3(left, right):
    rows = left.shape[0]
    left_hi, left_lo = split(left, 2)
    right_hi, right_lo = split(right, 2)
    out = mm(jnp.concatenate([left_hi, left_lo], axis=0), right_hi)
    return (mm(left_hi, right_lo) + out[rows:]) + out[:rows]


def mm3_deep(left, right):
    left_hi, left_lo = split(left, 2)
    right_hi, right_lo = split(right, 2)
    return mm(
        jnp.concatenate([left_hi, left_lo, left_hi], axis=1),
        jnp.concatenate([right_lo, right_hi, right_hi], axis=0),
    )


def mm_high(left, right):
    return jnp.dot(left, right, preferred_element_type=F32, precision=lax.Precision.HIGHEST)


def cmul(left, right, mul=mm3):
    rows = left[0].shape[0]
    both = jnp.concatenate(left, axis=0)
    by_real = mul(both, right[0])
    by_imag = mul(both, right[1])
    return (by_real[:rows] - by_imag[rows:], by_imag[:rows] + by_real[rows:])


def flip_cells(value, step):
    lanes = value.shape[1]
    ahead = pltpu.roll(value, step, 1)
    if 2 * step == lanes:
        return ahead
    behind = pltpu.roll(value, lanes - step, 1)
    return jnp.where(iota(value.shape, 1) // step % 2 == 1, ahead, behind)


def cell_orders(value, chans):
    count = value.shape[1] // chans
    orders = {0: value}
    at = 0
    for step in range(1, count):
        bit = count // 2
        while step % 2 == 0:
            step //= 2
            bit //= 2
        value = flip_cells(value, bit * chans)
        at ^= bit
        orders[at] = value
    return [orders[n] for n in range(count)]


def sum_cells(values, chans):
    bit = len(values) // 2
    while bit:
        values = [values[n] + flip_cells(values[n + bit], bit * chans) for n in range(bit)]
        bit //= 2
    return values[0]


def turned(value, turns, back=False):
    cos_t, sin_t = turns[0:1], turns[1:2]
    if back:
        sin_t = -sin_t
    return (cos_t * value[0] - sin_t * value[1], cos_t * value[1] + sin_t * value[0])


def cadd(*terms):
    real, imag = terms[0]
    for term in terms[1:]:
        real, imag = real + term[0], imag + term[1]
    return (real, imag)


def cscale(value, factor):
    return (value[0] * factor, value[1] * factor)


def block_diag(row, chans):
    width = row.shape[1]
    tiled = jnp.concatenate([row] * (width // chans), axis=0)
    keep = iota((width, width), 0) // chans == iota((width, width), 1) // chans
    return jnp.where(keep, tiled, 0.0)


def batch_mul(left, right, write, chans):
    group = 4

    def body(step, carry):
        base = step * (group * chans)
        sums = [[None] * 3 for _ in range(group)]
        for b in range(chans):
            rights = [right[part, b * chans : (b + 1) * chans, :] for part in range(3)]
            for g in range(group):
                for part in range(3):
                    lane = left[part, pl.ds(base + (g * chans + b), 1), :]
                    term = lane * rights[part]
                    old = sums[g][part]
                    sums[g][part] = term if old is None else old + term
        for g in range(group):
            both, twice, cross = sums[g]
            write(base + g * chans, both - twice, cross - both - twice)
        return carry

    lax.fori_loop(0, chans // group, body, 0)


def put3(ref, base, count, real, imag):
    rows = pl.ds(pl.multiple_of(base, count), count)
    ref[0, rows, :] = real
    ref[1, rows, :] = imag
    ref[2, rows, :] = real + imag


def kpoint_energy(medium, kmap, packed, z_out, y_out, y_s, g_s, f_s):
    flat, count_m = medium[0].shape
    count_k = kmap.shape[1]
    chans = math.isqrt(flat)
    width = packed.shape[1]
    onehot = (kmap == iota((count_m, count_k), 0)).astype(BF16)
    wide = (kmap == iota((width, count_k), 0) // chans).astype(BF16)
    same = iota((flat, width), 0) % chans == iota((flat, width), 1) % chans

    def fold(value):
        return jnp.sum(jnp.where(same, value, 0.0).reshape(chans, chans, width), axis=1)

    for part in range(2):
        value = mm_exact(medium[part], onehot)
        y_s[part] = value
        y_out[part] = value
    y_s[2] = y_s[0] + y_s[1]
    g_s[2] = g_s[0] + g_s[1]
    batch_mul(y_s, g_s, lambda base, real, imag: put3(f_s, base, chans, real, imag), chans)

    def write_z(base, real, imag):
        rows = pl.ds(pl.multiple_of(base, chans), chans)
        z_out[0, rows, :] = real + f_s[0, rows, :]
        z_out[1, rows, :] = imag + f_s[1, rows, :]

    batch_mul(f_s, f_s, write_z, chans)
    for part in range(2):
        parts = split(z_out[part], 3)
        total = mm_nt(parts[2], wide) + mm_nt(parts[1], wide) + mm_nt(parts[0], wide)
        packed[part * chans : (part + 1) * chans, :] = fold(total)

    return fold


def occupation_slots(place, occupation, weight, rows, width):
    count, sites = occupation.shape
    lane = iota((sites, width), 1) % SLOT
    to_slot = (iota((sites, width), 0) == lane).astype(BF16)
    slots = jnp.zeros((rows, width), F32)
    for g in range(count):
        filled = jnp.broadcast_to(occupation[g : g + 1, :].astype(BF16), (sites, sites))
        line = mm(filled, to_slot)[0:1] + jnp.where(lane[0:1] == sites, weight[g], 0.0)
        at = place * count + g
        per_row = width // SLOT
        here = (iota((rows, width), 0) == at // per_row) & (
            iota((rows, width), 1) // SLOT == at % per_row
        )
        slots = slots + jnp.where(here, line, 0.0)
    return slots


def send_kernel(
    place, weight, medium, structure, kmap, occupation,
    packed, z_out, y_out, medium_own, structure_own, kmap_own,
    y_s, g_s, f_s, medium_s, occupation_s, sems,
):
    own = place[0] % 2
    copies = [
        (kmap, kmap_own),
        (medium.at[1 - own], medium_s),
        (structure.at[1 - own, 0], g_s.at[0]),
        (structure.at[1 - own, 1], g_s.at[1]),
        (occupation, occupation_s),
        (medium.at[own], medium_own),
        (structure.at[own], structure_own),
    ]
    copies = [pltpu.make_async_copy(src, dst, sems.at[n]) for n, (src, dst) in enumerate(copies)]
    for copy in copies:
        copy.start()
    for copy in copies[:5]:
        copy.wait()
    medium_val = (medium_s[0], medium_s[1])
    kpoint_energy(medium_val, kmap_own[...], packed, z_out, y_out, y_s, g_s, f_s)
    half = 2 * math.isqrt(medium_s.shape[1])
    packed[half:, :] = occupation_slots(
        place[0], occupation_s[...], weight, packed.shape[0] - half, packed.shape[1]
    )
    for copy in copies[5:]:
        copy.wait()


def keep_kernel(sent, medium, structure, kmap, packed, z_out, y_out, y_row, y_s, g_s, f_s):
    for part in range(2):
        g_s[part] = structure[part]
    medium_val = (medium[0], medium[1])
    fold = kpoint_energy(medium_val, kmap[...], packed, z_out, y_out, y_s, g_s, f_s)
    half = 2 * y_row.shape[1]
    packed[half:, :] = sent[half:, :]
    count_m, width = medium.shape[2], packed.shape[1]
    lanes_of = (iota((count_m, width), 0) == iota((count_m, width), 1) * count_m // width).astype(BF16)
    for part in range(2):
        y_row[part] = fold(mm_exact(medium_val[part], lanes_of))


def square_kernel(y_in, z_in, out, y_s, z_s, t_s):
    flat = out.shape[1]
    chans = math.isqrt(flat)
    for part in range(2):
        y_s[part] = y_in[part]
        z_s[part] = z_in[part]
    y_s[2] = y_in[0] + y_in[1]
    z_s[2] = z_in[0] + z_in[1]

    def write_t(base, real, imag):
        rows = pl.ds(pl.multiple_of(base, chans), chans)
        put3(t_s, base, chans, real + y_s[0, rows, :], imag + y_s[1, rows, :])

    batch_mul(z_s, y_s, write_t, chans)

    def write_o(base, real, imag):
        rows = pl.ds(pl.multiple_of(base, chans), chans)
        out[0, rows, :] = real
        out[1, rows, :] = imag

    batch_mul(t_s, t_s, write_o, chans)


def cluster_kernel(
    per_moment, own_rows, place_diff,
    cfg_at, summed, y_row, shift_a, shift_b, to_cells, from_cells, turn_rows,
    keep, send, site_s, corr_s, p_s, a_s, n_s, c_s,
):
    own = cfg_at[0] % 2
    chans = shift_a.shape[2]
    width = summed.shape[1]
    sites = width // turn_rows.shape[0]
    cells = sites // 2
    half = cells * chans
    turns = turn_rows[0:2, :]
    own_sites = own_rows // chans
    rows_n = 2 * own_rows
    own_start = cfg_at[0] * own_sites
    other_start = (cfg_at[0] + 1 - 2 * own) * own_sites
    cols = (slice(0, chans), slice(chans, 2 * chans))

    y_val = (y_row[0], y_row[1])
    z_val = (summed[cols[0], :], summed[cols[1], :])
    y_diag = tuple(block_diag(v, chans) for v in y_val)
    coarse = cadd(y_val, cscale(cmul(z_val, y_diag), 1.0 / per_moment))

    base_t = (shift_b[own, 0], shift_b[own, 1])
    step_t = (shift_a[own, 0] - base_t[0], shift_a[own, 1] - base_t[1])

    stack = jnp.concatenate(base_t + step_t, axis=0)
    by_real = mm_high(stack, coarse[0])
    by_imag = mm_high(stack, coarse[1])

    def small_part(at):
        here, after = slice(at * chans, (at + 1) * chans), slice((at + 1) * chans, (at + 2) * chans)
        return (by_real[here] - by_imag[after], by_imag[here] + by_real[after])

    def rows_by(rows, diag):
        count = len(rows)
        out = cmul(
            tuple(jnp.concatenate([row[part] for row in rows], axis=0) for part in range(2)), diag
        )
        return [
            tuple(out[part][n * chans : (n + 1) * chans] for part in range(2)) for n in range(count)
        ]

    power, lead_kern = small_part(0), small_part(2)
    power_diag = tuple(block_diag(v, chans) for v in power)
    cell_map = to_cells[...]

    def to_differences(values):
        rows = []
        for step in range(2):
            for value in values:
                for variant in (value, turned(value, turns)):
                    rows += [split(part, 2)[step] for part in variant]
        out = mm(jnp.concatenate(rows, axis=0), cell_map)
        count = len(values) * 4 * chans
        out = out[count:] + out[:count]
        blocks = [out[n * chans : (n + 1) * chans] for n in range(4 * len(values))]
        return [
            [[blocks[4 * n + 2 * side + part] for part in range(2)] for side in range(2)]
            for n in range(len(values))
        ]

    def kern_to_sites(n, sides):
        start = n * width
        for part in range(2):
            lower = cell_orders(sides[0][part], chans)
            upper = cell_orders(sides[1][part], chans)
            for c in range(cells):
                low = slice(start + c * chans, start + (c + 1) * chans)
                high = slice(start + half + c * chans, start + half + (c + 1) * chans)
                site_s[part, low, 0:half] = lower[c]
                site_s[part, high, half:width] = lower[c]
                site_s[part, high, 0:half] = upper[c]
                site_s[part, low, half:width] = upper[c ^ (cells - 1)]

    first, first_kern, power = rows_by([coarse, lead_kern, power], power_diag)
    first, first_kern = cscale(first, -1.0), cscale(first_kern, -1.0)
    power_diag = tuple(block_diag(v, chans) for v in power)
    (lead_sides,) = to_differences([lead_kern])
    kern_to_sites(0, lead_sides)
    second, third, second_kern = rows_by([coarse, first, lead_kern], power_diag)
    series = [coarse, first, second, third]
    kern = [lead_kern, first_kern, second_kern]
    whole = cadd(*series)

    hi_lo = []
    for part in range(2):
        hi, lo = split(site_s[part, 0:width, 0:chans], 2)
        hi_lo += [hi.astype(F32), hi.astype(F32), lo.astype(F32)]
    for n, piece in enumerate(hi_lo):
        a_s[:, n * chans : (n + 1) * chans] = piece
    a_val = a_s[:, 0 : 6 * chans].astype(BF16)
    far = cells // 2
    for c in range(far):
        rows = slice(c * chans, (c + 1) * chans)
        high = slice(half + c * chans, half + (c + 1) * chans)
        pieces = []
        for part in range(2):
            line = jnp.concatenate([site_s[part, rows, 0:half], site_s[part, high, 0:half]], axis=1)
            pieces += split(line, 2)
        real_hi, real_lo, imag_hi, imag_lo = pieces
        for part, right in enumerate(
            (
                [real_hi, real_lo, real_hi, -imag_hi, -imag_lo, -imag_hi],
                [imag_hi, imag_lo, imag_hi, real_hi, real_lo, real_hi],
            )
        ):
            out = mm(a_val, jnp.concatenate(right, axis=0))
            for side in range(2):
                value = out[:, side * half : (side + 1) * half]
                p_s[c, side, part] = value
                p_s[c + far, side, part] = flip_cells(value, half // 2)

    others = [whole] + series[:3]
    sides_of = to_differences(kern[1:] + others)
    kern_to_sites(1, sides_of[0])
    base = 3 * width
    slots = summed[2 * chans :, :]
    groups = width // SLOT
    slot_of = iota(slots.shape, 1) // SLOT
    unpacked = jnp.concatenate([jnp.where(slot_of == n, slots, 0.0) for n in range(groups)], axis=0)
    place_in = iota((width, width), 0) % SLOT
    col = iota((width, width), 1)
    row_l = mm(unpacked.astype(BF16), (place_in == col // sites).astype(BF16))
    row_j = mm(unpacked.astype(BF16), (place_in == col % sites).astype(BF16))
    sites_in = (iota((sites, width), 1) % SLOT == iota((sites, width), 0)).astype(BF16)
    filled_t = mm_nt(sites_in, unpacked.astype(BF16)).astype(BF16)
    weights = jnp.sum(
        jnp.where(iota(unpacked.shape, 1) % SLOT == sites, unpacked, 0.0), axis=1, keepdims=True
    )
    norm = 1.0 / jnp.sum(weights, axis=0, keepdims=True)
    pieces = split(weights * (row_l * row_j), 3)
    triple = mm(filled_t, pieces[2]) + mm(filled_t, pieces[1]) + mm(filled_t, pieces[0])
    triple = triple * norm
    lane_l = iota((sites, width), 1) // sites
    lane_j = iota((sites, width), 1) % sites
    row_i = iota((sites, width), 0)
    pair = jnp.where(lane_l == row_i, triple, 0.0)
    single = jnp.sum(jnp.where(lane_j == row_i, pair, 0.0), axis=0, keepdims=True)
    stack = jnp.concatenate(
        [block_diag(triple, sites), pair, jnp.broadcast_to(single, (PAD_ROWS, width))], axis=0
    )
    spread_j = (
        iota((width, width), 0) % sites == iota((width, width), 1) // chans
    ).astype(BF16)
    corr_s[...] = mm_exact(stack, spread_j)

    occupied = corr_s[width + sites : width + sites + 1, :]

    pending = [(n, side, part) for n in range(4) for side in range(2) for part in range(2)]
    for i in range(sites):
        rows = slice(i * chans, (i + 1) * chans)
        after = slice(width + i * chans, width + (i + 1) * chans)
        pair_row = corr_s[width + i : width + i + 1, :]
        on_diag = iota((chans, width), 0) + i * chans == iota((chans, width), 1)
        halves = []
        for side in range(2):
            lanes = slice(side * half, (side + 1) * half)
            totals = [None, None]
            for at in range(sites):
                gap = int(place_diff[i, at])
                above, cell = divmod(at, cells)
                if side == 1 and above == 0:
                    cell = cell ^ (cells - 1)
                scale = corr_s[at * sites + i : at * sites + i + 1, lanes]
                scale = jnp.broadcast_to(scale, (chans, half))
                for part in range(2):
                    term = scale * p_s[cell, side ^ above, part, gap * chans : (gap + 1) * chans, :]
                    totals[part] = term if totals[part] is None else totals[part] + term
            halves.append(totals)
        for part in range(2):
            total = jnp.concatenate([halves[0][part], halves[1][part]], axis=1)
            lead = pair_row * site_s[part, rows, :]
            if part == 0:
                lead = lead - jnp.where(on_diag, occupied, 0.0)
            n_s[part, after, :] = lead
            n_s[part, rows, :] = lead + pair_row * site_s[part, after, :] - total
        if i == sites // 2:
            kern_to_sites(2, sides_of[1])
        for n, side, part in pending[i * len(pending) // sites : (i + 1) * len(pending) // sites]:
            for c, value in enumerate(cell_orders(sides_of[2 + n][side][part], chans)):
                c_s[n, side, part, c] = value
    for group, first_site in enumerate((own_start, other_start)):
        for i in range(own_sites):
            cell = (first_site + i) % cells
            above = (first_site + i) // cells
            turned_cell = above * cell + (1 - above) * (cells - 1 - cell)
            for n in range(4):
                start = base + n * rows_n + (group * own_sites + i) * chans
                for part in range(2):
                    site_s[part, start : start + chans, 0:half] = c_s[n, above, part, cell]
                    site_s[part, start : start + chans, half:width] = c_s[
                        n, 1 - above, part, turned_cell
                    ]

    mid = [(n_s[0, n * width : (n + 1) * width, :], n_s[1, n * width : (n + 1) * width, :]) for n in range(2)]

    def site_rows(n):
        start = base + n * rows_n
        return (site_s[0, start : start + rows_n, :], site_s[1, start : start + rows_n, :])

    def side_by_side(*values):
        return tuple(jnp.concatenate([v[part] for v in values], axis=1) for part in range(2))

    lead_rows = [site_rows(n) for n in range(4)]
    minus = -occupied
    q_zero = cadd(
        cmul(side_by_side(lead_rows[1], lead_rows[2]), (n_s[0], n_s[1]), mm3_deep),
        cscale(lead_rows[3], minus),
    )
    q_one = cadd(cmul(lead_rows[1], mid[1], mm3_deep), cscale(lead_rows[2], minus))
    stack = []
    for value in mid:
        for part in range(2):
            low = [value[part][c * chans : (c + 1) * chans] for c in range(cells)]
            high = [value[part][half + c * chans : half + (c + 1) * chans] for c in range(cells)]
            stack.append(
                sum_cells([low[c][:, :half] + high[c][:, half:] for c in range(cells)], chans)
            )
            crossed = sum_cells([low[c][:, half:] for c in range(cells)], chans)
            for bit in (1, 2, 4):
                crossed = flip_cells(crossed, bit * chans)
            stack.append(sum_cells([high[c][:, :half] for c in range(cells)], chans) + crossed)
    moved = mm_exact(jnp.concatenate(stack, axis=0), from_cells[...], pieces=2)
    moved = [moved[n * chans : (n + 1) * chans] for n in range(8)]
    means = [
        cadd(
            (moved[4 * n], moved[4 * n + 2]),
            turned((moved[4 * n + 1], moved[4 * n + 3]), turns, back=True),
        )
        for n in range(2)
    ]
    kern_diag = [tuple(block_diag(v, chans) for v in pair_val) for pair_val in kern[:2]]
    filled = -jnp.mean(occupied, axis=1, keepdims=True)
    mean_zero, mean_one, last = rows_by([means[0], means[1], series[2]], kern_diag[0])
    (mean_next,) = rows_by([means[1]], kern_diag[1])
    v_zero = cadd(mean_zero, mean_next, cscale(kern[2], filled))
    v_one = cadd(mean_one, cscale(kern[1], filled))
    change = cadd(
        series[1],
        series[2],
        series[3],
        cmul(series[0], tuple(block_diag(v, chans) for v in v_zero)),
        cmul(series[1], tuple(block_diag(v, chans) for v in v_one)),
        cscale(last, filled),
    )
    q_two = cscale(lead_rows[1], minus)
    kernels = (site_s[0, 0 : 3 * width, :], site_s[1, 0 : 3 * width, :])
    q_all = side_by_side(q_zero, q_one, q_two)
    parts = []
    for group in range(2):
        rows = slice(group * own_rows, (group + 1) * own_rows)
        parts.append(cmul(tuple(v[rows] for v in q_all), kernels, mm3_deep))
    result = cadd(
        lead_rows[0],
        tuple(jnp.concatenate([p[part] for p in parts], axis=0) for part in range(2)),
    )

    for ref, start in ((keep, 0), (send, own_rows)):
        for part in range(2):
            ref[part * own_rows : (part + 1) * own_rows, :] = result[part][start : start + own_rows]
            for n, value in enumerate((change, coarse)):
                at = 2 * own_rows + (2 * n + part) * chans
                ref[at : at + chans, :] = value[part]


def finish_energy(own_rows, ref, kmap, square, coarse, correction):
    chans = (ref.shape[0] - 2 * own_rows) // 4
    width = ref.shape[1]
    flat, count_m = coarse.shape[1:]
    count_k = kmap.shape[1]
    onehot = kmap[...] == iota((count_m, count_k), 0)
    spread_b = (iota((chans, flat), 0) == iota((chans, flat), 1) % chans).astype(BF16)
    same_b = iota((width, flat), 0) % chans == iota((width, flat), 1) // chans
    pick_m = (iota((width, count_m), 0) // chans == iota((width, count_m), 1)).astype(BF16)
    same_c = iota((flat, width), 0) % chans == iota((flat, width), 1) % chans
    moved = []
    for part in range(2):
        at = 2 * own_rows + part * chans
        wide = mm_exact(ref[at : at + chans, :].T, spread_b)
        wide = jnp.where(same_b, wide, 0.0).reshape(count_m, chans, flat)
        moved.append(jnp.sum(wide, axis=1))
    real, imag = cmul(tuple(moved), (square[0], square[1]))
    correction[0:1, :] = jnp.sum(jnp.where(onehot, real, 0.0), axis=0, keepdims=True)
    correction[1:2, :] = jnp.sum(jnp.where(onehot, imag, 0.0), axis=0, keepdims=True)
    for part in range(2):
        at = 2 * own_rows + (2 + part) * chans
        row = ref[at : at + chans, :]
        tall = jnp.broadcast_to(row[:, None, :], (chans, chans, width)).reshape(flat, width)
        coarse[part] = mm_exact(jnp.where(same_c, tall, 0.0), pick_m)


def own_kernel(own_rows, kept, kmap, square, coarse, correction):
    finish_energy(own_rows, kept, kmap, square, coarse, correction)


def other_kernel(
    own_rows,
    cfg_at, kept, got, kmap, square, coarse_own, correction_own,
    avg, coarse, correction,
    coarse_s, correction_s, sems,
):
    own = cfg_at[0] % 2
    copies = []

    def send_out(source, target):
        copy = pltpu.make_async_copy(source, target, sems.at[len(copies)])
        copy.start()
        copies.append(copy)

    for ref, energy in ((got, 1 - own), (kept, own)):
        for part in range(2):
            rows = pl.ds(part * own_rows, own_rows)
            send_out(ref.at[rows], avg.at[energy, part])
    send_out(coarse_own, coarse.at[own])
    send_out(correction_own, correction.at[own])
    finish_energy(own_rows, got, kmap, square, coarse_s, correction_s)
    send_out(coarse_s, coarse.at[1 - own])
    send_out(correction_s, correction.at[1 - own])
    for copy in copies:
        copy.wait()


def shape_of(*extent):
    return jax.ShapeDtypeStruct(extent, F32)


SMEM_SPEC = pl.BlockSpec(memory_space=pltpu.SMEM)
VMEM_SPEC = pl.BlockSpec(memory_space=pltpu.VMEM)


def call(body, outs, scratch, scalars, args, cost, spec=None, out_spec=VMEM_SPEC):
    return pl.pallas_call(
        body,
        out_shape=outs,
        in_specs=[SMEM_SPEC] * scalars + [spec or VMEM_SPEC] * (len(args) - scalars),
        out_specs=jax.tree.map(lambda _: out_spec, outs),
        scratch_shapes=scratch,
        compiler_params=pltpu.CompilerParams(vmem_limit_bytes=KERNEL_VMEM),
        cost_estimate=pl.CostEstimate(flops=cost, bytes_accessed=cost // 64, transcendentals=0),
    )(*args)


def exchange_stages(ka_size, cfg_size):
    total = ka_size * cfg_size
    bits = []
    step = 2
    while step < total:
        bits.append(step)
        step *= 2
    stages = []
    for at in range(0, len(bits), 2):
        group = bits[at : at + 2]
        stages.append(group if len(group) == 1 else [group[0], group[1], group[0] + group[1]])
    return stages


def swap(value, mask, total):
    return lax.ppermute(value, ("ka", "cfg"), [(i, i ^ mask) for i in range(total)])


def step(medium_t, structure, kmap, occupation, cfg_weight, shift_a, shift_b):
    ka_size, cfg_size = lax.axis_size("ka"), lax.axis_size("cfg")
    total = ka_size * cfg_size
    count_cfg = occupation.shape[0] * total
    sites = occupation.shape[1]
    chans, count_m = medium_t.shape[2], medium_t.shape[4]
    count_k = kmap.shape[0]
    flat = chans * chans
    width = count_m * chans
    per_moment = count_k * total // count_m
    own_sites = sites // cfg_size
    own_rows = own_sites * chans
    chip_rows = 2 * own_rows
    slot_rows = -(-count_cfg * SLOT // width)
    sum_rows = 2 * chans + -(-slot_rows // 8) * 8
    *tables, place_diff = phase_constants(sites, chans)

    cfg_at = lax.axis_index("cfg").astype(jnp.int32).reshape(1)
    kmap_row = kmap.reshape(1, count_k)

    place = lax.axis_index(("ka", "cfg")).astype(jnp.int32).reshape(1)
    inputs = (
        place,
        cfg_weight,
        medium_t.reshape(ENERGIES, 2, flat, count_m),
        structure.reshape(ENERGIES, 2, flat, count_k),
        kmap_row,
        occupation,
    )
    inputs = inputs[:2] + tuple(
        pltpu.with_memory_space_constraint(value, pltpu.HBM) for value in inputs[2:]
    )
    outs = (
        shape_of(sum_rows, width),
        shape_of(2, flat, count_k),
        shape_of(2, flat, count_k),
    )
    own_outs = (
        shape_of(2, flat, count_m),
        shape_of(2, flat, count_k),
        jax.ShapeDtypeStruct((1, count_k), jnp.int32),
    )
    work = [pltpu.VMEM((3, flat, count_k), F32)] * 3
    local = [
        pltpu.VMEM((2, flat, count_m), F32),
        pltpu.VMEM(occupation.shape, jnp.int32),
        pltpu.SemaphoreType.DMA((7,)),
    ]
    send, z_other, y_other, *own = call(
        send_kernel,
        outs + own_outs,
        work + local,
        2,
        inputs,
        1 << 23,
        spec=pl.BlockSpec(memory_space=pltpu.HBM),
    )
    arrived = swap(send, 1, total)
    keep, z_own, y_own, y_row = call(
        keep_kernel, outs + (shape_of(2, chans, width),), work, 0, (send, *own), 1 << 23
    )
    summed = keep + arrived
    y_z = ((y_own, z_own), (y_other, z_other))
    squares = []
    for energy in range(ENERGIES):
        squares.append(
            call(
                square_kernel,
                shape_of(2, flat, count_k),
                [pltpu.VMEM((3, flat, count_k), F32)] * 3,
                0,
                y_z[energy],
                1 << 24,
            )
        )
    for stage in exchange_stages(ka_size, cfg_size):
        arrived = []
        for mask in stage:
            arrived.append(swap(summed, mask, total))
        for value in arrived:
            summed = summed + value
    out_rows = 2 * own_rows + 4 * chans
    kept, sent = call(
        functools.partial(cluster_kernel, per_moment, own_rows, place_diff),
        (shape_of(out_rows, width), shape_of(out_rows, width)),
        [
            pltpu.VMEM((2, 3 * width + 4 * chip_rows, width), F32),
            pltpu.VMEM((width + sites + PAD_ROWS, width), F32),
            pltpu.VMEM((sites // 2, 2, 2, width, width // 2), F32),
            pltpu.VMEM((width, 128), F32),
            pltpu.VMEM((2, 2 * width, width), F32),
            pltpu.VMEM((4, 2, 2, sites // 2, chans, width // 2), F32),
        ],
        1,
        (
            cfg_at,
            summed,
            y_row,
            shift_a,
            shift_b,
            *tables,
        ),
        1 << 26,
    )
    got = swap(sent, 1, total)
    coarse_own, correction_own = call(
        functools.partial(own_kernel, own_rows),
        (shape_of(2, flat, count_m), shape_of(2, count_k)),
        [],
        0,
        (kept, own[2], squares[0]),
        1 << 22,
    )
    avg, coarse, correction = call(
        functools.partial(other_kernel, own_rows),
        (
            shape_of(ENERGIES, 2, own_rows, width),
            shape_of(ENERGIES, 2, flat, count_m),
            shape_of(ENERGIES, 2, count_k),
        ),
        [
            pltpu.VMEM((2, flat, count_m), F32),
            pltpu.VMEM((2, count_k), F32),
            pltpu.SemaphoreType.DMA((8,)),
        ],
        1,
        (cfg_at, kept, got, own[2], squares[1], coarse_own, correction_own),
        1 << 22,
        out_spec=pl.BlockSpec(memory_space=pltpu.HBM),
    )
    return (coarse.reshape(ENERGIES, 2, chans, chans, count_m), avg, correction)


def solution(mesh):
    placed = (
        P(),
        P(None, None, None, None, ("ka", "cfg")),
        P(("ka", "cfg")),
        P(("ka", "cfg"), None),
        P(("ka", "cfg")),
        P(),
        P(),
    )
    return jax.shard_map(
        step,
        mesh=mesh,
        in_specs=placed,
        out_specs=(P(), P(None, None, "cfg", None), P(None, None, ("ka", "cfg"))),
        check_vma=False,
    )
```

```python
import functools
import math

import jax
import jax.numpy as jnp
import numpy as np
from jax import lax
from jax.experimental import pallas as pl
from jax.experimental.pallas import tpu as pltpu
from jax.sharding import PartitionSpec as P

ENERGIES = 2
F32 = jnp.float32
BF16 = jnp.bfloat16
PAD_ROWS = 8
SLOT = 32
KERNEL_VMEM = 20 << 20


def site_geometry(count_sites):
    places = np.arange(count_sites)
    half_n = count_sites // 2
    cell = places % half_n
    site_xyz = np.stack([cell // 4, cell // 2 % 2, cell % 2], axis=1).astype(np.float64)
    site_xyz = site_xyz + 0.5 * (places >= half_n)[:, None]
    mom_hkl = np.stack([places // 4, places // 2 % 2, places % 2], axis=1).astype(np.float64)
    angles = math.pi * (mom_hkl[:, None, :] * site_xyz[None, :, :]).sum(axis=2)
    place_diff = np.zeros((count_sites, count_sites), np.int32)
    for i in range(count_sites):
        for j in range(count_sites):
            gap = (site_xyz[i] - site_xyz[j]) % 2.0
            place_diff[i, j] = int(np.argmin(np.abs(site_xyz % 2.0 - gap).sum(axis=1)))
    return angles, place_diff


def phase_constants(count_sites, chans):
    angles, place_diff = site_geometry(count_sites)
    cells = count_sites // 2
    signs = np.rint(np.cos(angles[:, :cells]))
    turn = angles[:, cells]
    to_cells = np.kron(signs, np.eye(chans)) / count_sites
    turns = np.stack([np.rint(np.cos(turn)), np.rint(np.sin(turn))])
    turns = np.repeat(turns, chans, axis=1)
    return (
        jnp.asarray(to_cells, BF16),
        jnp.asarray(to_cells.T, BF16),
        jnp.asarray(np.concatenate([turns] * (chans // 2)), F32),
        place_diff,
    )


def iota(shape, dim):
    return lax.broadcasted_iota(jnp.int32, shape, dim)


def split(value, pieces):
    out = []
    for step in range(pieces):
        part = value.astype(BF16)
        out.append(part)
        if step + 1 < pieces:
            value = value - part.astype(F32)
    return out


def mm(left, right):
    return jnp.dot(left, right, preferred_element_type=F32)


def mm_nt(left, right):
    return lax.dot_general(left, right, (((1,), (1,)), ((), ())), preferred_element_type=F32)


def mm_exact(left, right_bf16, pieces=3):
    rows = left.shape[0]
    out = mm(jnp.concatenate(split(left, pieces), axis=0), right_bf16)
    total = out[(pieces - 1) * rows :]
    for at in range(pieces - 2, -1, -1):
        total = total + out[at * rows : (at + 1) * rows]
    return total


def mm3(left, right):
    rows = left.shape[0]
    left_hi, left_lo = split(left, 2)
    right_hi, right_lo = split(right, 2)
    out = mm(jnp.concatenate([left_hi, left_lo], axis=0), right_hi)
    return (mm(left_hi, right_lo) + out[rows:]) + out[:rows]


def mm3_deep(left, right):
    left_hi, left_lo = split(left, 2)
    right_hi, right_lo = split(right, 2)
    return mm(
        jnp.concatenate([left_hi, left_lo, left_hi], axis=1),
        jnp.concatenate([right_lo, right_hi, right_hi], axis=0),
    )


def mm_high(left, right):
    return jnp.dot(left, right, preferred_element_type=F32, precision=lax.Precision.HIGHEST)


def cmul(left, right, mul=mm3):
    rows = left[0].shape[0]
    both = jnp.concatenate(left, axis=0)
    by_real = mul(both, right[0])
    by_imag = mul(both, right[1])
    return (by_real[:rows] - by_imag[rows:], by_imag[:rows] + by_real[rows:])


def flip_cells(value, step):
    lanes = value.shape[1]
    ahead = pltpu.roll(value, step, 1)
    if 2 * step == lanes:
        return ahead
    behind = pltpu.roll(value, lanes - step, 1)
    return jnp.where(iota(value.shape, 1) // step % 2 == 1, ahead, behind)


def cell_orders(value, chans):
    count = value.shape[1] // chans
    orders = {0: value}
    at = 0
    for step in range(1, count):
        bit = count // 2
        while step % 2 == 0:
            step //= 2
            bit //= 2
        value = flip_cells(value, bit * chans)
        at ^= bit
        orders[at] = value
    return [orders[n] for n in range(count)]


def sum_cells(values, chans):
    bit = len(values) // 2
    while bit:
        values = [values[n] + flip_cells(values[n + bit], bit * chans) for n in range(bit)]
        bit //= 2
    return values[0]


def turned(value, turns, back=False):
    cos_t, sin_t = turns[0:1], turns[1:2]
    if back:
        sin_t = -sin_t
    return (cos_t * value[0] - sin_t * value[1], cos_t * value[1] + sin_t * value[0])


def cadd(*terms):
    real, imag = terms[0]
    for term in terms[1:]:
        real, imag = real + term[0], imag + term[1]
    return (real, imag)


def cscale(value, factor):
    return (value[0] * factor, value[1] * factor)


def block_diag(row, chans):
    width = row.shape[1]
    tiled = jnp.concatenate([row] * (width // chans), axis=0)
    keep = iota((width, width), 0) // chans == iota((width, width), 1) // chans
    return jnp.where(keep, tiled, 0.0)


def batch_mul(left, right, write, chans):
    group = 8

    def body(step, carry):
        base = step * (group * chans)
        sums = [[None] * 3 for _ in range(group)]
        for b in range(chans):
            rights = [right[part, b * chans : (b + 1) * chans, :] for part in range(3)]
            for g in range(group):
                for part in range(3):
                    lane = left[part, pl.ds(base + (g * chans + b), 1), :]
                    term = lane * rights[part]
                    old = sums[g][part]
                    sums[g][part] = term if old is None else old + term
        for g in range(group):
            both, twice, cross = sums[g]
            write(base + g * chans, both - twice, cross - both - twice)
        return carry

    lax.fori_loop(0, chans // group, body, 0)


def put3(ref, base, count, real, imag):
    rows = pl.ds(pl.multiple_of(base, count), count)
    ref[0, rows, :] = real
    ref[1, rows, :] = imag
    ref[2, rows, :] = real + imag


def kpoint_energy(medium, kmap, packed, z_out, y_out, y_s, g_s, f_s, ready=None):
    flat, count_m = medium[0].shape
    count_k = kmap.shape[1]
    chans = math.isqrt(flat)
    width = packed.shape[1]
    onehot = (kmap == iota((count_m, count_k), 0)).astype(BF16)
    wide = (kmap == iota((width, count_k), 0) // chans).astype(BF16)
    same = iota((flat, width), 0) % chans == iota((flat, width), 1) % chans

    def fold(value):
        return jnp.sum(jnp.where(same, value, 0.0).reshape(chans, chans, width), axis=1)

    for part in range(2):
        value = mm_exact(medium[part], onehot)
        y_s[part] = value
        y_out[part] = value
    y_s[2] = y_s[0] + y_s[1]
    if ready is not None:
        ready()
    g_s[2] = g_s[0] + g_s[1]
    batch_mul(y_s, g_s, lambda base, real, imag: put3(f_s, base, chans, real, imag), chans)

    def write_z(base, real, imag):
        rows = pl.ds(pl.multiple_of(base, chans), chans)
        z_out[0, rows, :] = real + f_s[0, rows, :]
        z_out[1, rows, :] = imag + f_s[1, rows, :]

    batch_mul(f_s, f_s, write_z, chans)
    for part in range(2):
        parts = split(z_out[part], 2)
        total = mm_nt(parts[1], wide) + mm_nt(parts[0], wide)
        packed[part * chans : (part + 1) * chans, :] = fold(total)


def occupation_slots(place, occupation, weight, rows, width):
    count, sites = occupation.shape
    lane = iota((sites, width), 1) % SLOT
    to_slot = (iota((sites, width), 0) == lane).astype(BF16)
    slots = jnp.zeros((rows, width), F32)
    for g in range(count):
        filled = jnp.broadcast_to(occupation[g : g + 1, :].astype(BF16), (sites, sites))
        line = mm(filled, to_slot)[0:1] + jnp.where(lane[0:1] == sites, weight[g], 0.0)
        at = place * count + g
        per_row = width // SLOT
        here = (iota((rows, width), 0) == at // per_row) & (
            iota((rows, width), 1) // SLOT == at % per_row
        )
        slots = slots + jnp.where(here, line, 0.0)
    return slots


def send_kernel(
    place, weight, medium, structure, kmap, occupation,
    packed, z_out, y_out, medium_own, structure_own, kmap_own,
    y_s, g_s, f_s, medium_s, occupation_s, sems,
):
    own = place[0] % 2
    copies = [
        (kmap, kmap_own),
        (medium.at[1 - own], medium_s),
        (structure.at[1 - own, 0], g_s.at[0]),
        (structure.at[1 - own, 1], g_s.at[1]),
        (occupation, occupation_s),
        (medium.at[own], medium_own),
        (structure.at[own], structure_own),
    ]
    copies = [pltpu.make_async_copy(src, dst, sems.at[n]) for n, (src, dst) in enumerate(copies)]
    for copy in copies:
        copy.start()
    half = 2 * math.isqrt(medium_s.shape[1])
    copies[0].wait()
    copies[1].wait()

    def ready():
        for copy in copies[2:5]:
            copy.wait()

    medium_val = (medium_s[0], medium_s[1])
    kpoint_energy(medium_val, kmap_own[...], packed, z_out, y_out, y_s, g_s, f_s, ready)
    packed[half:, :] = occupation_slots(
        place[0], occupation_s[...], weight, packed.shape[0] - half, packed.shape[1]
    )
    for copy in copies[5:]:
        copy.wait()


def keep_kernel(sent, medium, structure, kmap, packed, z_out, y_out, y_s, g_s, f_s):
    for part in range(2):
        g_s[part] = structure[part]
    medium_val = (medium[0], medium[1])
    kpoint_energy(medium_val, kmap[...], packed, z_out, y_out, y_s, g_s, f_s)
    half = 2 * math.isqrt(medium.shape[1])
    packed[half:, :] = sent[half:, :]


def square_kernel(y_in, z_in, out, y_s, z_s, t_s):
    flat = out.shape[1]
    chans = math.isqrt(flat)
    for part in range(2):
        y_s[part] = y_in[part]
        z_s[part] = z_in[part]
    y_s[2] = y_in[0] + y_in[1]
    z_s[2] = z_in[0] + z_in[1]

    def write_t(base, real, imag):
        rows = pl.ds(pl.multiple_of(base, chans), chans)
        put3(t_s, base, chans, real + y_s[0, rows, :], imag + y_s[1, rows, :])

    batch_mul(z_s, y_s, write_t, chans)

    def write_o(base, real, imag):
        rows = pl.ds(pl.multiple_of(base, chans), chans)
        out[0, rows, :] = real
        out[1, rows, :] = imag

    batch_mul(t_s, t_s, write_o, chans)


def square_own_kernel(y_in, z_in, medium, out, y_row, y_s, z_s, t_s):
    square_kernel(y_in, z_in, out, y_s, z_s, t_s)
    flat, count_m = medium.shape[1:]
    chans, width = y_row.shape[1:]
    lanes_of = (iota((count_m, width), 0) == iota((count_m, width), 1) // chans).astype(BF16)
    same = iota((flat, width), 0) % chans == iota((flat, width), 1) % chans
    for part in range(2):
        value = jnp.where(same, mm_exact(medium[part], lanes_of), 0.0)
        y_row[part] = jnp.sum(value.reshape(chans, chans, width), axis=1)


def cluster_kernel(
    per_moment, own_rows, place_diff,
    cfg_at, summed, y_row, shift_a, shift_b, to_cells, from_cells, turn_rows,
    keep, send, site_s, corr_s, p_s, a_s, n_s, c_s,
):
    own = cfg_at[0] % 2
    chans = shift_a.shape[2]
    width = summed.shape[1]
    sites = width // turn_rows.shape[0]
    cells = sites // 2
    half = cells * chans
    turns = turn_rows[0:2, :]
    own_sites = own_rows // chans
    rows_n = 2 * own_rows
    own_start = cfg_at[0] * own_sites
    other_start = (cfg_at[0] + 1 - 2 * own) * own_sites
    cols = (slice(0, chans), slice(chans, 2 * chans))

    y_val = (y_row[0], y_row[1])
    z_val = (summed[cols[0], :], summed[cols[1], :])
    y_diag = tuple(block_diag(v, chans) for v in y_val)
    coarse = cadd(y_val, cscale(cmul(z_val, y_diag), 1.0 / per_moment))

    base_t = (shift_b[own, 0], shift_b[own, 1])
    step_t = (shift_a[own, 0] - base_t[0], shift_a[own, 1] - base_t[1])

    stack = jnp.concatenate(base_t + step_t, axis=0)
    by_real = mm_high(stack, coarse[0])
    by_imag = mm_high(stack, coarse[1])

    def small_part(at):
        here, after = slice(at * chans, (at + 1) * chans), slice((at + 1) * chans, (at + 2) * chans)
        return (by_real[here] - by_imag[after], by_imag[here] + by_real[after])

    def rows_by(rows, diag):
        count = len(rows)
        out = cmul(
            tuple(jnp.concatenate([row[part] for row in rows], axis=0) for part in range(2)), diag
        )
        return [
            tuple(out[part][n * chans : (n + 1) * chans] for part in range(2)) for n in range(count)
        ]

    power, lead_kern = small_part(0), small_part(2)
    power_diag = tuple(block_diag(v, chans) for v in power)
    cell_map = to_cells[...]

    def to_differences(values):
        rows = []
        for step in range(2):
            for value in values:
                for variant in (value, turned(value, turns)):
                    rows += [split(part, 2)[step] for part in variant]
        out = mm(jnp.concatenate(rows, axis=0), cell_map)
        count = len(values) * 4 * chans
        out = out[count:] + out[:count]
        blocks = [out[n * chans : (n + 1) * chans] for n in range(4 * len(values))]
        return [
            [[blocks[4 * n + 2 * side + part] for part in range(2)] for side in range(2)]
            for n in range(len(values))
        ]

    def kern_to_sites(n, sides):
        start = n * width
        for part in range(2):
            lower = cell_orders(sides[0][part], chans)
            upper = cell_orders(sides[1][part], chans)
            for c in range(cells):
                low = slice(start + c * chans, start + (c + 1) * chans)
                high = slice(start + half + c * chans, start + half + (c + 1) * chans)
                site_s[part, low, 0:half] = lower[c]
                site_s[part, high, half:width] = lower[c]
                site_s[part, high, 0:half] = upper[c]
                site_s[part, low, half:width] = upper[c ^ (cells - 1)]

    first, first_kern, power = rows_by([coarse, lead_kern, power], power_diag)
    first, first_kern = cscale(first, -1.0), cscale(first_kern, -1.0)
    power_diag = tuple(block_diag(v, chans) for v in power)
    (lead_sides,) = to_differences([lead_kern])
    kern_to_sites(0, lead_sides)
    second, third, second_kern = rows_by([coarse, first, lead_kern], power_diag)
    series = [coarse, first, second, third]
    kern = [lead_kern, first_kern, second_kern]
    whole = cadd(*series)

    hi_lo = []
    for part in range(2):
        hi, lo = split(site_s[part, 0:width, 0:chans], 2)
        hi_lo += [hi.astype(F32), hi.astype(F32), lo.astype(F32)]
    for n, piece in enumerate(hi_lo):
        a_s[:, n * chans : (n + 1) * chans] = piece
    a_val = a_s[:, 0 : 6 * chans].astype(BF16)
    far = cells // 2
    for c in range(far):
        rows = slice(c * chans, (c + 1) * chans)
        high = slice(half + c * chans, half + (c + 1) * chans)
        pieces = []
        for part in range(2):
            line = jnp.concatenate([site_s[part, rows, 0:half], site_s[part, high, 0:half]], axis=1)
            pieces += split(line, 2)
        real_hi, real_lo, imag_hi, imag_lo = pieces
        for part, right in enumerate(
            (
                [real_hi, real_lo, real_hi, -imag_hi, -imag_lo, -imag_hi],
                [imag_hi, imag_lo, imag_hi, real_hi, real_lo, real_hi],
            )
        ):
            out = mm(a_val, jnp.concatenate(right, axis=0))
            for side in range(2):
                value = out[:, side * half : (side + 1) * half]
                p_s[c, side, part] = value
                p_s[c + far, side, part] = flip_cells(value, half // 2)

    others = [whole] + series[:3]
    sides_of = to_differences(kern[1:] + others)
    kern_to_sites(1, sides_of[0])
    base = 3 * width
    slots = summed[2 * chans :, :]
    groups = width // SLOT
    slot_of = iota(slots.shape, 1) // SLOT
    unpacked = jnp.concatenate([jnp.where(slot_of == n, slots, 0.0) for n in range(groups)], axis=0)
    place_in = iota((width, width), 0) % SLOT
    col = iota((width, width), 1)
    row_l = mm(unpacked.astype(BF16), (place_in == col // sites).astype(BF16))
    row_j = mm(unpacked.astype(BF16), (place_in == col % sites).astype(BF16))
    sites_in = (iota((sites, width), 1) % SLOT == iota((sites, width), 0)).astype(BF16)
    filled_t = mm_nt(sites_in, unpacked.astype(BF16)).astype(BF16)
    weights = jnp.sum(
        jnp.where(iota(unpacked.shape, 1) % SLOT == sites, unpacked, 0.0), axis=1, keepdims=True
    )
    norm = 1.0 / jnp.sum(weights, axis=0, keepdims=True)
    pieces = split(weights * (row_l * row_j), 3)
    triple = mm(filled_t, pieces[2]) + mm(filled_t, pieces[1]) + mm(filled_t, pieces[0])
    triple = triple * norm
    lane_l = iota((sites, width), 1) // sites
    lane_j = iota((sites, width), 1) % sites
    row_i = iota((sites, width), 0)
    pair = jnp.where(lane_l == row_i, triple, 0.0)
    single = jnp.sum(jnp.where(lane_j == row_i, pair, 0.0), axis=0, keepdims=True)
    stack = jnp.concatenate(
        [block_diag(triple, sites), pair, jnp.broadcast_to(single, (PAD_ROWS, width))], axis=0
    )
    spread_j = (
        iota((width, width), 0) % sites == iota((width, width), 1) // chans
    ).astype(BF16)
    corr_s[...] = mm_exact(stack, spread_j, pieces=2)

    occupied = corr_s[width + sites : width + sites + 1, :]

    pending = [(n, side, part) for n in range(4) for side in range(2) for part in range(2)]
    for i in range(sites):
        rows = slice(i * chans, (i + 1) * chans)
        after = slice(width + i * chans, width + (i + 1) * chans)
        pair_row = corr_s[width + i : width + i + 1, :]
        on_diag = iota((chans, width), 0) + i * chans == iota((chans, width), 1)
        halves = []
        for side in range(2):
            lanes = slice(side * half, (side + 1) * half)
            totals = [None, None]
            for at in range(sites):
                gap = int(place_diff[i, at])
                above, cell = divmod(at, cells)
                if side == 1 and above == 0:
                    cell = cell ^ (cells - 1)
                scale = corr_s[at * sites + i : at * sites + i + 1, lanes]
                scale = jnp.broadcast_to(scale, (chans, half))
                for part in range(2):
                    term = scale * p_s[cell, side ^ above, part, gap * chans : (gap + 1) * chans, :]
                    totals[part] = term if totals[part] is None else totals[part] + term
            halves.append(totals)
        for part in range(2):
            total = jnp.concatenate([halves[0][part], halves[1][part]], axis=1)
            lead = pair_row * site_s[part, rows, :]
            if part == 0:
                lead = lead - jnp.where(on_diag, occupied, 0.0)
            n_s[part, after, :] = lead
            n_s[part, rows, :] = lead + pair_row * site_s[part, after, :] - total
        if i == sites // 2:
            kern_to_sites(2, sides_of[1])
        for n, side, part in pending[i * len(pending) // sites : (i + 1) * len(pending) // sites]:
            for c, value in enumerate(cell_orders(sides_of[2 + n][side][part], chans)):
                c_s[n, side, part, c] = value
    for group, first_site in enumerate((own_start, other_start)):
        for i in range(own_sites):
            cell = (first_site + i) % cells
            above = (first_site + i) // cells
            turned_cell = above * cell + (1 - above) * (cells - 1 - cell)
            for n in range(4):
                start = base + n * rows_n + (group * own_sites + i) * chans
                for part in range(2):
                    site_s[part, start : start + chans, 0:half] = c_s[n, above, part, cell]
                    site_s[part, start : start + chans, half:width] = c_s[
                        n, 1 - above, part, turned_cell
                    ]

    mid = [(n_s[0, n * width : (n + 1) * width, :], n_s[1, n * width : (n + 1) * width, :]) for n in range(2)]

    def site_rows(n):
        start = base + n * rows_n
        return (site_s[0, start : start + rows_n, :], site_s[1, start : start + rows_n, :])

    def side_by_side(*values):
        return tuple(jnp.concatenate([v[part] for v in values], axis=1) for part in range(2))

    lead_rows = [site_rows(n) for n in range(4)]
    minus = -occupied
    q_zero = cadd(
        cmul(side_by_side(lead_rows[1], lead_rows[2]), (n_s[0], n_s[1]), mm3_deep),
        cscale(lead_rows[3], minus),
    )
    q_one = cadd(cmul(lead_rows[1], mid[1], mm3_deep), cscale(lead_rows[2], minus))
    stack = []
    for value in mid:
        for part in range(2):
            low = [value[part][c * chans : (c + 1) * chans] for c in range(cells)]
            high = [value[part][half + c * chans : half + (c + 1) * chans] for c in range(cells)]
            stack.append(
                sum_cells([low[c][:, :half] + high[c][:, half:] for c in range(cells)], chans)
            )
            crossed = sum_cells([low[c][:, half:] for c in range(cells)], chans)
            for bit in (1, 2, 4):
                crossed = flip_cells(crossed, bit * chans)
            stack.append(sum_cells([high[c][:, :half] for c in range(cells)], chans) + crossed)
    moved = mm_exact(jnp.concatenate(stack, axis=0), from_cells[...], pieces=2)
    moved = [moved[n * chans : (n + 1) * chans] for n in range(8)]
    means = [
        cadd(
            (moved[4 * n], moved[4 * n + 2]),
            turned((moved[4 * n + 1], moved[4 * n + 3]), turns, back=True),
        )
        for n in range(2)
    ]
    kern_diag = [tuple(block_diag(v, chans) for v in pair_val) for pair_val in kern[:2]]
    filled = -jnp.mean(occupied, axis=1, keepdims=True)
    mean_zero, mean_one, last = rows_by([means[0], means[1], series[2]], kern_diag[0])
    (mean_next,) = rows_by([means[1]], kern_diag[1])
    v_zero = cadd(mean_zero, mean_next, cscale(kern[2], filled))
    v_one = cadd(mean_one, cscale(kern[1], filled))
    change = cadd(
        series[1],
        series[2],
        series[3],
        cmul(series[0], tuple(block_diag(v, chans) for v in v_zero)),
        cmul(series[1], tuple(block_diag(v, chans) for v in v_one)),
        cscale(last, filled),
    )
    q_two = cscale(lead_rows[1], minus)
    kernels = (site_s[0, 0 : 3 * width, :], site_s[1, 0 : 3 * width, :])
    q_all = side_by_side(q_zero, q_one, q_two)
    parts = []
    for group in range(2):
        rows = slice(group * own_rows, (group + 1) * own_rows)
        parts.append(cmul(tuple(v[rows] for v in q_all), kernels, mm3_deep))
    result = cadd(
        lead_rows[0],
        tuple(jnp.concatenate([p[part] for p in parts], axis=0) for part in range(2)),
    )

    for ref, start in ((keep, 0), (send, own_rows)):
        for part in range(2):
            ref[part * own_rows : (part + 1) * own_rows, :] = result[part][start : start + own_rows]
            for n, value in enumerate((change, coarse)):
                at = 2 * own_rows + (2 * n + part) * chans
                ref[at : at + chans, :] = value[part]


def finish_energy(own_rows, ref, kmap, square, coarse, correction):
    chans = (ref.shape[0] - 2 * own_rows) // 4
    width = ref.shape[1]
    flat, count_m = coarse.shape[1:]
    count_k = kmap.shape[1]
    onehot = kmap[...] == iota((count_m, count_k), 0)
    spread_b = (iota((chans, flat), 0) == iota((chans, flat), 1) % chans).astype(BF16)
    same_b = iota((width, flat), 0) % chans == iota((width, flat), 1) // chans
    pick_m = (iota((width, count_m), 0) // chans == iota((width, count_m), 1)).astype(BF16)
    same_c = iota((flat, width), 0) % chans == iota((flat, width), 1) % chans
    moved = []
    for part in range(2):
        at = 2 * own_rows + part * chans
        wide = mm_exact(ref[at : at + chans, :].T, spread_b, pieces=2)
        wide = jnp.where(same_b, wide, 0.0).reshape(count_m, chans, flat)
        moved.append(jnp.sum(wide, axis=1))
    real, imag = cmul(tuple(moved), (square[0], square[1]))
    correction[0:1, :] = jnp.sum(jnp.where(onehot, real, 0.0), axis=0, keepdims=True)
    correction[1:2, :] = jnp.sum(jnp.where(onehot, imag, 0.0), axis=0, keepdims=True)
    for part in range(2):
        at = 2 * own_rows + (2 + part) * chans
        row = ref[at : at + chans, :]
        tall = jnp.broadcast_to(row[:, None, :], (chans, chans, width)).reshape(flat, width)
        coarse[part] = mm_exact(jnp.where(same_c, tall, 0.0), pick_m, pieces=2)


def own_kernel(own_rows, kept, kmap, square, coarse, correction):
    finish_energy(own_rows, kept, kmap, square, coarse, correction)


def other_kernel(
    own_rows,
    cfg_at, kept, got, kmap, square, coarse_own, correction_own,
    avg, coarse, correction,
    coarse_s, correction_s, sems,
):
    own = cfg_at[0] % 2
    copies = []

    def send_out(source, target):
        copy = pltpu.make_async_copy(source, target, sems.at[len(copies)])
        copy.start()
        copies.append(copy)

    for ref, energy in ((got, 1 - own), (kept, own)):
        for part in range(2):
            rows = pl.ds(part * own_rows, own_rows)
            send_out(ref.at[rows], avg.at[energy, part])
    send_out(coarse_own, coarse.at[own])
    send_out(correction_own, correction.at[own])
    finish_energy(own_rows, got, kmap, square, coarse_s, correction_s)
    send_out(coarse_s, coarse.at[1 - own])
    send_out(correction_s, correction.at[1 - own])
    for copy in copies:
        copy.wait()


def shape_of(*extent):
    return jax.ShapeDtypeStruct(extent, F32)


SMEM_SPEC = pl.BlockSpec(memory_space=pltpu.SMEM)
VMEM_SPEC = pl.BlockSpec(memory_space=pltpu.VMEM)


def call(body, outs, scratch, scalars, args, cost, spec=None, out_spec=VMEM_SPEC):
    return pl.pallas_call(
        body,
        out_shape=outs,
        in_specs=[SMEM_SPEC] * scalars + [spec or VMEM_SPEC] * (len(args) - scalars),
        out_specs=jax.tree.map(lambda _: out_spec, outs),
        scratch_shapes=scratch,
        compiler_params=pltpu.CompilerParams(vmem_limit_bytes=KERNEL_VMEM),
        cost_estimate=pl.CostEstimate(flops=cost, bytes_accessed=cost // 64, transcendentals=0),
    )(*args)


def exchange_stages(ka_size, cfg_size):
    total = ka_size * cfg_size
    bits = []
    step = 2
    while step < total:
        bits.append(step)
        step *= 2
    stages = []
    for at in range(0, len(bits), 2):
        group = bits[at : at + 2]
        stages.append(group if len(group) == 1 else [group[0], group[1], group[0] + group[1]])
    return stages


def swap(value, mask, total):
    return lax.ppermute(value, ("ka", "cfg"), [(i, i ^ mask) for i in range(total)])


def step(medium_t, structure, kmap, occupation, cfg_weight, shift_a, shift_b):
    ka_size, cfg_size = lax.axis_size("ka"), lax.axis_size("cfg")
    total = ka_size * cfg_size
    count_cfg = occupation.shape[0] * total
    sites = occupation.shape[1]
    chans, count_m = medium_t.shape[2], medium_t.shape[4]
    count_k = kmap.shape[0]
    flat = chans * chans
    width = count_m * chans
    per_moment = count_k * total // count_m
    own_sites = sites // cfg_size
    own_rows = own_sites * chans
    chip_rows = 2 * own_rows
    slot_rows = -(-count_cfg * SLOT // width)
    sum_rows = 2 * chans + -(-slot_rows // 8) * 8
    *tables, place_diff = phase_constants(sites, chans)

    cfg_at = lax.axis_index("cfg").astype(jnp.int32).reshape(1)
    kmap_row = kmap.reshape(1, count_k)

    place = lax.axis_index(("ka", "cfg")).astype(jnp.int32).reshape(1)
    inputs = (
        place,
        cfg_weight,
        medium_t.reshape(ENERGIES, 2, flat, count_m),
        structure.reshape(ENERGIES, 2, flat, count_k),
        kmap_row,
        occupation,
    )
    inputs = inputs[:2] + tuple(
        pltpu.with_memory_space_constraint(value, pltpu.HBM) for value in inputs[2:]
    )
    outs = (
        shape_of(sum_rows, width),
        shape_of(2, flat, count_k),
        shape_of(2, flat, count_k),
    )
    own_outs = (
        shape_of(2, flat, count_m),
        shape_of(2, flat, count_k),
        jax.ShapeDtypeStruct((1, count_k), jnp.int32),
    )
    work = [pltpu.VMEM((3, flat, count_k), F32)] * 3
    local = [
        pltpu.VMEM((2, flat, count_m), F32),
        pltpu.VMEM(occupation.shape, jnp.int32),
        pltpu.SemaphoreType.DMA((7,)),
    ]
    send, z_other, y_other, *own = call(
        send_kernel,
        outs + own_outs,
        work + local,
        2,
        inputs,
        1 << 23,
        spec=pl.BlockSpec(memory_space=pltpu.HBM),
    )
    arrived = swap(send, 1, total)
    keep, z_own, y_own = call(keep_kernel, outs, work, 0, (send, *own), 1 << 23)
    summed = keep + arrived
    y_z = ((y_own, z_own), (y_other, z_other))
    squares = []
    for energy in range(ENERGIES):
        if energy == 0:
            square, y_row = call(
                square_own_kernel,
                (shape_of(2, flat, count_k), shape_of(2, chans, width)),
                work,
                0,
                (*y_z[energy], own[0]),
                1 << 24,
            )
        else:
            square = call(square_kernel, shape_of(2, flat, count_k), work, 0, y_z[energy], 1 << 24)
        squares.append(square)
    for stage in exchange_stages(ka_size, cfg_size):
        arrived = []
        for mask in stage:
            arrived.append(swap(summed, mask, total))
        for value in arrived:
            summed = summed + value
    out_rows = 2 * own_rows + 4 * chans
    kept, sent = call(
        functools.partial(cluster_kernel, per_moment, own_rows, place_diff),
        (shape_of(out_rows, width), shape_of(out_rows, width)),
        [
            pltpu.VMEM((2, 3 * width + 4 * chip_rows, width), F32),
            pltpu.VMEM((width + sites + PAD_ROWS, width), F32),
            pltpu.VMEM((sites // 2, 2, 2, width, width // 2), F32),
            pltpu.VMEM((width, 128), F32),
            pltpu.VMEM((2, 2 * width, width), F32),
            pltpu.VMEM((4, 2, 2, sites // 2, chans, width // 2), F32),
        ],
        1,
        (
            cfg_at,
            summed,
            y_row,
            shift_a,
            shift_b,
            *tables,
        ),
        1 << 26,
    )
    got = swap(sent, 1, total)
    coarse_own, correction_own = call(
        functools.partial(own_kernel, own_rows),
        (shape_of(2, flat, count_m), shape_of(2, count_k)),
        [],
        0,
        (kept, own[2], squares[0]),
        1 << 22,
    )
    avg, coarse, correction = call(
        functools.partial(other_kernel, own_rows),
        (
            shape_of(ENERGIES, 2, own_rows, width),
            shape_of(ENERGIES, 2, flat, count_m),
            shape_of(ENERGIES, 2, count_k),
        ),
        [
            pltpu.VMEM((2, flat, count_m), F32),
            pltpu.VMEM((2, count_k), F32),
            pltpu.SemaphoreType.DMA((8,)),
        ],
        1,
        (cfg_at, kept, got, own[2], squares[1], coarse_own, correction_own),
        1 << 22,
        out_spec=pl.BlockSpec(memory_space=pltpu.HBM),
    )
    return (coarse.reshape(ENERGIES, 2, chans, chans, count_m), avg, correction)


def solution(mesh):
    placed = (
        P(),
        P(None, None, None, None, ("ka", "cfg")),
        P(("ka", "cfg")),
        P(("ka", "cfg"), None),
        P(("ka", "cfg")),
        P(),
        P(),
    )
    return jax.shard_map(
        step,
        mesh=mesh,
        in_specs=placed,
        out_specs=(P(), P(None, None, "cfg", None), P(None, None, ("ka", "cfg"))),
        check_vma=False,
    )
```

```python
import functools
import math

import jax
import jax.numpy as jnp
import numpy as np
from jax import lax
from jax.experimental import pallas as pl
from jax.experimental.pallas import tpu as pltpu
from jax.sharding import PartitionSpec as P

ENERGIES = 2
F32 = jnp.float32
BF16 = jnp.bfloat16
PAD_ROWS = 8
SLOT = 32
KERNEL_VMEM = 20 << 20


def site_geometry(count_sites):
    places = np.arange(count_sites)
    half_n = count_sites // 2
    cell = places % half_n
    site_xyz = np.stack([cell // 4, cell // 2 % 2, cell % 2], axis=1).astype(np.float64)
    site_xyz = site_xyz + 0.5 * (places >= half_n)[:, None]
    mom_hkl = np.stack([places // 4, places // 2 % 2, places % 2], axis=1).astype(np.float64)
    angles = math.pi * (mom_hkl[:, None, :] * site_xyz[None, :, :]).sum(axis=2)
    place_diff = np.zeros((count_sites, count_sites), np.int32)
    for i in range(count_sites):
        for j in range(count_sites):
            gap = (site_xyz[i] - site_xyz[j]) % 2.0
            place_diff[i, j] = int(np.argmin(np.abs(site_xyz % 2.0 - gap).sum(axis=1)))
    return angles, place_diff


def phase_constants(count_sites, chans):
    angles, place_diff = site_geometry(count_sites)
    cells = count_sites // 2
    signs = np.rint(np.cos(angles[:, :cells]))
    turn = angles[:, cells]
    to_cells = np.kron(signs, np.eye(chans)) / count_sites
    turns = np.stack([np.rint(np.cos(turn)), np.rint(np.sin(turn))])
    turns = np.repeat(turns, chans, axis=1)
    return (
        jnp.asarray(to_cells, BF16),
        jnp.asarray(to_cells.T, BF16),
        jnp.asarray(np.concatenate([turns] * (chans // 2)), F32),
        place_diff,
    )


def iota(shape, dim):
    return lax.broadcasted_iota(jnp.int32, shape, dim)


def split(value, pieces):
    out = []
    for step in range(pieces):
        part = value.astype(BF16)
        out.append(part)
        if step + 1 < pieces:
            value = value - part.astype(F32)
    return out


def mm(left, right):
    return jnp.dot(left, right, preferred_element_type=F32)


def mm_nt(left, right):
    return lax.dot_general(left, right, (((1,), (1,)), ((), ())), preferred_element_type=F32)


def mm_exact(left, right_bf16, pieces=3):
    rows = left.shape[0]
    out = mm(jnp.concatenate(split(left, pieces), axis=0), right_bf16)
    total = out[(pieces - 1) * rows :]
    for at in range(pieces - 2, -1, -1):
        total = total + out[at * rows : (at + 1) * rows]
    return total


def mm3(left, right):
    rows = left.shape[0]
    left_hi, left_lo = split(left, 2)
    right_hi, right_lo = split(right, 2)
    out = mm(jnp.concatenate([left_hi, left_lo], axis=0), right_hi)
    return (mm(left_hi, right_lo) + out[rows:]) + out[:rows]


def mm3_deep(left, right):
    left_hi, left_lo = split(left, 2)
    right_hi, right_lo = split(right, 2)
    return mm(
        jnp.concatenate([left_hi, left_lo, left_hi], axis=1),
        jnp.concatenate([right_lo, right_hi, right_hi], axis=0),
    )


def mm_high(left, right):
    return jnp.dot(left, right, preferred_element_type=F32, precision=lax.Precision.HIGHEST)


def cmul(left, right, mul=mm3):
    rows = left[0].shape[0]
    both = jnp.concatenate(left, axis=0)
    by_real = mul(both, right[0])
    by_imag = mul(both, right[1])
    return (by_real[:rows] - by_imag[rows:], by_imag[:rows] + by_real[rows:])


def flip_cells(value, step):
    lanes = value.shape[1]
    ahead = pltpu.roll(value, step, 1)
    if 2 * step == lanes:
        return ahead
    behind = pltpu.roll(value, lanes - step, 1)
    return jnp.where(iota(value.shape, 1) // step % 2 == 1, ahead, behind)


def cell_orders(value, chans):
    count = value.shape[1] // chans
    orders = {0: value}
    at = 0
    for step in range(1, count):
        bit = count // 2
        while step % 2 == 0:
            step //= 2
            bit //= 2
        value = flip_cells(value, bit * chans)
        at ^= bit
        orders[at] = value
    return [orders[n] for n in range(count)]


def sum_cells(values, chans):
    bit = len(values) // 2
    while bit:
        values = [values[n] + flip_cells(values[n + bit], bit * chans) for n in range(bit)]
        bit //= 2
    return values[0]


def by_momentum(row, chans, inner_first):
    width = row.shape[1]
    flat = chans * chans
    outer, inner = iota((chans, flat), 1) // chans, iota((chans, flat), 1) % chans
    at = inner if inner_first else outer
    wide = mm_exact(row.T, (iota((chans, flat), 0) == at).astype(BF16), pieces=2)
    lane = iota((width, flat), 1)
    lane = lane // chans if inner_first else lane % chans
    wide = jnp.where(iota((width, flat), 0) % chans == lane, wide, 0.0)
    return jnp.sum(wide.reshape(width // chans, chans, flat), axis=1)


def turned(value, turns, back=False):
    cos_t, sin_t = turns[0:1], turns[1:2]
    if back:
        sin_t = -sin_t
    return (cos_t * value[0] - sin_t * value[1], cos_t * value[1] + sin_t * value[0])


def cadd(*terms):
    real, imag = terms[0]
    for term in terms[1:]:
        real, imag = real + term[0], imag + term[1]
    return (real, imag)


def cscale(value, factor):
    return (value[0] * factor, value[1] * factor)


def block_diag(row, chans):
    width = row.shape[1]
    tiled = jnp.concatenate([row] * (width // chans), axis=0)
    keep = iota((width, width), 0) // chans == iota((width, width), 1) // chans
    return jnp.where(keep, tiled, 0.0)


def batch_mul(left, right, write, chans):
    group = 8

    def body(step, carry):
        base = step * (group * chans)
        sums = [[None] * 3 for _ in range(group)]
        for b in range(chans):
            rights = [right[part, b * chans : (b + 1) * chans, :] for part in range(3)]
            for g in range(group):
                for part in range(3):
                    lane = left[part, pl.ds(base + (g * chans + b), 1), :]
                    term = lane * rights[part]
                    old = sums[g][part]
                    sums[g][part] = term if old is None else old + term
        for g in range(group):
            both, twice, cross = sums[g]
            write(base + g * chans, both - twice, cross - both - twice)
        return carry

    lax.fori_loop(0, chans // group, body, 0)


def put3(ref, base, count, real, imag):
    rows = pl.ds(pl.multiple_of(base, count), count)
    ref[0, rows, :] = real
    ref[1, rows, :] = imag
    ref[2, rows, :] = real + imag


def kpoint_energy(medium, kmap, packed, z_out, y_out, y_s, g_s, f_s, ready=None):
    flat, count_m = medium[0].shape
    count_k = kmap.shape[1]
    chans = math.isqrt(flat)
    width = 2 * packed.shape[1]
    onehot = (kmap == iota((count_m, count_k), 0)).astype(BF16)
    wide = (kmap == iota((width, count_k), 0) // chans).astype(BF16)
    same = iota((flat, width), 0) % chans == iota((flat, width), 1) % chans

    def fold(value):
        return jnp.sum(jnp.where(same, value, 0.0).reshape(chans, chans, width), axis=1)

    for part in range(2):
        value = mm_exact(medium[part], onehot)
        y_s[part] = value
        y_out[part] = value
    y_s[2] = y_s[0] + y_s[1]
    if ready is not None:
        ready()
    g_s[2] = g_s[0] + g_s[1]
    batch_mul(y_s, g_s, lambda base, real, imag: put3(f_s, base, chans, real, imag), chans)

    def write_z(base, real, imag):
        rows = pl.ds(pl.multiple_of(base, chans), chans)
        z_out[0, rows, :] = real + f_s[0, rows, :]
        z_out[1, rows, :] = imag + f_s[1, rows, :]

    batch_mul(f_s, f_s, write_z, chans)
    for part in range(2):
        parts = split(z_out[part], 2)
        total = mm_nt(parts[1], wide) + mm_nt(parts[0], wide)
        folded = fold(total)
        for side in range(2):
            at = (2 * side + part) * chans
            packed[at : at + chans, :] = folded[:, side * width // 2 : (side + 1) * width // 2]


def occupation_slots(place, occupation, weight, rows, width):
    count, sites = occupation.shape
    lane = iota((sites, width), 1) % SLOT
    to_slot = (iota((sites, width), 0) == lane).astype(BF16)
    slots = jnp.zeros((rows, width), F32)
    for g in range(count):
        filled = jnp.broadcast_to(occupation[g : g + 1, :].astype(BF16), (sites, sites))
        line = mm(filled, to_slot)[0:1] + jnp.where(lane[0:1] == sites, weight[g], 0.0)
        at = place * count + g
        per_row = width // SLOT
        here = (iota((rows, width), 0) == at // per_row) & (
            iota((rows, width), 1) // SLOT == at % per_row
        )
        slots = slots + jnp.where(here, line, 0.0)
    return slots


def send_kernel(
    place, weight, medium, structure, kmap, occupation,
    packed, z_out, y_out, medium_own, structure_own, kmap_own,
    y_s, g_s, f_s, medium_s, occupation_s, sems,
):
    own = place[0] % 2
    copies = [
        (kmap, kmap_own),
        (medium.at[1 - own], medium_s),
        (structure.at[1 - own, 0], g_s.at[0]),
        (structure.at[1 - own, 1], g_s.at[1]),
        (occupation, occupation_s),
        (medium.at[own], medium_own),
        (structure.at[own], structure_own),
    ]
    copies = [pltpu.make_async_copy(src, dst, sems.at[n]) for n, (src, dst) in enumerate(copies)]
    for copy in copies:
        copy.start()
    half = 4 * math.isqrt(medium_s.shape[1])
    copies[0].wait()
    copies[1].wait()

    def ready():
        for copy in copies[2:5]:
            copy.wait()

    medium_val = (medium_s[0], medium_s[1])
    kpoint_energy(medium_val, kmap_own[...], packed, z_out, y_out, y_s, g_s, f_s, ready)
    packed[half:, :] = occupation_slots(
        place[0], occupation_s[...], weight, packed.shape[0] - half, packed.shape[1]
    )
    for copy in copies[5:]:
        copy.wait()


def keep_kernel(sent, medium, structure, kmap, packed, z_out, y_out, y_s, g_s, f_s):
    for part in range(2):
        g_s[part] = structure[part]
    medium_val = (medium[0], medium[1])
    kpoint_energy(medium_val, kmap[...], packed, z_out, y_out, y_s, g_s, f_s)
    half = 4 * math.isqrt(medium.shape[1])
    packed[half:, :] = sent[half:, :]


def square_kernel(y_in, z_in, out, y_s, z_s, t_s):
    flat = out.shape[1]
    chans = math.isqrt(flat)
    for part in range(2):
        y_s[part] = y_in[part]
        z_s[part] = z_in[part]
    y_s[2] = y_in[0] + y_in[1]
    z_s[2] = z_in[0] + z_in[1]

    def write_t(base, real, imag):
        rows = pl.ds(pl.multiple_of(base, chans), chans)
        put3(t_s, base, chans, real + y_s[0, rows, :], imag + y_s[1, rows, :])

    batch_mul(z_s, y_s, write_t, chans)

    def write_o(base, real, imag):
        rows = pl.ds(pl.multiple_of(base, chans), chans)
        out[0, rows, :] = real
        out[1, rows, :] = imag

    batch_mul(t_s, t_s, write_o, chans)


def square_own_kernel(y_in, z_in, medium, out, y_row, y_s, z_s, t_s):
    square_kernel(y_in, z_in, out, y_s, z_s, t_s)
    flat, count_m = medium.shape[1:]
    chans, width = y_row.shape[1:]
    lanes_of = (iota((count_m, width), 0) == iota((count_m, width), 1) // chans).astype(BF16)
    same = iota((flat, width), 0) % chans == iota((flat, width), 1) % chans
    for part in range(2):
        value = jnp.where(same, mm_exact(medium[part], lanes_of), 0.0)
        y_row[part] = jnp.sum(value.reshape(chans, chans, width), axis=1)


def cluster_kernel(
    per_moment, own_rows, place_diff,
    cfg_at, summed, y_row, shift_a, shift_b, to_cells, from_cells, turn_rows,
    keep, send, site_s, corr_s, p_s, a_s, n_s, c_s,
):
    own = cfg_at[0] % 2
    chans = shift_a.shape[2]
    width = 2 * summed.shape[1]
    sites = width // turn_rows.shape[0]
    cells = sites // 2
    half = cells * chans
    turns = turn_rows[0:2, :]
    own_sites = own_rows // chans
    rows_n = 2 * own_rows
    own_start = cfg_at[0] * own_sites
    other_start = (cfg_at[0] + 1 - 2 * own) * own_sites

    y_val = (y_row[0], y_row[1])
    z_val = tuple(
        jnp.concatenate(
            [summed[(2 * side + part) * chans : (2 * side + part + 1) * chans, :] for side in range(2)],
            axis=1,
        )
        for part in range(2)
    )
    y_diag = tuple(block_diag(v, chans) for v in y_val)
    coarse = cadd(y_val, cscale(cmul(z_val, y_diag), 1.0 / per_moment))

    coarse_rows = tuple(by_momentum(value, chans, False) for value in coarse)
    count_m = width // chans
    base_t = (shift_b[own, 0], shift_b[own, 1])
    step_t = (shift_a[own, 0] - base_t[0], shift_a[own, 1] - base_t[1])

    stack = jnp.concatenate(base_t + step_t, axis=0)
    by_real = mm_high(stack, coarse[0])
    by_imag = mm_high(stack, coarse[1])

    def small_part(at):
        here, after = slice(at * chans, (at + 1) * chans), slice((at + 1) * chans, (at + 2) * chans)
        return (by_real[here] - by_imag[after], by_imag[here] + by_real[after])

    def rows_by(rows, diag):
        count = len(rows)
        out = cmul(
            tuple(jnp.concatenate([row[part] for row in rows], axis=0) for part in range(2)), diag
        )
        return [
            tuple(out[part][n * chans : (n + 1) * chans] for part in range(2)) for n in range(count)
        ]

    power, lead_kern = small_part(0), small_part(2)
    power_diag = tuple(block_diag(v, chans) for v in power)
    cell_map = to_cells[...]

    def to_differences(values):
        rows = []
        for step in range(2):
            for value in values:
                for variant in (value, turned(value, turns)):
                    rows += [split(part, 2)[step] for part in variant]
        out = mm(jnp.concatenate(rows, axis=0), cell_map)
        count = len(values) * 4 * chans
        out = out[count:] + out[:count]
        blocks = [out[n * chans : (n + 1) * chans] for n in range(4 * len(values))]
        return [
            [[blocks[4 * n + 2 * side + part] for part in range(2)] for side in range(2)]
            for n in range(len(values))
        ]

    def kern_to_sites(n, sides):
        start = n * width
        for part in range(2):
            lower = cell_orders(sides[0][part], chans)
            upper = cell_orders(sides[1][part], chans)
            for c in range(cells):
                low = slice(start + c * chans, start + (c + 1) * chans)
                high = slice(start + half + c * chans, start + half + (c + 1) * chans)
                site_s[part, low, 0:half] = lower[c]
                site_s[part, high, half:width] = lower[c]
                site_s[part, high, 0:half] = upper[c]
                site_s[part, low, half:width] = upper[c ^ (cells - 1)]

    first, first_kern, power = rows_by([coarse, lead_kern, power], power_diag)
    first, first_kern = cscale(first, -1.0), cscale(first_kern, -1.0)
    power_diag = tuple(block_diag(v, chans) for v in power)
    (lead_sides,) = to_differences([lead_kern])
    kern_to_sites(0, lead_sides)
    second, third, second_kern = rows_by([coarse, first, lead_kern], power_diag)
    series = [coarse, first, second, third]
    kern = [lead_kern, first_kern, second_kern]
    whole = cadd(*series)

    hi_lo = []
    for part in range(2):
        hi, lo = split(site_s[part, 0:width, 0:chans], 2)
        hi_lo += [hi.astype(F32), hi.astype(F32), lo.astype(F32)]
    for n, piece in enumerate(hi_lo):
        a_s[:, n * chans : (n + 1) * chans] = piece
    a_val = a_s[:, 0 : 6 * chans].astype(BF16)
    far = cells // 2
    for c in range(far):
        rows = slice(c * chans, (c + 1) * chans)
        high = slice(half + c * chans, half + (c + 1) * chans)
        pieces = []
        for part in range(2):
            line = jnp.concatenate([site_s[part, rows, 0:half], site_s[part, high, 0:half]], axis=1)
            pieces += split(line, 2)
        real_hi, real_lo, imag_hi, imag_lo = pieces
        for part, right in enumerate(
            (
                [real_hi, real_lo, real_hi, -imag_hi, -imag_lo, -imag_hi],
                [imag_hi, imag_lo, imag_hi, real_hi, real_lo, real_hi],
            )
        ):
            out = mm(a_val, jnp.concatenate(right, axis=0))
            for side in range(2):
                value = out[:, side * half : (side + 1) * half]
                p_s[c, side, part] = value
                p_s[c + far, side, part] = flip_cells(value, half // 2)

    others = [whole] + series[:3]
    sides_of = to_differences(kern[1:] + others)
    kern_to_sites(1, sides_of[0])
    base = 3 * width
    slots = summed[4 * chans :, :]
    lanes_n = slots.shape[1]
    groups = lanes_n // SLOT
    slot_of = iota(slots.shape, 1) // SLOT
    unpacked = jnp.concatenate([jnp.where(slot_of == n, slots, 0.0) for n in range(groups)], axis=0)
    place_in = iota((lanes_n, width), 0) % SLOT
    col = iota((lanes_n, width), 1)
    row_l = mm(unpacked.astype(BF16), (place_in == col // sites).astype(BF16))
    row_j = mm(unpacked.astype(BF16), (place_in == col % sites).astype(BF16))
    sites_in = (iota((sites, lanes_n), 1) % SLOT == iota((sites, lanes_n), 0)).astype(BF16)
    filled_t = mm_nt(sites_in, unpacked.astype(BF16)).astype(BF16)
    weights = jnp.sum(
        jnp.where(iota(unpacked.shape, 1) % SLOT == sites, unpacked, 0.0), axis=1, keepdims=True
    )
    norm = 1.0 / jnp.sum(weights, axis=0, keepdims=True)
    pieces = split(weights * (row_l * row_j), 3)
    triple = mm(filled_t, pieces[2]) + mm(filled_t, pieces[1]) + mm(filled_t, pieces[0])
    triple = triple * norm
    lane_l = iota((sites, width), 1) // sites
    lane_j = iota((sites, width), 1) % sites
    row_i = iota((sites, width), 0)
    pair = jnp.where(lane_l == row_i, triple, 0.0)
    single = jnp.sum(jnp.where(lane_j == row_i, pair, 0.0), axis=0, keepdims=True)
    stack = jnp.concatenate(
        [block_diag(triple, sites), pair, jnp.broadcast_to(single, (PAD_ROWS, width))], axis=0
    )
    spread_j = (
        iota((width, width), 0) % sites == iota((width, width), 1) // chans
    ).astype(BF16)
    corr_s[...] = mm_exact(stack, spread_j, pieces=2)

    occupied = corr_s[width + sites : width + sites + 1, :]

    pending = [(n, side, part) for n in range(4) for side in range(2) for part in range(2)]
    for i in range(sites):
        rows = slice(i * chans, (i + 1) * chans)
        after = slice(width + i * chans, width + (i + 1) * chans)
        pair_row = corr_s[width + i : width + i + 1, :]
        on_diag = iota((chans, width), 0) + i * chans == iota((chans, width), 1)
        halves = []
        for side in range(2):
            lanes = slice(side * half, (side + 1) * half)
            totals = [None, None]
            for at in range(sites):
                gap = int(place_diff[i, at])
                above, cell = divmod(at, cells)
                if side == 1 and above == 0:
                    cell = cell ^ (cells - 1)
                scale = corr_s[at * sites + i : at * sites + i + 1, lanes]
                scale = jnp.broadcast_to(scale, (chans, half))
                for part in range(2):
                    term = scale * p_s[cell, side ^ above, part, gap * chans : (gap + 1) * chans, :]
                    totals[part] = term if totals[part] is None else totals[part] + term
            halves.append(totals)
        for part in range(2):
            total = jnp.concatenate([halves[0][part], halves[1][part]], axis=1)
            lead = pair_row * site_s[part, rows, :]
            if part == 0:
                lead = lead - jnp.where(on_diag, occupied, 0.0)
            n_s[part, after, :] = lead
            n_s[part, rows, :] = lead + pair_row * site_s[part, after, :] - total
        if i == sites // 2:
            kern_to_sites(2, sides_of[1])
        for n, side, part in pending[i * len(pending) // sites : (i + 1) * len(pending) // sites]:
            for c, value in enumerate(cell_orders(sides_of[2 + n][side][part], chans)):
                c_s[n, side, part, c] = value
    for group, first_site in enumerate((own_start, other_start)):
        for i in range(own_sites):
            cell = (first_site + i) % cells
            above = (first_site + i) // cells
            turned_cell = above * cell + (1 - above) * (cells - 1 - cell)
            for n in range(4):
                start = base + n * rows_n + (group * own_sites + i) * chans
                for part in range(2):
                    site_s[part, start : start + chans, 0:half] = c_s[n, above, part, cell]
                    site_s[part, start : start + chans, half:width] = c_s[
                        n, 1 - above, part, turned_cell
                    ]

    mid = [(n_s[0, n * width : (n + 1) * width, :], n_s[1, n * width : (n + 1) * width, :]) for n in range(2)]

    def site_rows(n):
        start = base + n * rows_n
        return (site_s[0, start : start + rows_n, :], site_s[1, start : start + rows_n, :])

    def side_by_side(*values):
        return tuple(jnp.concatenate([v[part] for v in values], axis=1) for part in range(2))

    lead_rows = [site_rows(n) for n in range(4)]
    minus = -occupied
    q_zero = cadd(
        cmul(side_by_side(lead_rows[1], lead_rows[2]), (n_s[0], n_s[1]), mm3_deep),
        cscale(lead_rows[3], minus),
    )
    q_one = cadd(cmul(lead_rows[1], mid[1], mm3_deep), cscale(lead_rows[2], minus))
    stack = []
    for value in mid:
        for part in range(2):
            low = [value[part][c * chans : (c + 1) * chans] for c in range(cells)]
            high = [value[part][half + c * chans : half + (c + 1) * chans] for c in range(cells)]
            stack.append(
                sum_cells([low[c][:, :half] + high[c][:, half:] for c in range(cells)], chans)
            )
            crossed = sum_cells([low[c][:, half:] for c in range(cells)], chans)
            for bit in (1, 2, 4):
                crossed = flip_cells(crossed, bit * chans)
            stack.append(sum_cells([high[c][:, :half] for c in range(cells)], chans) + crossed)
    moved = mm_exact(jnp.concatenate(stack, axis=0), from_cells[...], pieces=2)
    moved = [moved[n * chans : (n + 1) * chans] for n in range(8)]
    means = [
        cadd(
            (moved[4 * n], moved[4 * n + 2]),
            turned((moved[4 * n + 1], moved[4 * n + 3]), turns, back=True),
        )
        for n in range(2)
    ]
    kern_diag = [tuple(block_diag(v, chans) for v in pair_val) for pair_val in kern[:2]]
    filled = -jnp.mean(occupied, axis=1, keepdims=True)
    mean_zero, mean_one, last = rows_by([means[0], means[1], series[2]], kern_diag[0])
    (mean_next,) = rows_by([means[1]], kern_diag[1])
    v_zero = cadd(mean_zero, mean_next, cscale(kern[2], filled))
    v_one = cadd(mean_one, cscale(kern[1], filled))
    change = cadd(
        series[1],
        series[2],
        series[3],
        cmul(series[0], tuple(block_diag(v, chans) for v in v_zero)),
        cmul(series[1], tuple(block_diag(v, chans) for v in v_one)),
        cscale(last, filled),
    )
    change_rows = tuple(by_momentum(value, chans, True) for value in change)
    q_two = cscale(lead_rows[1], minus)
    kernels = (site_s[0, 0 : 3 * width, :], site_s[1, 0 : 3 * width, :])
    q_all = side_by_side(q_zero, q_one, q_two)
    parts = []
    for group in range(2):
        rows = slice(group * own_rows, (group + 1) * own_rows)
        parts.append(cmul(tuple(v[rows] for v in q_all), kernels, mm3_deep))
    result = cadd(
        lead_rows[0],
        tuple(jnp.concatenate([p[part] for p in parts], axis=0) for part in range(2)),
    )

    for ref, start in ((keep, 0), (send, own_rows)):
        for part in range(2):
            ref[part * own_rows : (part + 1) * own_rows, :] = result[part][start : start + own_rows]
            for n, value in enumerate((change_rows, coarse_rows)):
                at = 2 * own_rows + (2 * n + part) * count_m
                ref[at : at + count_m, :] = value[part]


def finish_energy(own_rows, ref, kmap, square, coarse, correction):
    count_m = coarse.shape[2]
    count_k = kmap.shape[1]
    onehot = kmap[...] == iota((count_m, count_k), 0)
    blocks = [ref[2 * own_rows + n * count_m : 2 * own_rows + (n + 1) * count_m, :] for n in range(4)]
    for part in range(2):
        coarse[part] = blocks[2 + part].T
    real, imag = cmul((blocks[0], blocks[1]), (square[0], square[1]))
    correction[0:1, :] = jnp.sum(jnp.where(onehot, real, 0.0), axis=0, keepdims=True)
    correction[1:2, :] = jnp.sum(jnp.where(onehot, imag, 0.0), axis=0, keepdims=True)


def own_kernel(own_rows, kept, kmap, square, coarse, correction):
    finish_energy(own_rows, kept, kmap, square, coarse, correction)


def other_kernel(
    own_rows,
    cfg_at, kept, got, kmap, square, coarse_own, correction_own,
    avg, coarse, correction,
    coarse_s, correction_s, sems,
):
    own = cfg_at[0] % 2
    copies = []

    def send_out(source, target):
        copy = pltpu.make_async_copy(source, target, sems.at[len(copies)])
        copy.start()
        copies.append(copy)

    for ref, energy in ((got, 1 - own), (kept, own)):
        for part in range(2):
            rows = pl.ds(part * own_rows, own_rows)
            send_out(ref.at[rows], avg.at[energy, part])
    send_out(coarse_own, coarse.at[own])
    send_out(correction_own, correction.at[own])
    finish_energy(own_rows, got, kmap, square, coarse_s, correction_s)
    send_out(coarse_s, coarse.at[1 - own])
    send_out(correction_s, correction.at[1 - own])
    for copy in copies:
        copy.wait()


def shape_of(*extent):
    return jax.ShapeDtypeStruct(extent, F32)


SMEM_SPEC = pl.BlockSpec(memory_space=pltpu.SMEM)
VMEM_SPEC = pl.BlockSpec(memory_space=pltpu.VMEM)


def call(body, outs, scratch, scalars, args, cost, spec=None, out_spec=VMEM_SPEC):
    return pl.pallas_call(
        body,
        out_shape=outs,
        in_specs=[SMEM_SPEC] * scalars + [spec or VMEM_SPEC] * (len(args) - scalars),
        out_specs=jax.tree.map(lambda _: out_spec, outs),
        scratch_shapes=scratch,
        compiler_params=pltpu.CompilerParams(vmem_limit_bytes=KERNEL_VMEM),
        cost_estimate=pl.CostEstimate(flops=cost, bytes_accessed=cost // 64, transcendentals=0),
    )(*args)


def exchange_stages(ka_size, cfg_size):
    total = ka_size * cfg_size
    bits = []
    step = 2
    while step < total:
        bits.append(step)
        step *= 2
    stages = []
    for at in range(0, len(bits), 2):
        group = bits[at : at + 2]
        stages.append(group if len(group) == 1 else [group[0], group[1], group[0] + group[1]])
    return stages


def swap(value, mask, total):
    return lax.ppermute(value, ("ka", "cfg"), [(i, i ^ mask) for i in range(total)])


def step(medium_t, structure, kmap, occupation, cfg_weight, shift_a, shift_b):
    ka_size, cfg_size = lax.axis_size("ka"), lax.axis_size("cfg")
    total = ka_size * cfg_size
    count_cfg = occupation.shape[0] * total
    sites = occupation.shape[1]
    chans, count_m = medium_t.shape[2], medium_t.shape[4]
    count_k = kmap.shape[0]
    flat = chans * chans
    width = count_m * chans
    per_moment = count_k * total // count_m
    own_sites = sites // cfg_size
    own_rows = own_sites * chans
    chip_rows = 2 * own_rows
    slot_rows = -(-count_cfg * SLOT // (width // 2))
    sum_rows = 4 * chans + -(-slot_rows // 8) * 8
    *tables, place_diff = phase_constants(sites, chans)

    cfg_at = lax.axis_index("cfg").astype(jnp.int32).reshape(1)
    kmap_row = kmap.reshape(1, count_k)

    place = lax.axis_index(("ka", "cfg")).astype(jnp.int32).reshape(1)
    inputs = (
        place,
        cfg_weight,
        medium_t.reshape(ENERGIES, 2, flat, count_m),
        structure.reshape(ENERGIES, 2, flat, count_k),
        kmap_row,
        occupation,
    )
    inputs = inputs[:2] + tuple(
        pltpu.with_memory_space_constraint(value, pltpu.HBM) for value in inputs[2:]
    )
    outs = (
        shape_of(sum_rows, width // 2),
        shape_of(2, flat, count_k),
        shape_of(2, flat, count_k),
    )
    own_outs = (
        shape_of(2, flat, count_m),
        shape_of(2, flat, count_k),
        jax.ShapeDtypeStruct((1, count_k), jnp.int32),
    )
    work = [pltpu.VMEM((3, flat, count_k), F32)] * 3
    local = [
        pltpu.VMEM((2, flat, count_m), F32),
        pltpu.VMEM(occupation.shape, jnp.int32),
        pltpu.SemaphoreType.DMA((7,)),
    ]
    send, z_other, y_other, *own = call(
        send_kernel,
        outs + own_outs,
        work + local,
        2,
        inputs,
        1 << 23,
        spec=pl.BlockSpec(memory_space=pltpu.HBM),
    )
    arrived = swap(send, 1, total)
    keep, z_own, y_own = call(keep_kernel, outs, work, 0, (send, *own), 1 << 23)
    summed = keep + arrived
    y_z = ((y_own, z_own), (y_other, z_other))
    squares = []
    for energy in range(ENERGIES):
        if energy == 0:
            square, y_row = call(
                square_own_kernel,
                (shape_of(2, flat, count_k), shape_of(2, chans, width)),
                work,
                0,
                (*y_z[energy], own[0]),
                1 << 24,
            )
        else:
            square = call(square_kernel, shape_of(2, flat, count_k), work, 0, y_z[energy], 1 << 24)
        squares.append(square)
    for stage in exchange_stages(ka_size, cfg_size):
        arrived = []
        for mask in stage:
            arrived.append(swap(summed, mask, total))
        for value in arrived:
            summed = summed + value
    out_rows = 2 * own_rows + 4 * count_m
    kept, sent = call(
        functools.partial(cluster_kernel, per_moment, own_rows, place_diff),
        (shape_of(out_rows, flat), shape_of(out_rows, flat)),
        [
            pltpu.VMEM((2, 3 * width + 4 * chip_rows, width), F32),
            pltpu.VMEM((width + sites + PAD_ROWS, width), F32),
            pltpu.VMEM((sites // 2, 2, 2, width, width // 2), F32),
            pltpu.VMEM((width, 128), F32),
            pltpu.VMEM((2, 2 * width, width), F32),
            pltpu.VMEM((4, 2, 2, sites // 2, chans, width // 2), F32),
        ],
        1,
        (
            cfg_at,
            summed,
            y_row,
            shift_a,
            shift_b,
            *tables,
        ),
        1 << 26,
    )
    got = swap(sent, 1, total)
    coarse_own, correction_own = call(
        functools.partial(own_kernel, own_rows),
        (shape_of(2, flat, count_m), shape_of(2, count_k)),
        [],
        0,
        (kept, own[2], squares[0]),
        1 << 22,
    )
    avg, coarse, correction = call(
        functools.partial(other_kernel, own_rows),
        (
            shape_of(ENERGIES, 2, own_rows, width),
            shape_of(ENERGIES, 2, flat, count_m),
            shape_of(ENERGIES, 2, count_k),
        ),
        [
            pltpu.VMEM((2, flat, count_m), F32),
            pltpu.VMEM((2, count_k), F32),
            pltpu.SemaphoreType.DMA((8,)),
        ],
        1,
        (cfg_at, kept, got, own[2], squares[1], coarse_own, correction_own),
        1 << 22,
        out_spec=pl.BlockSpec(memory_space=pltpu.HBM),
    )
    return (coarse.reshape(ENERGIES, 2, chans, chans, count_m), avg, correction)


def solution(mesh):
    placed = (
        P(),
        P(None, None, None, None, ("ka", "cfg")),
        P(("ka", "cfg")),
        P(("ka", "cfg"), None),
        P(("ka", "cfg")),
        P(),
        P(),
    )
    return jax.shard_map(
        step,
        mesh=mesh,
        in_specs=placed,
        out_specs=(P(), P(None, None, "cfg", None), P(None, None, ("ka", "cfg"))),
        check_vma=False,
    )
```

```python
import functools
import math

import jax
import jax.numpy as jnp
import numpy as np
from jax import lax
from jax.experimental import pallas as pl
from jax.experimental.pallas import tpu as pltpu
from jax.sharding import PartitionSpec as P

ENERGIES = 2
F32 = jnp.float32
BF16 = jnp.bfloat16
PAD_ROWS = 8
SLOT = 32
KERNEL_VMEM = 20 << 20


def site_geometry(count_sites):
    places = np.arange(count_sites)
    half_n = count_sites // 2
    cell = places % half_n
    site_xyz = np.stack([cell // 4, cell // 2 % 2, cell % 2], axis=1).astype(np.float64)
    site_xyz = site_xyz + 0.5 * (places >= half_n)[:, None]
    mom_hkl = np.stack([places // 4, places // 2 % 2, places % 2], axis=1).astype(np.float64)
    angles = math.pi * (mom_hkl[:, None, :] * site_xyz[None, :, :]).sum(axis=2)
    place_diff = np.zeros((count_sites, count_sites), np.int32)
    for i in range(count_sites):
        for j in range(count_sites):
            gap = (site_xyz[i] - site_xyz[j]) % 2.0
            place_diff[i, j] = int(np.argmin(np.abs(site_xyz % 2.0 - gap).sum(axis=1)))
    return angles, place_diff


def phase_constants(count_sites, chans):
    angles, place_diff = site_geometry(count_sites)
    cells = count_sites // 2
    signs = np.rint(np.cos(angles[:, :cells]))
    turn = angles[:, cells]
    to_cells = np.kron(signs, np.eye(chans)) / count_sites
    turns = np.stack([np.rint(np.cos(turn)), np.rint(np.sin(turn))])
    turns = np.repeat(turns, chans, axis=1)
    return (
        jnp.asarray(to_cells, BF16),
        jnp.asarray(to_cells.T, BF16),
        jnp.asarray(np.concatenate([turns] * (chans // 2)), F32),
        place_diff,
    )


def iota(shape, dim):
    return lax.broadcasted_iota(jnp.int32, shape, dim)


def split(value, pieces):
    out = []
    for step in range(pieces):
        part = value.astype(BF16)
        out.append(part)
        if step + 1 < pieces:
            value = value - part.astype(F32)
    return out


def mm(left, right):
    return jnp.dot(left, right, preferred_element_type=F32)


def mm_nt(left, right):
    return lax.dot_general(left, right, (((1,), (1,)), ((), ())), preferred_element_type=F32)


def mm_exact(left, right_bf16, pieces=3):
    rows = left.shape[0]
    out = mm(jnp.concatenate(split(left, pieces), axis=0), right_bf16)
    total = out[(pieces - 1) * rows :]
    for at in range(pieces - 2, -1, -1):
        total = total + out[at * rows : (at + 1) * rows]
    return total


def mm3(left, right):
    rows = left.shape[0]
    left_hi, left_lo = split(left, 2)
    right_hi, right_lo = split(right, 2)
    out = mm(jnp.concatenate([left_hi, left_lo], axis=0), right_hi)
    return (mm(left_hi, right_lo) + out[rows:]) + out[:rows]


def mm3_deep(left, right):
    left_hi, left_lo = split(left, 2)
    right_hi, right_lo = split(right, 2)
    return mm(
        jnp.concatenate([left_hi, left_lo, left_hi], axis=1),
        jnp.concatenate([right_lo, right_hi, right_hi], axis=0),
    )


def mm_high(left, right):
    return jnp.dot(left, right, preferred_element_type=F32, precision=lax.Precision.HIGHEST)


def cmul(left, right, mul=mm3):
    rows = left[0].shape[0]
    both = jnp.concatenate(left, axis=0)
    by_real = mul(both, right[0])
    by_imag = mul(both, right[1])
    return (by_real[:rows] - by_imag[rows:], by_imag[:rows] + by_real[rows:])


def flip_cells(value, step):
    lanes = value.shape[1]
    ahead = pltpu.roll(value, step, 1)
    if 2 * step == lanes:
        return ahead
    behind = pltpu.roll(value, lanes - step, 1)
    return jnp.where(iota(value.shape, 1) // step % 2 == 1, ahead, behind)


def cell_orders(value, chans):
    count = value.shape[1] // chans
    orders = {0: value}
    at = 0
    for step in range(1, count):
        bit = count // 2
        while step % 2 == 0:
            step //= 2
            bit //= 2
        value = flip_cells(value, bit * chans)
        at ^= bit
        orders[at] = value
    return [orders[n] for n in range(count)]


def sum_cells(values, chans):
    bit = len(values) // 2
    while bit:
        values = [values[n] + flip_cells(values[n + bit], bit * chans) for n in range(bit)]
        bit //= 2
    return values[0]


def by_momentum(row, chans):
    high, wide = row.shape[0] // 2, row.shape[1] // 2
    tiles = [[row[i * high : (i + 1) * high, j * wide : (j + 1) * wide] for j in range(2)] for i in range(2)]
    tiles[0][1], tiles[1][0] = tiles[1][0], tiles[0][1]
    bit = high // 2
    while bit:
        step = bit * chans
        low_row = iota((high, wide), 0) // bit % 2 == 0
        low_lane = iota((high, wide), 1) // step % 2 == 0
        for i in range(2):
            for j in range(2):
                tile = tiles[i][j]
                ahead = pltpu.roll(pltpu.roll(tile, high - bit, 0), step, 1)
                if 2 * bit == high:
                    behind = ahead
                else:
                    behind = pltpu.roll(pltpu.roll(tile, bit, 0), wide - step, 1)
                moved = jnp.where(low_row, ahead, behind)
                tiles[i][j] = jnp.where(low_row == low_lane, tile, moved)
        bit //= 2
    return jnp.concatenate([jnp.concatenate(line, axis=1) for line in tiles], axis=0)


def turned(value, turns, back=False):
    cos_t, sin_t = turns[0:1], turns[1:2]
    if back:
        sin_t = -sin_t
    return (cos_t * value[0] - sin_t * value[1], cos_t * value[1] + sin_t * value[0])


def cadd(*terms):
    real, imag = terms[0]
    for term in terms[1:]:
        real, imag = real + term[0], imag + term[1]
    return (real, imag)


def cscale(value, factor):
    return (value[0] * factor, value[1] * factor)


def block_diag(row, chans):
    width = row.shape[1]
    tiled = jnp.concatenate([row] * (width // chans), axis=0)
    keep = iota((width, width), 0) // chans == iota((width, width), 1) // chans
    return jnp.where(keep, tiled, 0.0)


def batch_mul(left, right, write, chans):
    group = 8

    def body(step, carry):
        base = step * (group * chans)
        sums = [[None] * 3 for _ in range(group)]
        for b in range(chans):
            rights = [right[part, b * chans : (b + 1) * chans, :] for part in range(3)]
            for g in range(group):
                for part in range(3):
                    lane = left[part, pl.ds(base + (g * chans + b), 1), :]
                    term = lane * rights[part]
                    old = sums[g][part]
                    sums[g][part] = term if old is None else old + term
        for g in range(group):
            both, twice, cross = sums[g]
            write(base + g * chans, both - twice, cross - both - twice)
        return carry

    lax.fori_loop(0, chans // group, body, 0)


def put3(ref, base, count, real, imag):
    rows = pl.ds(pl.multiple_of(base, count), count)
    ref[0, rows, :] = real
    ref[1, rows, :] = imag
    ref[2, rows, :] = real + imag


def kpoint_energy(medium, kmap, packed, z_out, y_out, y_s, g_s, f_s, ready=None):
    flat, count_m = medium[0].shape
    count_k = kmap.shape[1]
    chans = math.isqrt(flat)
    width = 2 * packed.shape[1]
    onehot = (kmap == iota((count_m, count_k), 0)).astype(BF16)
    wide = (kmap == iota((width, count_k), 0) // chans).astype(BF16)
    same = iota((flat, width), 0) % chans == iota((flat, width), 1) % chans

    def fold(value):
        return jnp.sum(jnp.where(same, value, 0.0).reshape(chans, chans, width), axis=1)

    for part in range(2):
        value = mm_exact(medium[part], onehot)
        y_s[part] = value
        y_out[part] = value
    y_s[2] = y_s[0] + y_s[1]
    if ready is not None:
        ready()
    g_s[2] = g_s[0] + g_s[1]
    batch_mul(y_s, g_s, lambda base, real, imag: put3(f_s, base, chans, real, imag), chans)

    def write_z(base, real, imag):
        rows = pl.ds(pl.multiple_of(base, chans), chans)
        z_out[0, rows, :] = real + f_s[0, rows, :]
        z_out[1, rows, :] = imag + f_s[1, rows, :]

    batch_mul(f_s, f_s, write_z, chans)
    for part in range(2):
        parts = split(z_out[part], 2)
        total = mm_nt(parts[1], wide) + mm_nt(parts[0], wide)
        folded = fold(total)
        for side in range(2):
            at = (2 * side + part) * chans
            packed[at : at + chans, :] = folded[:, side * width // 2 : (side + 1) * width // 2]


def occupation_slots(place, occupation, weight, rows, width):
    count, sites = occupation.shape
    lane = iota((sites, width), 1) % SLOT
    to_slot = (iota((sites, width), 0) == lane).astype(BF16)
    slots = jnp.zeros((rows, width), F32)
    for g in range(count):
        filled = jnp.broadcast_to(occupation[g : g + 1, :].astype(BF16), (sites, sites))
        line = mm(filled, to_slot)[0:1] + jnp.where(lane[0:1] == sites, weight[g], 0.0)
        at = place * count + g
        per_row = width // SLOT
        here = (iota((rows, width), 0) == at // per_row) & (
            iota((rows, width), 1) // SLOT == at % per_row
        )
        slots = slots + jnp.where(here, line, 0.0)
    return slots


def send_kernel(
    place, weight, medium, structure, kmap, occupation,
    packed, z_out, y_out, medium_own, structure_own, kmap_own,
    y_s, g_s, f_s, medium_s, occupation_s, sems,
):
    own = place[0] % 2
    copies = [
        (kmap, kmap_own),
        (medium.at[1 - own], medium_s),
        (structure.at[1 - own, 0], g_s.at[0]),
        (structure.at[1 - own, 1], g_s.at[1]),
        (occupation, occupation_s),
        (medium.at[own], medium_own),
        (structure.at[own], structure_own),
    ]
    copies = [pltpu.make_async_copy(src, dst, sems.at[n]) for n, (src, dst) in enumerate(copies)]
    for copy in copies:
        copy.start()
    half = 4 * math.isqrt(medium_s.shape[1])
    copies[0].wait()
    copies[1].wait()

    def ready():
        for copy in copies[2:5]:
            copy.wait()

    medium_val = (medium_s[0], medium_s[1])
    kpoint_energy(medium_val, kmap_own[...], packed, z_out, y_out, y_s, g_s, f_s, ready)
    packed[half:, :] = occupation_slots(
        place[0], occupation_s[...], weight, packed.shape[0] - half, packed.shape[1]
    )
    for copy in copies[5:]:
        copy.wait()


def keep_kernel(sent, medium, structure, kmap, packed, z_out, y_out, y_s, g_s, f_s):
    for part in range(2):
        g_s[part] = structure[part]
    medium_val = (medium[0], medium[1])
    kpoint_energy(medium_val, kmap[...], packed, z_out, y_out, y_s, g_s, f_s)
    half = 4 * math.isqrt(medium.shape[1])
    packed[half:, :] = sent[half:, :]


def square_kernel(y_in, z_in, out, y_s, z_s, t_s):
    flat = out.shape[1]
    chans = math.isqrt(flat)
    for part in range(2):
        y_s[part] = y_in[part]
        z_s[part] = z_in[part]
    y_s[2] = y_in[0] + y_in[1]
    z_s[2] = z_in[0] + z_in[1]

    def write_t(base, real, imag):
        rows = pl.ds(pl.multiple_of(base, chans), chans)
        put3(t_s, base, chans, real + y_s[0, rows, :], imag + y_s[1, rows, :])

    batch_mul(z_s, y_s, write_t, chans)

    def write_o(base, real, imag):
        rows = pl.ds(pl.multiple_of(base, chans), chans)
        y_s[0, rows, :] = real
        y_s[1, rows, :] = imag

    batch_mul(t_s, t_s, write_o, chans)
    for part in range(2):
        for col in range(chans):
            out[part, col * chans : (col + 1) * chans, :] = y_s[part, pl.ds(col, chans, stride=chans), :]


def square_own_kernel(y_in, z_in, medium, out, y_row, y_s, z_s, t_s):
    square_kernel(y_in, z_in, out, y_s, z_s, t_s)
    flat, count_m = medium.shape[1:]
    chans, width = y_row.shape[1:]
    lanes_of = (iota((count_m, width), 0) == iota((count_m, width), 1) // chans).astype(BF16)
    same = iota((flat, width), 0) % chans == iota((flat, width), 1) % chans
    for part in range(2):
        value = jnp.where(same, mm_exact(medium[part], lanes_of), 0.0)
        y_row[part] = jnp.sum(value.reshape(chans, chans, width), axis=1)


def cluster_kernel(
    per_moment, own_rows, place_diff,
    cfg_at, summed, y_row, shift_a, shift_b, to_cells, from_cells, turn_rows,
    keep, send, site_s, corr_s, p_s, a_s, n_s, c_s,
):
    own = cfg_at[0] % 2
    chans = shift_a.shape[2]
    width = 2 * summed.shape[1]
    sites = width // turn_rows.shape[0]
    cells = sites // 2
    half = cells * chans
    turns = turn_rows[0:2, :]
    own_sites = own_rows // chans
    rows_n = 2 * own_rows
    own_start = cfg_at[0] * own_sites
    other_start = (cfg_at[0] + 1 - 2 * own) * own_sites

    y_val = (y_row[0], y_row[1])
    z_val = tuple(
        jnp.concatenate(
            [summed[(2 * side + part) * chans : (2 * side + part + 1) * chans, :] for side in range(2)],
            axis=1,
        )
        for part in range(2)
    )
    y_diag = tuple(block_diag(v, chans) for v in y_val)
    coarse = cadd(y_val, cscale(cmul(z_val, y_diag), 1.0 / per_moment))

    coarse_rows = tuple(by_momentum(value, chans) for value in coarse)
    count_m = width // chans
    base_t = (shift_b[own, 0], shift_b[own, 1])
    step_t = (shift_a[own, 0] - base_t[0], shift_a[own, 1] - base_t[1])

    stack = jnp.concatenate(base_t + step_t, axis=0)
    by_real = mm_high(stack, coarse[0])
    by_imag = mm_high(stack, coarse[1])

    def small_part(at):
        here, after = slice(at * chans, (at + 1) * chans), slice((at + 1) * chans, (at + 2) * chans)
        return (by_real[here] - by_imag[after], by_imag[here] + by_real[after])

    def rows_by(rows, diag):
        count = len(rows)
        out = cmul(
            tuple(jnp.concatenate([row[part] for row in rows], axis=0) for part in range(2)), diag
        )
        return [
            tuple(out[part][n * chans : (n + 1) * chans] for part in range(2)) for n in range(count)
        ]

    power, lead_kern = small_part(0), small_part(2)
    power_diag = tuple(block_diag(v, chans) for v in power)
    cell_map = to_cells[...]

    def to_differences(values):
        rows = []
        for step in range(2):
            for value in values:
                for variant in (value, turned(value, turns)):
                    rows += [split(part, 2)[step] for part in variant]
        out = mm(jnp.concatenate(rows, axis=0), cell_map)
        count = len(values) * 4 * chans
        out = out[count:] + out[:count]
        blocks = [out[n * chans : (n + 1) * chans] for n in range(4 * len(values))]
        return [
            [[blocks[4 * n + 2 * side + part] for part in range(2)] for side in range(2)]
            for n in range(len(values))
        ]

    def kern_to_sites(n, sides):
        start = n * width
        for part in range(2):
            lower = cell_orders(sides[0][part], chans)
            upper = cell_orders(sides[1][part], chans)
            for c in range(cells):
                low = slice(start + c * chans, start + (c + 1) * chans)
                high = slice(start + half + c * chans, start + half + (c + 1) * chans)
                site_s[part, low, 0:half] = lower[c]
                site_s[part, high, half:width] = lower[c]
                site_s[part, high, 0:half] = upper[c]
                site_s[part, low, half:width] = upper[c ^ (cells - 1)]

    first, first_kern, power = rows_by([coarse, lead_kern, power], power_diag)
    first, first_kern = cscale(first, -1.0), cscale(first_kern, -1.0)
    power_diag = tuple(block_diag(v, chans) for v in power)
    (lead_sides,) = to_differences([lead_kern])
    kern_to_sites(0, lead_sides)
    second, third, second_kern = rows_by([coarse, first, lead_kern], power_diag)
    series = [coarse, first, second, third]
    kern = [lead_kern, first_kern, second_kern]
    whole = cadd(*series)

    hi_lo = []
    for part in range(2):
        hi, lo = split(site_s[part, 0:width, 0:chans], 2)
        hi_lo += [hi.astype(F32), hi.astype(F32), lo.astype(F32)]
    for n, piece in enumerate(hi_lo):
        a_s[:, n * chans : (n + 1) * chans] = piece
    a_val = a_s[:, 0 : 6 * chans].astype(BF16)
    far = cells // 2
    for c in range(far):
        rows = slice(c * chans, (c + 1) * chans)
        high = slice(half + c * chans, half + (c + 1) * chans)
        pieces = []
        for part in range(2):
            line = jnp.concatenate([site_s[part, rows, 0:half], site_s[part, high, 0:half]], axis=1)
            pieces += split(line, 2)
        real_hi, real_lo, imag_hi, imag_lo = pieces
        for part, right in enumerate(
            (
                [real_hi, real_lo, real_hi, -imag_hi, -imag_lo, -imag_hi],
                [imag_hi, imag_lo, imag_hi, real_hi, real_lo, real_hi],
            )
        ):
            out = mm(a_val, jnp.concatenate(right, axis=0))
            for side in range(2):
                value = out[:, side * half : (side + 1) * half]
                p_s[c, side, part] = value
                p_s[c + far, side, part] = flip_cells(value, half // 2)

    others = [whole] + series[:3]
    sides_of = to_differences(kern[1:] + others)
    kern_to_sites(1, sides_of[0])
    base = 3 * width
    slots = summed[4 * chans :, :]
    lanes_n = slots.shape[1]
    groups = lanes_n // SLOT
    slot_of = iota(slots.shape, 1) // SLOT
    unpacked = jnp.concatenate([jnp.where(slot_of == n, slots, 0.0) for n in range(groups)], axis=0)
    place_in = iota((lanes_n, width), 0) % SLOT
    col = iota((lanes_n, width), 1)
    row_l = mm(unpacked.astype(BF16), (place_in == col // sites).astype(BF16))
    row_j = mm(unpacked.astype(BF16), (place_in == col % sites).astype(BF16))
    sites_in = (iota((sites, lanes_n), 1) % SLOT == iota((sites, lanes_n), 0)).astype(BF16)
    filled_t = mm_nt(sites_in, unpacked.astype(BF16)).astype(BF16)
    weights = jnp.sum(
        jnp.where(iota(unpacked.shape, 1) % SLOT == sites, unpacked, 0.0), axis=1, keepdims=True
    )
    norm = 1.0 / jnp.sum(weights, axis=0, keepdims=True)
    pieces = split(weights * (row_l * row_j), 3)
    triple = mm(filled_t, pieces[2]) + mm(filled_t, pieces[1]) + mm(filled_t, pieces[0])
    triple = triple * norm
    lane_l = iota((sites, width), 1) // sites
    lane_j = iota((sites, width), 1) % sites
    row_i = iota((sites, width), 0)
    pair = jnp.where(lane_l == row_i, triple, 0.0)
    single = jnp.sum(jnp.where(lane_j == row_i, pair, 0.0), axis=0, keepdims=True)
    stack = jnp.concatenate(
        [block_diag(triple, sites), pair, jnp.broadcast_to(single, (PAD_ROWS, width))], axis=0
    )
    spread_j = (
        iota((width, width), 0) % sites == iota((width, width), 1) // chans
    ).astype(BF16)
    corr_s[...] = mm_exact(stack, spread_j, pieces=2)

    occupied = corr_s[width + sites : width + sites + 1, :]

    pending = [(n, side, part) for n in range(4) for side in range(2) for part in range(2)]
    for i in range(sites):
        rows = slice(i * chans, (i + 1) * chans)
        after = slice(width + i * chans, width + (i + 1) * chans)
        pair_row = corr_s[width + i : width + i + 1, :]
        on_diag = iota((chans, width), 0) + i * chans == iota((chans, width), 1)
        halves = []
        for side in range(2):
            lanes = slice(side * half, (side + 1) * half)
            totals = [None, None]
            for at in range(sites):
                gap = int(place_diff[i, at])
                above, cell = divmod(at, cells)
                if side == 1 and above == 0:
                    cell = cell ^ (cells - 1)
                scale = corr_s[at * sites + i : at * sites + i + 1, lanes]
                scale = jnp.broadcast_to(scale, (chans, half))
                for part in range(2):
                    term = scale * p_s[cell, side ^ above, part, gap * chans : (gap + 1) * chans, :]
                    totals[part] = term if totals[part] is None else totals[part] + term
            halves.append(totals)
        for part in range(2):
            total = jnp.concatenate([halves[0][part], halves[1][part]], axis=1)
            lead = pair_row * site_s[part, rows, :]
            if part == 0:
                lead = lead - jnp.where(on_diag, occupied, 0.0)
            n_s[part, after, :] = lead
            n_s[part, rows, :] = lead + pair_row * site_s[part, after, :] - total
        if i == sites // 2:
            kern_to_sites(2, sides_of[1])
        for n, side, part in pending[i * len(pending) // sites : (i + 1) * len(pending) // sites]:
            for c, value in enumerate(cell_orders(sides_of[2 + n][side][part], chans)):
                c_s[n, side, part, c] = value
    for group, first_site in enumerate((own_start, other_start)):
        for i in range(own_sites):
            cell = (first_site + i) % cells
            above = (first_site + i) // cells
            turned_cell = above * cell + (1 - above) * (cells - 1 - cell)
            for n in range(4):
                start = base + n * rows_n + (group * own_sites + i) * chans
                for part in range(2):
                    site_s[part, start : start + chans, 0:half] = c_s[n, above, part, cell]
                    site_s[part, start : start + chans, half:width] = c_s[
                        n, 1 - above, part, turned_cell
                    ]

    mid = [(n_s[0, n * width : (n + 1) * width, :], n_s[1, n * width : (n + 1) * width, :]) for n in range(2)]

    def site_rows(n):
        start = base + n * rows_n
        return (site_s[0, start : start + rows_n, :], site_s[1, start : start + rows_n, :])

    def side_by_side(*values):
        return tuple(jnp.concatenate([v[part] for v in values], axis=1) for part in range(2))

    lead_rows = [site_rows(n) for n in range(4)]
    minus = -occupied
    q_zero = cadd(
        cmul(side_by_side(lead_rows[1], lead_rows[2]), (n_s[0], n_s[1]), mm3_deep),
        cscale(lead_rows[3], minus),
    )
    q_one = cadd(cmul(lead_rows[1], mid[1], mm3_deep), cscale(lead_rows[2], minus))
    stack = []
    for value in mid:
        for part in range(2):
            low = [value[part][c * chans : (c + 1) * chans] for c in range(cells)]
            high = [value[part][half + c * chans : half + (c + 1) * chans] for c in range(cells)]
            stack.append(
                sum_cells([low[c][:, :half] + high[c][:, half:] for c in range(cells)], chans)
            )
            crossed = sum_cells([low[c][:, half:] for c in range(cells)], chans)
            for bit in (1, 2, 4):
                crossed = flip_cells(crossed, bit * chans)
            stack.append(sum_cells([high[c][:, :half] for c in range(cells)], chans) + crossed)
    moved = mm_exact(jnp.concatenate(stack, axis=0), from_cells[...], pieces=2)
    moved = [moved[n * chans : (n + 1) * chans] for n in range(8)]
    means = [
        cadd(
            (moved[4 * n], moved[4 * n + 2]),
            turned((moved[4 * n + 1], moved[4 * n + 3]), turns, back=True),
        )
        for n in range(2)
    ]
    kern_diag = [tuple(block_diag(v, chans) for v in pair_val) for pair_val in kern[:2]]
    filled = -jnp.mean(occupied, axis=1, keepdims=True)
    mean_zero, mean_one, last = rows_by([means[0], means[1], series[2]], kern_diag[0])
    (mean_next,) = rows_by([means[1]], kern_diag[1])
    v_zero = cadd(mean_zero, mean_next, cscale(kern[2], filled))
    v_one = cadd(mean_one, cscale(kern[1], filled))
    change = cadd(
        series[1],
        series[2],
        series[3],
        cmul(series[0], tuple(block_diag(v, chans) for v in v_zero)),
        cmul(series[1], tuple(block_diag(v, chans) for v in v_one)),
        cscale(last, filled),
    )
    change_rows = tuple(by_momentum(value, chans) for value in change)
    q_two = cscale(lead_rows[1], minus)
    kernels = (site_s[0, 0 : 3 * width, :], site_s[1, 0 : 3 * width, :])
    q_all = side_by_side(q_zero, q_one, q_two)
    parts = []
    for group in range(2):
        rows = slice(group * own_rows, (group + 1) * own_rows)
        parts.append(cmul(tuple(v[rows] for v in q_all), kernels, mm3_deep))
    result = cadd(
        lead_rows[0],
        tuple(jnp.concatenate([p[part] for p in parts], axis=0) for part in range(2)),
    )

    for ref, start in ((keep, 0), (send, own_rows)):
        for part in range(2):
            ref[part * own_rows : (part + 1) * own_rows, :] = result[part][start : start + own_rows]
            for n, value in enumerate((change_rows, coarse_rows)):
                at = 2 * own_rows + (2 * n + part) * count_m
                ref[at : at + count_m, :] = value[part]


def finish_energy(own_rows, ref, kmap, square, coarse, correction):
    count_m = coarse.shape[2]
    count_k = kmap.shape[1]
    onehot = kmap[...] == iota((count_m, count_k), 0)
    blocks = [ref[2 * own_rows + n * count_m : 2 * own_rows + (n + 1) * count_m, :] for n in range(4)]
    for part in range(2):
        coarse[part] = blocks[2 + part].T
    real, imag = cmul((blocks[0], blocks[1]), (square[0], square[1]))
    correction[0:1, :] = jnp.sum(jnp.where(onehot, real, 0.0), axis=0, keepdims=True)
    correction[1:2, :] = jnp.sum(jnp.where(onehot, imag, 0.0), axis=0, keepdims=True)


def own_kernel(own_rows, kept, kmap, square, coarse, correction):
    finish_energy(own_rows, kept, kmap, square, coarse, correction)


def other_kernel(
    own_rows,
    cfg_at, kept, got, kmap, square, coarse_own, correction_own,
    avg, coarse, correction,
    coarse_s, correction_s, sems,
):
    own = cfg_at[0] % 2
    copies = []

    def send_out(source, target):
        copy = pltpu.make_async_copy(source, target, sems.at[len(copies)])
        copy.start()
        copies.append(copy)

    for ref, energy in ((got, 1 - own), (kept, own)):
        for part in range(2):
            rows = pl.ds(part * own_rows, own_rows)
            send_out(ref.at[rows], avg.at[energy, part])
    send_out(coarse_own, coarse.at[own])
    send_out(correction_own, correction.at[own])
    finish_energy(own_rows, got, kmap, square, coarse_s, correction_s)
    send_out(coarse_s, coarse.at[1 - own])
    send_out(correction_s, correction.at[1 - own])
    for copy in copies:
        copy.wait()


def shape_of(*extent):
    return jax.ShapeDtypeStruct(extent, F32)


SMEM_SPEC = pl.BlockSpec(memory_space=pltpu.SMEM)
VMEM_SPEC = pl.BlockSpec(memory_space=pltpu.VMEM)


def call(body, outs, scratch, scalars, args, cost, spec=None, out_spec=VMEM_SPEC):
    return pl.pallas_call(
        body,
        out_shape=outs,
        in_specs=[SMEM_SPEC] * scalars + [spec or VMEM_SPEC] * (len(args) - scalars),
        out_specs=jax.tree.map(lambda _: out_spec, outs),
        scratch_shapes=scratch,
        compiler_params=pltpu.CompilerParams(vmem_limit_bytes=KERNEL_VMEM),
        cost_estimate=pl.CostEstimate(flops=cost, bytes_accessed=cost // 64, transcendentals=0),
    )(*args)


def exchange_stages(ka_size, cfg_size):
    total = ka_size * cfg_size
    bits = []
    step = 2
    while step < total:
        bits.append(step)
        step *= 2
    stages = []
    for at in range(0, len(bits), 2):
        group = bits[at : at + 2]
        stages.append(group if len(group) == 1 else [group[0], group[1], group[0] + group[1]])
    return stages


def swap(value, mask, total):
    return lax.ppermute(value, ("ka", "cfg"), [(i, i ^ mask) for i in range(total)])


def step(medium_t, structure, kmap, occupation, cfg_weight, shift_a, shift_b):
    ka_size, cfg_size = lax.axis_size("ka"), lax.axis_size("cfg")
    total = ka_size * cfg_size
    count_cfg = occupation.shape[0] * total
    sites = occupation.shape[1]
    chans, count_m = medium_t.shape[2], medium_t.shape[4]
    count_k = kmap.shape[0]
    flat = chans * chans
    width = count_m * chans
    per_moment = count_k * total // count_m
    own_sites = sites // cfg_size
    own_rows = own_sites * chans
    chip_rows = 2 * own_rows
    slot_rows = -(-count_cfg * SLOT // (width // 2))
    sum_rows = 4 * chans + -(-slot_rows // 8) * 8
    *tables, place_diff = phase_constants(sites, chans)

    cfg_at = lax.axis_index("cfg").astype(jnp.int32).reshape(1)
    kmap_row = kmap.reshape(1, count_k)

    place = lax.axis_index(("ka", "cfg")).astype(jnp.int32).reshape(1)
    inputs = (
        place,
        cfg_weight,
        medium_t.reshape(ENERGIES, 2, flat, count_m),
        structure.reshape(ENERGIES, 2, flat, count_k),
        kmap_row,
        occupation,
    )
    inputs = inputs[:2] + tuple(
        pltpu.with_memory_space_constraint(value, pltpu.HBM) for value in inputs[2:]
    )
    outs = (
        shape_of(sum_rows, width // 2),
        shape_of(2, flat, count_k),
        shape_of(2, flat, count_k),
    )
    own_outs = (
        shape_of(2, flat, count_m),
        shape_of(2, flat, count_k),
        jax.ShapeDtypeStruct((1, count_k), jnp.int32),
    )
    work = [pltpu.VMEM((3, flat, count_k), F32)] * 3
    local = [
        pltpu.VMEM((2, flat, count_m), F32),
        pltpu.VMEM(occupation.shape, jnp.int32),
        pltpu.SemaphoreType.DMA((7,)),
    ]
    send, z_other, y_other, *own = call(
        send_kernel,
        outs + own_outs,
        work + local,
        2,
        inputs,
        1 << 23,
        spec=pl.BlockSpec(memory_space=pltpu.HBM),
    )
    arrived = swap(send, 1, total)
    keep, z_own, y_own = call(keep_kernel, outs, work, 0, (send, *own), 1 << 23)
    summed = keep + arrived
    y_z = ((y_own, z_own), (y_other, z_other))
    squares = []
    for energy in range(ENERGIES):
        if energy == 0:
            square, y_row = call(
                square_own_kernel,
                (shape_of(2, flat, count_k), shape_of(2, chans, width)),
                work,
                0,
                (*y_z[energy], own[0]),
                1 << 24,
            )
        else:
            square = call(square_kernel, shape_of(2, flat, count_k), work, 0, y_z[energy], 1 << 24)
        squares.append(square)
    for stage in exchange_stages(ka_size, cfg_size):
        arrived = []
        for mask in stage:
            arrived.append(swap(summed, mask, total))
        for value in arrived:
            summed = summed + value
    out_rows = 2 * own_rows + 4 * count_m
    kept, sent = call(
        functools.partial(cluster_kernel, per_moment, own_rows, place_diff),
        (shape_of(out_rows, flat), shape_of(out_rows, flat)),
        [
            pltpu.VMEM((2, 3 * width + 4 * chip_rows, width), F32),
            pltpu.VMEM((width + sites + PAD_ROWS, width), F32),
            pltpu.VMEM((sites // 2, 2, 2, width, width // 2), F32),
            pltpu.VMEM((width, 128), F32),
            pltpu.VMEM((2, 2 * width, width), F32),
            pltpu.VMEM((4, 2, 2, sites // 2, chans, width // 2), F32),
        ],
        1,
        (
            cfg_at,
            summed,
            y_row,
            shift_a,
            shift_b,
            *tables,
        ),
        1 << 26,
    )
    got = swap(sent, 1, total)
    coarse_own, correction_own = call(
        functools.partial(own_kernel, own_rows),
        (shape_of(2, flat, count_m), shape_of(2, count_k)),
        [],
        0,
        (kept, own[2], squares[0]),
        1 << 22,
    )
    avg, coarse, correction = call(
        functools.partial(other_kernel, own_rows),
        (
            shape_of(ENERGIES, 2, own_rows, width),
            shape_of(ENERGIES, 2, flat, count_m),
            shape_of(ENERGIES, 2, count_k),
        ),
        [
            pltpu.VMEM((2, flat, count_m), F32),
            pltpu.VMEM((2, count_k), F32),
            pltpu.SemaphoreType.DMA((8,)),
        ],
        1,
        (cfg_at, kept, got, own[2], squares[1], coarse_own, correction_own),
        1 << 22,
        out_spec=pl.BlockSpec(memory_space=pltpu.HBM),
    )
    return (coarse.reshape(ENERGIES, 2, chans, chans, count_m), avg, correction)


def solution(mesh):
    placed = (
        P(),
        P(None, None, None, None, ("ka", "cfg")),
        P(("ka", "cfg")),
        P(("ka", "cfg"), None),
        P(("ka", "cfg")),
        P(),
        P(),
    )
    return jax.shard_map(
        step,
        mesh=mesh,
        in_specs=placed,
        out_specs=(P(), P(None, None, "cfg", None), P(None, None, ("ka", "cfg"))),
        check_vma=False,
    )
```
